32 devices in a mesh: fsdp: 2 (over y), dp: 16 (over z, x, core).
Axes of the slice: x: 2, y: 2, z: 4, core: 2. Of those that a mesh axis runs over, the one named last changes fastest.
Arguments:
- doc_tokens: bfloat16 [32, 1024, 1024], P(('fsdp', 'dp')), may hold values from -6 to 6
- query_tokens: bfloat16 [64, 32, 1024], P(('fsdp', 'dp')), may hold values from -6 to 6
- doc_lengths: int32 [32], P(('fsdp', 'dp')), may hold values from 50 to 1024, as said below
- positives: int32 [64], P(('fsdp', 'dp')), may hold values from 0 to 31
- query_weight: bfloat16 [1024, 1024], P(('fsdp', 'dp')), may hold values from -0.1875 to 0.1875
- key_weight: bfloat16 [1024, 1024], P(('fsdp', 'dp')), may hold values from -0.1875 to 0.1875
- value_weight: bfloat16 [1024, 1024], P(('fsdp', 'dp')), may hold values from -0.1875 to 0.1875
- output_weight: bfloat16 [1024, 1024], P(('fsdp', 'dp')), may hold values from -0.75 to 0.75
- query_bias: bfloat16 [1024], P(('fsdp', 'dp')), may hold values from -3 to 3
- key_bias: bfloat16 [1024], P(('fsdp', 'dp')), may hold values from -3 to 3
- value_bias: bfloat16 [1024], P(('fsdp', 'dp')), may hold values from -3 to 3
- output_bias: bfloat16 [1024], P(('fsdp', 'dp')), may hold values from -3 to 3
- attn_gain: bfloat16 [1024], P(('fsdp', 'dp')), may hold values from 0.099609375 to 1.8984375
- attn_shift: bfloat16 [1024], P(('fsdp', 'dp')), may hold values from -3 to 3
- inner_weight: bfloat16 [1024, 4096], P(('fsdp', 'dp')), may hold values from -0.1875 to 0.1875
- inner_bias: bfloat16 [4096], P(('fsdp', 'dp')), may hold values from -3 to 3
- outer_weight: bfloat16 [4096, 1024], P(('fsdp', 'dp')), may hold values from -0.09375 to 0.09375
- outer_bias: bfloat16 [1024], P(('fsdp', 'dp')), may hold values from -3 to 3
- final_gain: bfloat16 [1024], P(('fsdp', 'dp')), may hold values from 0.099609375 to 1.8984375
- final_shift: bfloat16 [1024], P(('fsdp', 'dp')), may hold values from -3 to 3
- proj_weight: bfloat16 [1024, 128], P(('fsdp', 'dp')), may hold values from -0.1875 to 0.1875
Outputs:
- query_loss: float32 [64], P(('fsdp', 'dp'))
- doc_states: bfloat16 [32, 1024, 1024], P(('fsdp', 'dp'))
- query_states: bfloat16 [64, 32, 1024], P(('fsdp', 'dp'))
- doc_tokens_grad: float32 [32, 1024, 1024], P(('fsdp', 'dp'))
- query_tokens_grad: float32 [64, 32, 1024], P(('fsdp', 'dp'))
- query_weight_grad: float32 [1024, 1024], P(('fsdp', 'dp'))
- key_weight_grad: float32 [1024, 1024], P(('fsdp', 'dp'))
- value_weight_grad: float32 [1024, 1024], P(('fsdp', 'dp'))
- output_weight_grad: float32 [1024, 1024], P(('fsdp', 'dp'))
- query_bias_grad: float32 [1024], P(('fsdp', 'dp'))
- key_bias_grad: float32 [1024], P(('fsdp', 'dp'))
- value_bias_grad: float32 [1024], P(('fsdp', 'dp'))
- output_bias_grad: float32 [1024], P(('fsdp', 'dp'))
- attn_gain_grad: float32 [1024], P(('fsdp', 'dp'))
- attn_shift_grad: float32 [1024], P(('fsdp', 'dp'))
- inner_weight_grad: float32 [1024, 4096], P(('fsdp', 'dp'))
- inner_bias_grad: float32 [4096], P(('fsdp', 'dp'))
- outer_weight_grad: float32 [4096, 1024], P(('fsdp', 'dp'))
- outer_bias_grad: float32 [1024], P(('fsdp', 'dp'))
- final_gain_grad: float32 [1024], P(('fsdp', 'dp'))
- final_shift_grad: float32 [1024], P(('fsdp', 'dp'))
- proj_weight_grad: float32 [1024, 128], P(('fsdp', 'dp'))
The draws below stay inside these ranges and needn't reach their ends.
Inputs may be any that keep to these rules, and one draw needn't show every extreme that they name: `doc_lengths`: tokens of a slot at or beyond its document's length are padding. Some document fills its whole slot of 1024 tokens.
All inputs are finite; a program needn't handle non-finite values.
Results may differ from the reference program's by a relative error of at most 0.04.
Values may be sent and summed in bfloat16 or wider, within the bound.
A program may use at most 256 MiB of HBM per device.

```python
import math
import jax
import jax.numpy as jnp
from jax import lax

D = 1024
HEADS = 16
FF = 4096
PROJ = 128
QUESTION_TOKENS = 32
SLOT = 1024
MINLEN = 50
NDOCS = 32
NQ = 64


def draw_doc_lengths(key, part):
    grade_key = jax.random.fold_in(key, 11)
    extra_key = jax.random.fold_in(key, 12)
    chosen_key = jax.random.fold_in(key, 13)
    grades = jax.random.randint(grade_key, (NDOCS,), 0, 5)
    reaches = max(SLOT // 16, 1) * jnp.left_shift(jnp.ones((NDOCS,), jnp.int32), 2 * grades)
    extras = jax.random.randint(extra_key, (NDOCS,), 0, reaches)
    lengths = jnp.minimum(MINLEN + extras, SLOT)
    chosen = jax.random.randint(chosen_key, (), 0, NDOCS)
    return jnp.where(jnp.arange(NDOCS) == chosen, SLOT, lengths).astype(jnp.int32)


def set_ends(entries, stream_key, low, top_value):
    shape = entries.shape
    place = [jax.random.randint(jax.random.fold_in(stream_key, axis), (), 0, shape[axis]) for axis in range(len(shape))]
    entries = entries.at[tuple(place)].set(low)
    longest = shape.index(max(shape))
    place[longest] = (place[longest] + 1) % shape[longest]
    return entries.at[tuple(place)].set(top_value)


def level_of(own_key, dims, shards, least, top_value):
    def one(axis_at, blocks):
        heights = jax.random.uniform(jax.random.fold_in(jax.random.fold_in(own_key, 6), axis_at), (blocks,), jnp.float32, least / len(shards), top_value / len(shards))
        return jnp.repeat(jnp.exp(heights), dims[axis_at] // blocks).reshape((-1,) + (1,) * (len(dims) - axis_at - 1))

    factor_of = one(*shards[0])
    for cut in shards[1:]:
        factor_of = factor_of * one(*cut)
    return factor_of


def normal_values(rng, dims, scale, limit, shards=(), kind=jnp.bfloat16):
    level = level_of(rng, dims, shards, -0.22, 0.18) if shards else 1.0
    entries = jax.random.normal(rng, dims, jnp.float32) * scale * level
    return jnp.minimum(jnp.maximum(entries, -limit), limit).astype(kind)


def setup_inputs(seed: int = 0) -> dict:
    key_of = jax.random.split(jax.random.key(seed), 22)
    doc_tokens = normal_values(key_of[0], (NDOCS, SLOT, D), 1.0, 6.0, ((0, 32),))
    query_tokens = normal_values(key_of[1], (NQ, QUESTION_TOKENS, D), 1.0, 6.0, ((0, 32),))
    doc_lengths = draw_doc_lengths(jax.random.fold_in(key_of[21], 71), 0)
    positives = set_ends(jax.random.randint(key_of[3], (NQ,), 0, NDOCS), jax.random.fold_in(key_of[3], 1), 0, NDOCS - 1).astype(jnp.int32)
    query_weight = normal_values(key_of[4], (D, D), D ** -0.5, 0.1875, ((0, 32),))
    key_weight = normal_values(key_of[5], (D, D), D ** -0.5, 0.1875, ((0, 32),))
    value_weight = normal_values(key_of[6], (D, D), D ** -0.5, 0.1875, ((0, 32),))
    output_weight = normal_values(key_of[7], (D, D), (D // 16) ** -0.5, 0.75, ((0, 32),))
    query_bias = normal_values(key_of[8], (D,), 0.5, 3.0, ((0, 32),))
    key_bias = normal_values(key_of[9], (D,), 0.5, 3.0, ((0, 32),))
    value_bias = normal_values(key_of[10], (D,), 0.5, 3.0, ((0, 32),))
    output_bias = normal_values(key_of[11], (D,), 0.5, 3.0, ((0, 32),))
    attn_gain = jnp.clip(1.0 + 0.18 * jax.random.normal(key_of[12], (D,), jnp.float32), 0.099609375, 1.8984375).astype(jnp.bfloat16)
    attn_shift = normal_values(key_of[13], (D,), 0.5, 3.0, ((0, 32),))
    inner_weight = normal_values(key_of[14], (D, FF), D ** -0.5, 0.1875, ((0, 32),))
    inner_bias = normal_values(key_of[15], (FF,), 0.5, 3.0, ((0, 32),))
    outer_weight = normal_values(key_of[16], (FF, D), FF ** -0.5, 0.09375, ((0, 32),))
    outer_bias = normal_values(key_of[17], (D,), 0.5, 3.0, ((0, 32),))
    final_gain = jnp.clip(1.0 + 0.18 * jax.random.normal(key_of[18], (D,), jnp.float32), 0.099609375, 1.8984375).astype(jnp.bfloat16)
    final_shift = normal_values(key_of[19], (D,), 0.5, 3.0, ((0, 32),))
    proj_weight = normal_values(key_of[20], (D, PROJ), D ** -0.5, 0.1875, ((0, 32),))
    return dict(doc_tokens=doc_tokens, query_tokens=query_tokens, doc_lengths=doc_lengths, positives=positives, query_weight=query_weight, key_weight=key_weight, value_weight=value_weight, output_weight=output_weight, query_bias=query_bias, key_bias=key_bias, value_bias=value_bias, output_bias=output_bias, attn_gain=attn_gain, attn_shift=attn_shift, inner_weight=inner_weight, inner_bias=inner_bias, outer_weight=outer_weight, outer_bias=outer_bias, final_gain=final_gain, final_shift=final_shift, proj_weight=proj_weight)


@jax.custom_vjp
def low(v):
    return lax.optimization_barrier(v.astype(jnp.bfloat16)).astype(jnp.float32)

@jax.custom_vjp
def lowered_gradient_pass(v):
    return v

def low_keep(v):
    return (low(v), None)

def low_pass(kept, grad):
    return (grad,)

def back_keep(v):
    return (v, None)

def back_low(kept, grad):
    return (low(grad),)
low.defvjp(low_keep, low_pass)
lowered_gradient_pass.defvjp(back_keep, back_low)
finest_numeric_accuracy = lax.Precision.HIGHEST
norm_eps = 1e-05
unit_eps = 1e-06
sharpness_divisor = 0.0625
loss_scale = 256.0
masked_value = -1e+30

def dense_apply(operand, matrix):
    return jnp.einsum('...k,kn->...n', operand, matrix, precision=finest_numeric_accuracy)

def rotate_half(values):
    first_half, second_half = jnp.split(values, 2, axis=-1)
    return jnp.concatenate([-second_half, first_half], axis=-1)

def rotary_tables(length, head_size):
    position = jnp.arange(length).astype(jnp.float32)[:, None]
    channel = jnp.arange(head_size // 2).astype(jnp.float32)[None, :]
    angles = position * jnp.exp(channel * (-2.0 * math.log(10000.0) / head_size))
    angles = jnp.concatenate([angles, angles], axis=1)
    return (jnp.cos(angles), jnp.sin(angles))

def apply_rotary(values, cosine, sine_table):
    return values * cosine[:, None, :] + rotate_half(values) * sine_table[:, None, :]

def layer_norm(values, gain, shift):
    center = lax.optimization_barrier(jnp.mean(values, axis=-1, keepdims=True))
    centered = values - center
    variance = lax.optimization_barrier(jnp.mean(centered * centered, axis=-1, keepdims=True))
    return centered * lax.rsqrt(variance + norm_eps) * gain + shift

def gelu_value(values):
    return 0.5 * values * (1.0 + lax.erf(values * math.sqrt(0.5)))

def smooth_peak_value(pairwise_dot_products):
    row_peak = lax.optimization_barrier(jnp.max(pairwise_dot_products, axis=-1, keepdims=True))
    return row_peak[..., 0] + jnp.log(lax.optimization_barrier(jnp.sum(jnp.exp(pairwise_dot_products - row_peak), axis=-1)))

def layer_forward(tokens, key_valid, params):
    w_query, w_key, w_value, w_output, b_query, b_key, b_value, b_output, attn_gain, attn_shift, w_inner, b_inner, w_outer, b_outer, final_gain, final_shift, w_proj = params
    batch_size, length, model_width = tokens.shape
    head_size = model_width // HEADS
    cosine, sine_table = rotary_tables(length, head_size)

    def split_heads(values):
        return values.reshape(batch_size, length, HEADS, head_size)
    query_rot = low(apply_rotary(split_heads(lowered_gradient_pass(dense_apply(tokens, w_query) + b_query)), cosine, sine_table))
    key_rot = low(apply_rotary(split_heads(lowered_gradient_pass(dense_apply(tokens, w_key) + b_key)), cosine, sine_table))
    value_low = low(lowered_gradient_pass(dense_apply(tokens, w_value) + b_value))
    logits = lowered_gradient_pass(jnp.einsum('bqhd,bkhd->bhqk', query_rot, key_rot, precision=finest_numeric_accuracy)) * 0.125
    logits = jnp.where(key_valid[:, None, None, :], logits, masked_value)
    row_peak = lax.optimization_barrier(jnp.max(logits, axis=-1, keepdims=True))
    exponent = jnp.exp(logits - row_peak)
    weights = low(exponent / lax.optimization_barrier(jnp.sum(exponent, axis=-1, keepdims=True)))
    mixed_heads = jnp.einsum('bhqk,bkhd->bqhd', weights, split_heads(value_low), precision=finest_numeric_accuracy)
    mixed_heads = low(lowered_gradient_pass(mixed_heads.reshape(batch_size, length, model_width)))
    attended = lowered_gradient_pass(dense_apply(mixed_heads, w_output) + b_output)
    normed = layer_norm(tokens + attended, attn_gain, attn_shift)
    hidden = lowered_gradient_pass(dense_apply(low(normed), w_inner) + b_inner)
    outer_branch = lowered_gradient_pass(dense_apply(low(gelu_value(hidden)), w_outer) + b_outer)
    states = layer_norm(normed + outer_branch, final_gain, final_shift)
    projected = lowered_gradient_pass(dense_apply(low(states), w_proj))
    encoded_token_arrays = projected * lax.rsqrt(lax.optimization_barrier(jnp.sum(projected * projected, axis=-1, keepdims=True)) + unit_eps)
    return (states, low(encoded_token_arrays))

def query_losses(query_vectors, doc_vectors, doc_lengths, positives):
    question_token_grid = query_vectors.reshape(-1, query_vectors.shape[-1])

    def one_doc(inputs):
        encoded_token_arrays, length = inputs
        pairwise_dot_products = lowered_gradient_pass(jnp.dot(question_token_grid, encoded_token_arrays.T, preferred_element_type=jnp.float32, precision=finest_numeric_accuracy)) / sharpness_divisor
        key_valid = jnp.arange(encoded_token_arrays.shape[0]) < length
        pairwise_dot_products = jnp.where(key_valid[None, :], pairwise_dot_products, masked_value)
        return (sharpness_divisor * smooth_peak_value(pairwise_dot_products)).reshape(-1, QUESTION_TOKENS).sum(axis=1)
    totals = lax.map(jax.checkpoint(one_doc), (doc_vectors, doc_lengths)).T
    is_positive = jnp.arange(totals.shape[1])[None, :] == positives[:, None]
    return smooth_peak_value(totals) - lax.optimization_barrier(jnp.sum(jnp.where(is_positive, totals, 0.0), axis=1))

def reference(doc_tokens, query_tokens, doc_lengths, positives, query_weight, key_weight, value_weight, output_weight, query_bias, key_bias, value_bias, output_bias, attn_gain, attn_shift, inner_weight, inner_bias, outer_weight, outer_bias, final_gain, final_shift, proj_weight):
    params = (query_weight.astype(jnp.float32), key_weight.astype(jnp.float32), value_weight.astype(jnp.float32), output_weight.astype(jnp.float32), query_bias.astype(jnp.float32), key_bias.astype(jnp.float32), value_bias.astype(jnp.float32), output_bias.astype(jnp.float32), attn_gain.astype(jnp.float32), attn_shift.astype(jnp.float32), inner_weight.astype(jnp.float32), inner_bias.astype(jnp.float32), outer_weight.astype(jnp.float32), outer_bias.astype(jnp.float32), final_gain.astype(jnp.float32), final_shift.astype(jnp.float32), proj_weight.astype(jnp.float32))
    doc_values = doc_tokens.astype(jnp.float32)
    query_values = query_tokens.astype(jnp.float32)

    def objective(doc_inputs, query_inputs, weights):

        def one_doc(unused, inputs):
            tokens, length = inputs
            key_valid = (jnp.arange(SLOT) < length)[None, :]
            states, encoded_token_arrays = layer_forward(tokens[None], key_valid, weights)
            return (unused, (states[0], encoded_token_arrays[0]))
        unused, (doc_out, doc_vectors) = lax.scan(jax.checkpoint(one_doc), jnp.zeros((), jnp.float32), (doc_inputs, doc_lengths))
        query_valid = jnp.ones((NQ, QUESTION_TOKENS), dtype=jnp.bool_)
        query_out, query_vectors = layer_forward(query_inputs, query_valid, weights)
        losses = query_losses(query_vectors, doc_vectors, doc_lengths, positives)
        return (loss_scale * jnp.sum(losses), (losses, doc_out, query_out))
    scaled, pullback, (losses, doc_out, query_out) = jax.vjp(objective, doc_values, query_values, params, has_aux=True)
    doc_grad, query_grad, gradients = pullback(jnp.ones_like(scaled))
    g_query_weight, g_key_weight, g_value_weight, g_output_weight, g_query_bias, g_key_bias, g_value_bias, g_output_bias, g_attn_gain, g_attn_shift, g_inner_weight, g_inner_bias, g_outer_weight, g_outer_bias, g_final_gain, g_final_shift, g_proj_weight = gradients
    return (losses, doc_out.astype(jnp.bfloat16), query_out.astype(jnp.bfloat16), doc_grad, query_grad, g_query_weight, g_key_weight, g_value_weight, g_output_weight, g_query_bias, g_key_bias, g_value_bias, g_output_bias, g_attn_gain, g_attn_shift, g_inner_weight, g_inner_bias, g_outer_weight, g_outer_bias, g_final_gain, g_final_shift, g_proj_weight)
```

```python
import functools
import math

import jax
import jax.numpy as jnp
import numpy as np
from jax import lax
from jax.experimental import pallas as pl
from jax.experimental.pallas import tpu as pltpu
from jax.sharding import PartitionSpec as P

HEADS = 16
HEAD = 64
AXES = ("fsdp", "dp")
MESH = pl.DeviceIdType.MESH
f32 = jnp.float32
bf16 = jnp.bfloat16
norm_eps = 1e-05
unit_eps = 1e-06
sharpness_divisor = 0.0625
loss_scale = 256.0
masked_value = -1e30
score_scale = 0.125 * math.log2(math.e)
vmem_bytes = 62 * 1024 * 1024


def nt(a, b):
    return lax.dot_general(a, b, (((1,), (1,)), ((), ())), preferred_element_type=f32)


def nn(a, b):
    return lax.dot_general(a, b, (((1,), (0,)), ((), ())), preferred_element_type=f32)


def tn(a, b):
    return lax.dot_general(a, b, (((0,), (0,)), ((), ())), preferred_element_type=f32)


def lane_of(shape):
    return lax.broadcasted_iota(jnp.int32, shape, 1)


def row_of(shape):
    return lax.broadcasted_iota(jnp.int32, shape, 0)


def wide(table):
    return jnp.concatenate([table, table], axis=1)


def rope(values, cosine, signed_sine):
    width = values.shape[1]
    turned = jnp.where(
        lane_of(values.shape) % HEAD < HEAD // 2,
        pltpu.roll(values, width - HEAD // 2, 1),
        pltpu.roll(values, HEAD // 2, 1),
    )
    return values * cosine + turned * signed_sine


def rope_back(gradient, cosine, signed_sine):
    width = gradient.shape[1]
    scaled = gradient * signed_sine
    turned = jnp.where(
        lane_of(gradient.shape) % HEAD < HEAD // 2,
        pltpu.roll(scaled, width - HEAD // 2, 1),
        pltpu.roll(scaled, HEAD // 2, 1),
    )
    return gradient * cosine + turned


def heads_apart(values, heads):
    rows = values.shape[0]
    tall = jnp.concatenate([values] * heads, axis=0)
    keep = (row_of(tall.shape) // rows) == (lane_of(tall.shape) // HEAD)
    return jnp.where(keep, tall, jnp.zeros_like(tall))


def heads_joined(values, heads):
    rows = values.shape[0] // heads
    keep = (row_of(values.shape) // rows) == (lane_of(values.shape) // HEAD)
    values = jnp.where(keep, values, 0.0)
    total = values[0:rows]
    for h in range(1, heads):
        total = total + values[h * rows : (h + 1) * rows]
    return total


def question_probs(apart, key, question):
    rows = key.shape[0]
    scores = nt(apart, key) * 0.125
    same = (row_of(scores.shape) % rows) // question == lane_of(scores.shape) // question
    scores = jnp.where(same, scores, masked_value)
    weight = jnp.exp(scores - jnp.max(scores, axis=1, keepdims=True))
    return weight / jnp.sum(weight, axis=1, keepdims=True)


def attend_step(slot, question, length_ref, tokens_ref, wq_ref, wk_ref, wv_ref, bias_ref, cos_ref, sin_ref, q_ref, k_ref, v_ref, mixed_ref, mass_ref):
    tokens = tokens_ref[...]
    cosine = wide(cos_ref[...])
    sine = wide(sin_ref[...])
    q_ref[...] = rope(nn(tokens, wq_ref[...]) + bias_ref[0:1, :].astype(f32), cosine, sine).astype(bf16)
    k_ref[...] = rope(nn(tokens, wk_ref[...]) + bias_ref[1:2, :].astype(f32), cosine, sine).astype(bf16)
    v_ref[...] = (nn(tokens, wv_ref[...]) + bias_ref[2:3, :].astype(f32)).astype(bf16)
    total = tokens.shape[0]
    length = length_ref[0]
    pair = (slot, 2 * HEAD)
    lane = lane_of(pair)
    mask = jnp.where(row_of(pair) < length, 0.0, masked_value).astype(bf16)
    for p in range(2):
        cols = slice(p * 2 * HEAD, (p + 1) * 2 * HEAD)
        query = q_ref[0:slot, cols]
        key = k_ref[0:slot, cols]
        value = v_ref[0:slot, cols]
        parts = []
        masses = []
        for h in range(2):
            mine = (lane // HEAD) == h
            spare = (1 - h) * HEAD
            query_h = jnp.where(mine, query, jnp.where(lane == spare, 1.0, 0.0).astype(bf16))
            key_h = jnp.where(lane == spare, mask, key)
            value_h = jnp.where(mine, value, jnp.ones_like(value))
            scores = nt(query_h, key_h)
            peak = jnp.max(scores, axis=1, keepdims=True)
            weight = jnp.exp2((scores - peak) * score_scale).astype(bf16)
            mixed = nn(weight, value_h)
            parts.append(mixed / pltpu.roll(mixed, HEAD, 1))
            masses.append(peak * score_scale + jnp.log2(mixed))
        mixed_ref[0:slot, cols] = jnp.where(lane < HEAD, parts[0], parts[1]).astype(bf16)
        turned = jnp.where(lane < HEAD, masses[1], masses[0]).T
        mass_ref[0, 2 * p : 2 * p + 1, 0:slot] = turned[HEAD : HEAD + 1, :]
        mass_ref[0, 2 * p + 1 : 2 * p + 2, 0:slot] = turned[0:1, :]
    rest = slice(slot, total)
    weight = question_probs(heads_apart(q_ref[rest, :], 4), k_ref[rest, :], question)
    mixed_ref[rest, :] = heads_joined(nn(weight.astype(bf16), v_ref[rest, :]), 4).astype(bf16)


def group_spec(rows):
    return pl.BlockSpec((rows, 4 * HEAD), lambda i: (0, i))


def whole_spec(shape):
    return pl.BlockSpec(shape, lambda i: (0,) * len(shape))


def mass_spec(total):
    return pl.BlockSpec((1, 8, total), lambda i: (i, 0, 0))


def attend_forward(length, tokens, wq, wk, wv, biases, cosine, sine, slot, question):
    total, width = tokens.shape
    groups = width // (4 * HEAD)
    return pl.pallas_call(
        functools.partial(attend_step, slot, question),
        grid=(groups,),
        in_specs=[
            pl.BlockSpec(memory_space=pltpu.SMEM),
            whole_spec((total, width)),
            group_spec(width),
            group_spec(width),
            group_spec(width),
            group_spec(8),
            whole_spec((total, 2 * HEAD)),
            whole_spec((total, 2 * HEAD)),
        ],
        out_specs=[group_spec(total)] * 4 + [mass_spec(total)],
        out_shape=[jax.ShapeDtypeStruct((total, width), bf16)] * 4
        + [jax.ShapeDtypeStruct((groups, 8, total), f32)],
        compiler_params=pltpu.CompilerParams(vmem_limit_bytes=vmem_bytes),
        name="attend_forward",
    )(length, tokens, wq, wk, wv, biases, cosine, sine)


def attend_back_step(slot, question, length_ref, q_ref, k_ref, v_ref, mixed_ref, grad_ref, mass_ref, cos_ref, sin_ref, dq_ref, dk_ref, dv_ref):
    total = q_ref.shape[0]
    length = length_ref[0]
    pair = (slot, 2 * HEAD)
    lane = lane_of(pair)
    mask = jnp.where(row_of(pair) < length, 0.0, masked_value).astype(bf16)
    cosine = cos_ref[0:slot, :]
    sine = sin_ref[0:slot, :]
    for p in range(2):
        cols = slice(p * 2 * HEAD, (p + 1) * 2 * HEAD)
        query = q_ref[0:slot, cols]
        key = k_ref[0:slot, cols]
        value = v_ref[0:slot, cols]
        grad = grad_ref[0:slot, cols]
        key_turned = key.T
        product = (grad.astype(f32) * mixed_ref[0:slot, cols].astype(f32)).T
        dq = []
        dk = []
        dv = []
        for h in range(2):
            mine = (lane // HEAD) == h
            spare = (1 - h) * HEAD
            query_h = jnp.where(mine, query, jnp.where(lane == spare, 1.0, 0.0).astype(bf16))
            key_h = jnp.where(lane == spare, mask, key)
            value_h = jnp.where(mine, value, jnp.zeros_like(value))
            row_dot = jnp.sum(product[h * HEAD : (h + 1) * HEAD], axis=0, keepdims=True)
            mass = mass_ref[0, 2 * p + h : 2 * p + h + 1, 0:slot]
            probs = jnp.exp2(nt(key_h, query_h) * score_scale - mass)
            slope = (probs * (nt(value_h, grad) - row_dot)).astype(bf16)
            dv.append(nn(probs.astype(bf16), grad))
            dk.append(nn(slope, query))
            dq.append(nn(key_turned[h * HEAD : (h + 1) * HEAD], slope))
        dq_all = jnp.concatenate(dq, axis=0).T * 0.125
        dk_all = jnp.where(lane < HEAD, dk[0], dk[1]) * 0.125
        dq_ref[0:slot, cols] = rope_back(dq_all, cosine, sine).astype(bf16)
        dk_ref[0:slot, cols] = rope_back(dk_all, cosine, sine).astype(bf16)
        dv_ref[0:slot, cols] = jnp.where(lane < HEAD, dv[0], dv[1]).astype(bf16)
    rest = slice(slot, total)
    cosine = wide(cos_ref[rest, :])
    sine = wide(sin_ref[rest, :])
    apart = heads_apart(q_ref[rest, :], 4)
    grad_apart = heads_apart(grad_ref[rest, :], 4)
    key = k_ref[rest, :]
    probs = question_probs(apart, key, question)
    grad_prob = nt(grad_apart, v_ref[rest, :])
    row_dot = jnp.sum(probs * grad_prob, axis=1, keepdims=True)
    slope = (probs * (grad_prob - row_dot) * 0.125).astype(bf16)
    dq_ref[rest, :] = rope_back(heads_joined(nn(slope, key), 4), cosine, sine).astype(bf16)
    dk_ref[rest, :] = rope_back(tn(slope, apart), cosine, sine).astype(bf16)
    dv_ref[rest, :] = tn(probs.astype(bf16), grad_apart).astype(bf16)


def attend_backward(length, q, k, v, mixed, grad, mass, cosine, sine, slot, question):
    total, width = q.shape
    groups = width // (4 * HEAD)
    return pl.pallas_call(
        functools.partial(attend_back_step, slot, question),
        grid=(groups,),
        in_specs=[pl.BlockSpec(memory_space=pltpu.SMEM)]
        + [group_spec(total)] * 5
        + [mass_spec(total), whole_spec((total, 2 * HEAD)), whole_spec((total, 2 * HEAD))],
        out_specs=[group_spec(total)] * 3,
        out_shape=[jax.ShapeDtypeStruct((total, width), bf16)] * 3,
        compiler_params=pltpu.CompilerParams(vmem_limit_bytes=vmem_bytes),
        name="attend_backward",
    )(length, q, k, v, mixed, grad, mass, cosine, sine)


class Place:
    def __init__(self):
        y = lax.axis_index("fsdp")
        d = lax.axis_index("dp")
        z, x, c = d // 4, (d // 2) % 2, d % 2
        self.y, self.z, self.x, self.c = y, z, x, c
        x1, y1 = (1 - c) * (1 - x) + c * x, c * (1 - y) + (1 - c) * y
        x2, y2 = c * (1 - x) + (1 - c) * x, (1 - c) * (1 - y) + c * y
        self.first = (y1, z * 4 + x1 * 2 + c)
        self.second = (y2, z * 4 + x2 * 2 + c)
        self.twin = (y, z * 4 + x * 2 + (1 - c))
        self.along = [(y, ((z + k) % 4) * 4 + x * 2 + c) for k in (1, 2, 3)]
        self.lines = [(y, x), (y1, x1), (y2, x2), (1 - y, 1 - x)]

    def greet(self):
        barrier = pltpu.get_barrier_semaphore()
        peers = [self.first, self.second, self.twin] + self.along
        for peer in peers:
            pl.semaphore_signal(barrier, inc=1, device_id=peer, device_id_type=MESH)
        pl.semaphore_wait(barrier, len(peers))


class Sender:
    def __init__(self):
        self.sent = []

    def go(self, src, dst, send_sem, recv_sem, device):
        copy = pltpu.make_async_remote_copy(
            src_ref=src,
            dst_ref=dst,
            send_sem=send_sem,
            recv_sem=recv_sem,
            device_id=device,
            device_id_type=MESH,
        )
        copy.start()
        self.sent.append(copy)

    def drain(self):
        for copy in self.sent:
            copy.wait_send()


def arrived(ref, sem):
    pltpu.make_async_copy(ref, ref, sem).wait()


class Gather:
    def __init__(self, place, shards, wholes, send_sem, recv_sem, own_sem):
        self.at, self.shards, self.wholes = place, shards, wholes
        self.send_sem, self.recv_sem, self.own_sem = send_sem, recv_sem, own_sem
        self.out = Sender()

    def line(self, t, k, core):
        y, x = self.at.lines[k]
        return self.wholes[t].at[y, :, x, core]

    def own(self, t):
        at = self.at
        return pltpu.make_async_copy(
            self.shards[t], self.wholes[t].at[at.y, at.z, at.x, at.c], self.own_sem.at[t]
        )

    def begin(self, t):
        at = self.at
        for k, peer in enumerate(at.along):
            self.out.go(
                self.shards[t],
                self.wholes[t].at[at.y, at.z, at.x, at.c],
                self.send_sem.at[t, k],
                self.recv_sem.at[t, 0],
                peer,
            )
        self.own(t).start()

    def pass_line(self, t, k, targets):
        line = self.line(t, k, self.at.c)
        for send, recv, peer in targets:
            self.out.go(line, line, self.send_sem.at[t, send], self.recv_sem.at[t, recv], peer)

    def own_line(self, t):
        at = self.at
        arrived(self.wholes[t].at[at.y, 0:3, at.x, at.c], self.recv_sem.at[t, 0])
        self.own(t).wait()
        self.pass_line(t, 0, [(3, 1, at.first), (4, 2, at.second), (5, 4, at.twin)])

    def first_line(self, t):
        at = self.at
        arrived(self.line(t, 1, at.c), self.recv_sem.at[t, 1])
        self.pass_line(t, 1, [(6, 3, at.second), (7, 5, at.twin)])

    def second_line(self, t):
        arrived(self.line(t, 2, self.at.c), self.recv_sem.at[t, 2])
        self.pass_line(t, 2, [(8, 6, self.at.twin)])

    def far_line(self, t):
        arrived(self.line(t, 3, self.at.c), self.recv_sem.at[t, 3])
        self.pass_line(t, 3, [(9, 7, self.at.twin)])

    def twin_lines(self, t):
        for k in range(4):
            arrived(self.line(t, k, 1 - self.at.c), self.recv_sem.at[t, 4 + k])


def gather_body(count, *refs):
    shards, wholes = refs[:count], refs[count : 2 * count]
    place = Place()
    place.greet()
    run = Gather(place, shards, wholes, *refs[2 * count :])
    for t in range(count):
        run.begin(t)
    for s in range(count + 2):
        if s < count:
            run.own_line(s)
        if 0 <= s - 1 < count:
            run.first_line(s - 1)
            run.second_line(s - 1)
        if 0 <= s - 2 < count:
            run.far_line(s - 2)
    for t in range(count):
        run.twin_lines(t)
    run.out.drain()


def gather(shards, collective_id):
    count = len(shards)
    wholes = pl.pallas_call(
        functools.partial(gather_body, count),
        in_specs=[pl.BlockSpec(memory_space=pltpu.VMEM)] * count,
        out_specs=[pl.BlockSpec(memory_space=pl.ANY)] * count,
        out_shape=[jax.ShapeDtypeStruct((2, 4, 2, 2) + a.shape, a.dtype) for a in shards],
        scratch_shapes=[
            pltpu.SemaphoreType.DMA((count, 10)),
            pltpu.SemaphoreType.DMA((count, 8)),
            pltpu.SemaphoreType.DMA((count,)),
        ],
        compiler_params=pltpu.CompilerParams(
            collective_id=collective_id, has_side_effects=True, vmem_limit_bytes=vmem_bytes
        ),
        name="gather",
    )(*shards)
    return [w.reshape((32 * a.shape[0],) + a.shape[1:]) for w, a in zip(wholes, shards)]


class Scatter:
    twin_slot = (0, 2, 1, 3)

    def __init__(self, place, parts, outs, buffers, send_sem, recv_sem, own_sem):
        self.at, self.parts, self.outs, self.buffers = place, parts, outs, buffers
        self.send_sem, self.recv_sem, self.own_sem = send_sem, recv_sem, own_sem
        self.out = Sender()

    def own(self, t, k):
        y, x = self.at.lines[k]
        return pltpu.make_async_copy(
            self.parts[t].at[y, :, x, self.at.c], self.buffers[t][0].at[k], self.own_sem.at[t, k]
        )

    def begin(self, t):
        at = self.at
        for k in (3, 2, 1, 0):
            y, x = at.lines[k]
            slot = self.twin_slot[k]
            self.out.go(
                self.parts[t].at[y, :, x, 1 - at.c],
                self.buffers[t][1].at[slot],
                self.send_sem.at[t, k],
                self.recv_sem.at[t, slot],
                at.twin,
            )
            self.own(t, k).start()

    def join_twin(self, t, k):
        total, twin = self.buffers[t][:2]
        self.own(t, k).wait()
        arrived(twin.at[k], self.recv_sem.at[t, k])
        total[k] = total[k] + twin[k]

    def to_second(self, t):
        total, second = self.buffers[t][0], self.buffers[t][2]
        self.join_twin(t, 3)
        self.out.go(total.at[3], second.at[1], self.send_sem.at[t, 4], self.recv_sem.at[t, 5], self.at.second)
        self.join_twin(t, 2)
        self.out.go(total.at[2], second.at[0], self.send_sem.at[t, 5], self.recv_sem.at[t, 4], self.at.second)
        self.join_twin(t, 1)
        self.join_twin(t, 0)

    def to_first(self, t):
        total, second, first = self.buffers[t][0], self.buffers[t][2], self.buffers[t][3]
        arrived(second.at[1], self.recv_sem.at[t, 5])
        total[1] = total[1] + second[1]
        self.out.go(total.at[1], first, self.send_sem.at[t, 6], self.recv_sem.at[t, 6], self.at.first)
        arrived(second.at[0], self.recv_sem.at[t, 4])
        total[0] = total[0] + second[0]

    def to_line(self, t):
        total, first, last = self.buffers[t][0], self.buffers[t][3], self.buffers[t][4]
        arrived(first, self.recv_sem.at[t, 6])
        total[0] = total[0] + first[...]
        for k, peer in enumerate(self.at.along):
            self.out.go(
                total.at[0, (self.at.z + k + 1) % 4],
                last.at[k],
                self.send_sem.at[t, 7 + k],
                self.recv_sem.at[t, 7 + k],
                peer,
            )

    def finish(self, t):
        total, last = self.buffers[t][0], self.buffers[t][4]
        for k in range(3):
            arrived(last.at[k], self.recv_sem.at[t, 7 + k])
        self.outs[t][...] = (total[0, self.at.z].astype(f32) + last[0].astype(f32)) + (
            last[1].astype(f32) + last[2].astype(f32)
        )


def scatter_buffers(shape, dtype):
    return [
        pltpu.VMEM((4, 4) + shape, dtype),
        pltpu.VMEM((4, 4) + shape, dtype),
        pltpu.VMEM((2, 4) + shape, dtype),
        pltpu.VMEM((4,) + shape, dtype),
        pltpu.VMEM((3,) + shape, dtype),
    ]


def scatter_body(count, *refs):
    parts, outs = refs[:count], refs[count : 2 * count]
    flat = refs[2 * count : 7 * count]
    buffers = [flat[5 * t : 5 * t + 5] for t in range(count)]
    place = Place()
    place.greet()
    run = Scatter(place, parts, outs, buffers, *refs[7 * count :])
    for t in range(count):
        run.begin(t)
    for s in range(count + 3):
        if s < count:
            run.to_second(s)
        if 0 <= s - 1 < count:
            run.to_first(s - 1)
        if 0 <= s - 2 < count:
            run.to_line(s - 2)
        if 0 <= s - 3 < count:
            run.finish(s - 3)
    run.out.drain()


def scatter(parts, collective_id):
    count = len(parts)
    shapes = [(p.shape[0] // 32, p.shape[1]) for p in parts]
    scratch = []
    for p, shape in zip(parts, shapes):
        scratch += scatter_buffers(shape, p.dtype)
    return pl.pallas_call(
        functools.partial(scatter_body, count),
        in_specs=[pl.BlockSpec(memory_space=pl.ANY)] * count,
        out_specs=[pl.BlockSpec(memory_space=pltpu.VMEM)] * count,
        out_shape=[jax.ShapeDtypeStruct(shape, f32) for shape in shapes],
        scratch_shapes=scratch
        + [
            pltpu.SemaphoreType.DMA((count, 10)),
            pltpu.SemaphoreType.DMA((count, 10)),
            pltpu.SemaphoreType.DMA((count, 4)),
        ],
        compiler_params=pltpu.CompilerParams(
            collective_id=collective_id, has_side_effects=True, vmem_limit_bytes=vmem_bytes
        ),
        name="scatter",
    )(*[p.reshape((2, 4, 2, 2) + shape) for p, shape in zip(parts, shapes)])


def rotary_tables(slot, question, count):
    place = np.concatenate([np.arange(slot)] + [np.arange(question)] * count)
    channel = np.arange(HEAD // 2, dtype=np.float32)[None, :]
    rate = np.exp(channel * np.float32(-2.0 * math.log(10000.0) / HEAD))
    angle = place.astype(np.float32)[:, None] * rate
    cosine, sine = np.cos(angle), np.sin(angle)
    return (
        jnp.asarray(np.concatenate([cosine] * 4, axis=1)),
        jnp.asarray(np.concatenate([-sine, sine] * 2, axis=1)),
    )


def dense(operand, matrix):
    return jnp.einsum("ld,de->le", operand, matrix, preferred_element_type=f32)


def dense_back(gradient, matrix):
    return jnp.einsum("le,de->ld", gradient, matrix, preferred_element_type=f32)


def weight_grad(operand, gradient):
    return jnp.einsum("ld,le->de", operand, gradient, preferred_element_type=f32).astype(bf16)


def row_sum(values):
    return jnp.sum(values.astype(f32), axis=0)


def normalize_rows(values):
    center = jnp.mean(values, axis=-1, keepdims=True)
    centered = values - center
    variance = jnp.mean(centered * centered, axis=-1, keepdims=True)
    inverse_std = lax.rsqrt(variance + norm_eps)
    return (centered * inverse_std, inverse_std)


def norm_back(gradient, normal, inverse_std):
    return inverse_std * (
        gradient
        - jnp.mean(gradient, axis=-1, keepdims=True)
        - normal * jnp.mean(gradient * normal, axis=-1, keepdims=True)
    )


def gelu_both(values):
    half = 0.5 * (1.0 + lax.erf(values * math.sqrt(0.5)))
    bell = jnp.exp(-0.5 * values * values) * (1.0 / math.sqrt(2.0 * math.pi))
    return (values * half, half + values * bell)


def padded(rows, lanes):
    return jnp.pad(rows, ((0, 0), (0, lanes - rows.shape[1])))


class Close:
    def weights(self, matrices, vectors, wide_vector, positives):
        lanes = wide_vector.shape[0]
        rows = jnp.concatenate(
            [wide_vector[None], padded(jnp.stack(vectors), lanes), padded(positives.astype(bf16)[None], lanes)]
        )
        pack = jnp.pad(rows, ((0, 16 - rows.shape[0]), (0, 0)))
        *wholes, packs = gather(list(matrices) + [pack], 0)
        packs = packs.reshape(32, 16, lanes)
        count, size = len(vectors), vectors[0].shape[0]
        small = packs[:, 1 : 1 + count, :size].transpose(1, 0, 2).reshape(count, 32 * size)
        chosen = packs[:, 1 + count, : positives.shape[0]].reshape(-1).astype(jnp.int32)
        return wholes, small, packs[:, 0].reshape(-1), chosen

    def rows(self, rows):
        return gather([rows], 1)[0]

    def totals(self, totals):
        block = jnp.broadcast_to(padded(totals[None], 128), (8, 128))
        return gather([block], 2)[0].reshape(32, 8, 128)[:, 0, : totals.shape[0]]

    def row_grads(self, grads):
        return scatter([grads], 3)[0]

    def grads(self, matrices, vectors, wide_vector):
        count, size = len(vectors), vectors[0].shape[0] // 32
        lanes = wide_vector.shape[0] // 32
        small = jnp.stack(vectors).reshape(count, 32, size).transpose(1, 0, 2)
        small = jnp.pad(small, ((0, 0), (0, 15 - count), (0, lanes - size)))
        pack = jnp.concatenate([wide_vector.reshape(32, 1, lanes), small], axis=1)
        *shards, packed = scatter(list(matrices) + [pack.reshape(32 * 16, lanes)], 4)
        return shards, [packed[1 + i, :size] for i in range(count)], packed[0]


class Far:
    def one(self, value):
        return lax.all_gather(value, AXES, axis=0, tiled=True)

    def back(self, value):
        return lax.psum_scatter(value.astype(f32), AXES, scatter_dimension=0, tiled=True)

    def weights(self, matrices, vectors, wide_vector, positives):
        return (
            [self.one(m) for m in matrices],
            jnp.stack([self.one(v) for v in vectors]),
            self.one(wide_vector),
            self.one(positives),
        )

    def rows(self, rows):
        return self.one(rows)

    def totals(self, totals):
        return self.one(totals[None])

    def row_grads(self, grads):
        return self.back(grads)

    def grads(self, matrices, vectors, wide_vector):
        return [self.back(m) for m in matrices], [self.back(v) for v in vectors], self.back(wide_vector)


def local(
    link,
    doc_tokens,
    query_tokens,
    doc_lengths,
    positives,
    query_weight,
    key_weight,
    value_weight,
    output_weight,
    query_bias,
    key_bias,
    value_bias,
    output_bias,
    attn_gain,
    attn_shift,
    inner_weight,
    inner_bias,
    outer_weight,
    outer_bias,
    final_gain,
    final_shift,
    proj_weight,
):
    slot, width = doc_tokens.shape[1:]
    count, question = query_tokens.shape[:2]
    tokens = jnp.concatenate([doc_tokens[0], query_tokens.reshape(count * question, width)])
    cosine, sine = rotary_tables(slot, question, count)

    matrices, vectors, b_inner, chosen = link.weights(
        [query_weight, key_weight, value_weight, output_weight, inner_weight, outer_weight, proj_weight],
        [
            query_bias,
            key_bias,
            value_bias,
            output_bias,
            attn_gain,
            attn_shift,
            outer_bias,
            final_gain,
            final_shift,
        ],
        inner_bias,
        positives,
    )
    w_query, w_key, w_value, w_output, w_inner, w_outer, w_proj = matrices
    b_output, g_attn, s_attn, b_outer, g_final, s_final = [vectors[i].astype(f32) for i in range(3, 9)]

    query_rot, key_rot, value_low, mixed, mass = attend_forward(
        doc_lengths, tokens, w_query, w_key, w_value, vectors[0:8], cosine, sine, slot, question
    )
    attended = dense(mixed, w_output) + b_output
    first_normal, first_inverse = normalize_rows(tokens.astype(f32) + attended)
    normed = first_normal * g_attn + s_attn
    normed_low = normed.astype(bf16)
    activated, slope = gelu_both(dense(normed_low, w_inner) + b_inner.astype(f32))
    activated = activated.astype(bf16)
    slope = slope.astype(bf16)
    outer_branch = dense(activated, w_outer) + b_outer
    second_normal, second_inverse = normalize_rows(normed + outer_branch)
    states_low = (second_normal * g_final + s_final).astype(bf16)
    projected = dense(states_low, w_proj)
    inverse_norm = lax.rsqrt(jnp.sum(projected * projected, axis=-1, keepdims=True) + unit_eps)
    encoded = (projected * inverse_norm).astype(bf16)

    doc_rows = encoded[:slot]
    all_rows = link.rows(encoded[slot:])
    key_mask = jnp.arange(slot)[None, :] < doc_lengths[0]
    vector_width = encoded.shape[1]
    block_rows = 32 * question
    row_blocks = all_rows.reshape(-1, block_rows, vector_width)

    def block_scores(rows_block):
        scores = jnp.einsum("qe,ke->qk", rows_block, doc_rows, preferred_element_type=f32)
        return jnp.where(key_mask, scores / sharpness_divisor, masked_value)

    def smooth_block(unused, rows_block):
        scores = block_scores(rows_block)
        peak = jnp.max(scores, axis=1, keepdims=True)
        return unused, sharpness_divisor * (
            peak[:, 0] + jnp.log(jnp.sum(jnp.exp(scores - peak), axis=1))
        )

    unused, smooth = lax.scan(smooth_block, jnp.zeros((), f32), row_blocks)
    totals = smooth.reshape(-1, question).sum(axis=1)
    doc_index = lax.axis_index(AXES)
    all_totals = link.totals(totals)
    peak = jnp.max(all_totals, axis=0)
    log_total = peak + jnp.log(jnp.sum(jnp.exp(all_totals - peak), axis=0))
    hit = jnp.arange(all_totals.shape[0])[:, None] == chosen[None, :]
    losses = log_total - jnp.sum(jnp.where(hit, all_totals, 0.0), axis=0)
    query_loss = lax.dynamic_slice_in_dim(losses, doc_index * count, count, 0)
    coefficient = loss_scale * (jnp.exp(totals - log_total) - (chosen == doc_index).astype(f32))
    token_coefficient = jnp.broadcast_to(coefficient[:, None], (coefficient.shape[0], question))
    token_coefficient = token_coefficient.reshape(row_blocks.shape[0], block_rows)

    def grad_block(doc_grad, inputs):
        rows_block, smooth_rows, coefficient_rows = inputs
        weight = jnp.exp(block_scores(rows_block) - (smooth_rows / sharpness_divisor)[:, None])
        score_grad = (weight * coefficient_rows[:, None]).astype(bf16)
        row_grad = jnp.einsum("qk,ke->qe", score_grad, doc_rows, preferred_element_type=f32)
        doc_grad = doc_grad + jnp.einsum("qk,qe->ke", score_grad, rows_block, preferred_element_type=f32)
        return doc_grad, row_grad

    doc_vector_grad, row_grads = lax.scan(
        grad_block, jnp.zeros(doc_rows.shape, f32), (row_blocks, smooth, token_coefficient)
    )
    query_vector_grad = link.row_grads(row_grads.reshape(-1, vector_width))
    vector_grad = jnp.concatenate([doc_vector_grad, query_vector_grad])

    radial = jnp.sum(vector_grad * projected, axis=-1, keepdims=True)
    proj_grad = (
        vector_grad * inverse_norm - projected * (inverse_norm * inverse_norm * inverse_norm) * radial
    ).astype(bf16)
    proj_weight_grad = weight_grad(states_low, proj_grad)
    states_grad = dense_back(proj_grad, w_proj)
    final_gain_grad = row_sum(states_grad * second_normal)
    final_shift_grad = row_sum(states_grad)
    second_grad = norm_back(states_grad * g_final, second_normal, second_inverse)
    outer_grad = second_grad.astype(bf16)
    outer_weight_grad = weight_grad(activated, outer_grad)
    outer_bias_grad = row_sum(outer_grad)
    hidden_grad = (dense_back(outer_grad, w_outer) * slope.astype(f32)).astype(bf16)
    inner_weight_grad = weight_grad(normed_low, hidden_grad)
    inner_bias_grad = row_sum(hidden_grad)
    normed_grad = second_grad + dense_back(hidden_grad, w_inner)
    attn_gain_grad = row_sum(normed_grad * first_normal)
    attn_shift_grad = row_sum(normed_grad)
    first_grad = norm_back(normed_grad * g_attn, first_normal, first_inverse)
    attended_grad = first_grad.astype(bf16)
    output_weight_grad = weight_grad(mixed, attended_grad)
    output_bias_grad = row_sum(attended_grad)
    mixed_grad = dense_back(attended_grad, w_output).astype(bf16)
    query_grad, key_grad, value_grad = attend_backward(
        doc_lengths, query_rot, key_rot, value_low, mixed, mixed_grad, mass, cosine, sine, slot, question
    )
    tokens_grad = (
        first_grad
        + dense_back(query_grad, w_query)
        + dense_back(key_grad, w_key)
        + dense_back(value_grad, w_value)
    )
    shards, small, inner_bias_shard = link.grads(
        [
            outer_weight_grad,
            inner_weight_grad,
            proj_weight_grad,
            output_weight_grad,
            weight_grad(tokens, query_grad),
            weight_grad(tokens, key_grad),
            weight_grad(tokens, value_grad),
        ],
        [
            row_sum(query_grad),
            row_sum(key_grad),
            row_sum(value_grad),
            output_bias_grad,
            attn_gain_grad,
            attn_shift_grad,
            outer_bias_grad,
            final_gain_grad,
            final_shift_grad,
        ],
        inner_bias_grad,
    )
    outer_shard, inner_shard, proj_shard, output_shard, query_shard, key_shard, value_shard = shards
    return (
        query_loss,
        states_low[None, :slot],
        states_low[slot:].reshape(count, question, width),
        tokens_grad[None, :slot],
        tokens_grad[slot:].reshape(count, question, width),
        query_shard,
        key_shard,
        value_shard,
        output_shard,
        *small[:6],
        inner_shard,
        inner_bias_shard,
        outer_shard,
        *small[6:],
        proj_shard,
    )


def solution(mesh):
    row = P(AXES)
    flat = P(AXES, None)
    deep = P(AXES, None, None)
    in_specs = (deep, deep, row, row) + (flat,) * 4 + (row,) * 6 + (flat, row, flat, row, row, row, flat)
    out_specs = (row, deep, deep, deep, deep) + (flat,) * 4 + (row,) * 6 + (flat, row, flat, row, row, row, flat)
    link = Close() if (mesh.shape["fsdp"], mesh.shape["dp"]) == (2, 16) else Far()
    return jax.shard_map(
        functools.partial(local, link), mesh=mesh, in_specs=in_specs, out_specs=out_specs, check_vma=False
    )
```

```python
import functools
import math

import jax
import jax.numpy as jnp
import numpy as np
from jax import lax
from jax.experimental import pallas as pl
from jax.experimental.pallas import tpu as pltpu
from jax.sharding import PartitionSpec as P

HEADS = 16
HEAD = 64
AXES = ("fsdp", "dp")
MESH = pl.DeviceIdType.MESH
f32 = jnp.float32
bf16 = jnp.bfloat16
norm_eps = 1e-05
unit_eps = 1e-06
sharpness_divisor = 0.0625
loss_scale = 256.0
masked_value = -1e30
score_scale = 0.125 * math.log2(math.e)
vmem_bytes = 62 * 1024 * 1024


def nt(a, b):
    return lax.dot_general(a, b, (((1,), (1,)), ((), ())), preferred_element_type=f32)


def nn(a, b):
    return lax.dot_general(a, b, (((1,), (0,)), ((), ())), preferred_element_type=f32)


def tn(a, b):
    return lax.dot_general(a, b, (((0,), (0,)), ((), ())), preferred_element_type=f32)


def lane_of(shape):
    return lax.broadcasted_iota(jnp.int32, shape, 1)


def row_of(shape):
    return lax.broadcasted_iota(jnp.int32, shape, 0)


def wide(table):
    return jnp.concatenate([table, table], axis=1)


def rope(values, cosine, signed_sine):
    width = values.shape[1]
    turned = jnp.where(
        lane_of(values.shape) % HEAD < HEAD // 2,
        pltpu.roll(values, width - HEAD // 2, 1),
        pltpu.roll(values, HEAD // 2, 1),
    )
    return values * cosine + turned * signed_sine


def rope_back(gradient, cosine, signed_sine):
    width = gradient.shape[1]
    scaled = gradient * signed_sine
    turned = jnp.where(
        lane_of(gradient.shape) % HEAD < HEAD // 2,
        pltpu.roll(scaled, width - HEAD // 2, 1),
        pltpu.roll(scaled, HEAD // 2, 1),
    )
    return gradient * cosine + turned


def heads_apart(values, heads):
    rows = values.shape[0]
    tall = jnp.concatenate([values] * heads, axis=0)
    keep = (row_of(tall.shape) // rows) == (lane_of(tall.shape) // HEAD)
    return jnp.where(keep, tall, jnp.zeros_like(tall))


def heads_joined(values, heads):
    rows = values.shape[0] // heads
    keep = (row_of(values.shape) // rows) == (lane_of(values.shape) // HEAD)
    values = jnp.where(keep, values, 0.0)
    total = values[0:rows]
    for h in range(1, heads):
        total = total + values[h * rows : (h + 1) * rows]
    return total


def question_probs(apart, key, question):
    rows = key.shape[0]
    scores = nt(apart, key) * 0.125
    same = (row_of(scores.shape) % rows) // question == lane_of(scores.shape) // question
    scores = jnp.where(same, scores, masked_value)
    weight = jnp.exp(scores - jnp.max(scores, axis=1, keepdims=True))
    return weight / jnp.sum(weight, axis=1, keepdims=True)


def attend_step(slot, question, length_ref, tokens_ref, wq_ref, wk_ref, wv_ref, bias_ref, cos_ref, sin_ref, q_ref, k_ref, v_ref, mixed_ref, mass_ref, go=lambda part: None):
    tokens = tokens_ref[...]
    cosine = wide(cos_ref[...])
    sine = wide(sin_ref[...])
    q_ref[...] = rope(nn(tokens, wq_ref[...]) + bias_ref[0:1, :].astype(f32), cosine, sine).astype(bf16)
    k_ref[...] = rope(nn(tokens, wk_ref[...]) + bias_ref[1:2, :].astype(f32), cosine, sine).astype(bf16)
    v_ref[...] = (nn(tokens, wv_ref[...]) + bias_ref[2:3, :].astype(f32)).astype(bf16)
    go(0)
    total = tokens.shape[0]
    length = length_ref[0]
    pair = (slot, 2 * HEAD)
    lane = lane_of(pair)
    mask = jnp.where(row_of(pair) < length, 0.0, masked_value).astype(bf16)
    for p in range(2):
        cols = slice(p * 2 * HEAD, (p + 1) * 2 * HEAD)
        query = q_ref[0:slot, cols]
        key = k_ref[0:slot, cols]
        value = v_ref[0:slot, cols]
        parts = []
        masses = []
        for h in range(2):
            mine = (lane // HEAD) == h
            spare = (1 - h) * HEAD
            query_h = jnp.where(mine, query, jnp.where(lane == spare, 1.0, 0.0).astype(bf16))
            key_h = jnp.where(lane == spare, mask, key)
            value_h = jnp.where(mine, value, jnp.ones_like(value))
            scores = nt(query_h, key_h)
            peak = jnp.max(scores, axis=1, keepdims=True)
            weight = jnp.exp2((scores - peak) * score_scale).astype(bf16)
            mixed = nn(weight, value_h)
            parts.append(mixed / pltpu.roll(mixed, HEAD, 1))
            masses.append(peak * score_scale + jnp.log2(mixed))
        mixed_ref[0:slot, cols] = jnp.where(lane < HEAD, parts[0], parts[1]).astype(bf16)
        turned = jnp.where(lane < HEAD, masses[1], masses[0]).T
        mass_ref[0, 2 * p : 2 * p + 1, 0:slot] = turned[HEAD : HEAD + 1, :]
        mass_ref[0, 2 * p + 1 : 2 * p + 2, 0:slot] = turned[0:1, :]
        if p == 0:
            go(1)
    rest = slice(slot, total)
    weight = question_probs(heads_apart(q_ref[rest, :], 4), k_ref[rest, :], question)
    mixed_ref[rest, :] = heads_joined(nn(weight.astype(bf16), v_ref[rest, :]), 4).astype(bf16)
    go(2)


def group_spec(rows):
    return pl.BlockSpec((rows, 4 * HEAD), lambda i: (0, i))


def whole_spec(shape):
    return pl.BlockSpec(shape, lambda i: (0,) * len(shape))


def mass_spec(total):
    return pl.BlockSpec((1, 8, total), lambda i: (i, 0, 0))


def attend_forward(length, tokens, wq, wk, wv, biases, cosine, sine, slot, question):
    total, width = tokens.shape
    groups = width // (4 * HEAD)
    return pl.pallas_call(
        functools.partial(attend_step, slot, question),
        grid=(groups,),
        in_specs=[
            pl.BlockSpec(memory_space=pltpu.SMEM),
            whole_spec((total, width)),
            group_spec(width),
            group_spec(width),
            group_spec(width),
            group_spec(8),
            whole_spec((total, 2 * HEAD)),
            whole_spec((total, 2 * HEAD)),
        ],
        out_specs=[group_spec(total)] * 4 + [mass_spec(total)],
        out_shape=[jax.ShapeDtypeStruct((total, width), bf16)] * 4
        + [jax.ShapeDtypeStruct((groups, 8, total), f32)],
        compiler_params=pltpu.CompilerParams(vmem_limit_bytes=vmem_bytes),
        name="attend_forward",
    )(length, tokens, wq, wk, wv, biases, cosine, sine)


class Place:
    def __init__(self):
        y = lax.axis_index("fsdp")
        d = lax.axis_index("dp")
        z, x, c = d // 4, (d // 2) % 2, d % 2
        self.y, self.z, self.x, self.c = y, z, x, c
        x1, y1 = (1 - c) * (1 - x) + c * x, c * (1 - y) + (1 - c) * y
        x2, y2 = c * (1 - x) + (1 - c) * x, (1 - c) * (1 - y) + c * y
        self.first = (y1, z * 4 + x1 * 2 + c)
        self.second = (y2, z * 4 + x2 * 2 + c)
        self.twin = (y, z * 4 + x * 2 + (1 - c))
        self.along = [(y, ((z + k) % 4) * 4 + x * 2 + c) for k in (1, 2, 3)]
        self.lines = [(y, x), (y1, x1), (y2, x2), (1 - y, 1 - x)]
        self.ahead = [(z + k) % 4 for k in (1, 2, 3)]
        self.other = 1 - c

    def greet(self):
        barrier = pltpu.get_barrier_semaphore()
        peers = [self.first, self.second, self.twin] + self.along
        for peer in peers:
            pl.semaphore_signal(barrier, inc=1, device_id=peer, device_id_type=MESH)
        pl.semaphore_wait(barrier, len(peers))


class Sender:
    def __init__(self):
        self.sent = []

    def go(self, src, dst, send_sem, recv_sem, device):
        copy = pltpu.make_async_remote_copy(
            src_ref=src,
            dst_ref=dst,
            send_sem=send_sem,
            recv_sem=recv_sem,
            device_id=device,
            device_id_type=MESH,
        )
        copy.start()
        self.sent.append(copy)

    def drain(self):
        for copy in self.sent:
            copy.wait_send()


def arrived(ref, sem):
    pltpu.make_async_copy(ref, ref, sem).wait()


class LateSender:
    def __init__(self):
        self.sent = []

    def copy(self, parts):
        src, dst, send_sem, recv_sem, device = parts()
        return pltpu.make_async_remote_copy(
            src_ref=src, dst_ref=dst, send_sem=send_sem, recv_sem=recv_sem, device_id=device, device_id_type=MESH
        )

    def go(self, parts):
        self.copy(parts).start()
        self.sent.append(parts)

    def drain(self):
        for parts in self.sent:
            self.copy(parts).wait_send()


class Gather:
    def __init__(self, place, shards, wholes, send_sem, recv_sem, own_sem):
        self.at, self.shards = place, shards
        self.wholes = [w if isinstance(w, tuple) else (w, ()) for w in wholes]
        self.send_sem, self.recv_sem, self.own_sem = send_sem, recv_sem, own_sem
        self.out = LateSender()

    def block(self, t, *where):
        whole, tail = self.wholes[t]
        return whole.at[where + tail]

    def line(self, t, k, core):
        y, x = self.at.lines[k]
        return self.block(t, y, slice(None), x, core)

    def mine(self, t):
        at = self.at
        return self.block(t, at.y, at.z, at.x, at.c)

    def own(self, t):
        return pltpu.make_async_copy(self.shards[t], self.mine(t), self.own_sem.at[t])

    def begin(self, t):
        for k, peer in enumerate(self.at.along):
            self.out.go(
                lambda k=k, peer=peer: (
                    self.shards[t], self.mine(t), self.send_sem.at[t, k], self.recv_sem.at[t, 0], peer,
                )
            )
        self.own(t).start()

    def pass_line(self, t, k, targets):
        for send, recv, peer in targets:
            self.out.go(
                lambda send=send, recv=recv, peer=peer: (
                    self.line(t, k, self.at.c),
                    self.line(t, k, self.at.c),
                    self.send_sem.at[t, send],
                    self.recv_sem.at[t, recv],
                    peer,
                )
            )

    def own_line(self, t):
        at = self.at
        arrived(self.block(t, at.y, slice(0, 3), at.x, at.c), self.recv_sem.at[t, 0])
        self.own(t).wait()
        self.pass_line(t, 0, [(3, 1, at.first), (4, 2, at.second), (5, 4, at.twin)])

    def first_line(self, t):
        at = self.at
        arrived(self.line(t, 1, at.c), self.recv_sem.at[t, 1])
        self.pass_line(t, 1, [(6, 3, at.second), (7, 5, at.twin)])

    def second_line(self, t):
        arrived(self.line(t, 2, self.at.c), self.recv_sem.at[t, 2])
        self.pass_line(t, 2, [(8, 6, self.at.twin)])

    def far_line(self, t):
        arrived(self.line(t, 3, self.at.c), self.recv_sem.at[t, 3])
        self.pass_line(t, 3, [(9, 7, self.at.twin)])

    def twin_lines(self, t):
        for k in range(4):
            arrived(self.line(t, k, self.at.other), self.recv_sem.at[t, 4 + k])

    def perform(self, names):
        moves = {
            "B": self.begin, "O": self.own_line, "F": self.first_line, "S": self.second_line,
            "R": self.far_line, "T": self.twin_lines,
        }
        for some in names:
            for name in some.split():
                moves[name[0]](int(name[1:]))


def gather_sems(count):
    return [
        pltpu.SemaphoreType.DMA((count, 10)),
        pltpu.SemaphoreType.DMA((count, 8)),
        pltpu.SemaphoreType.DMA((count,)),
    ]


def spread_shape(shard):
    return jax.ShapeDtypeStruct((2, 4, 2, 2) + shard.shape, shard.dtype)


def joined_shards(whole):
    return whole.reshape((32 * whole.shape[4],) + whole.shape[5:])


def gather_body(count, *refs):
    shards, wholes = refs[:count], refs[count : 2 * count]
    place = Place()
    place.greet()
    run = Gather(place, shards, wholes, *refs[2 * count :])
    for t in range(count):
        run.begin(t)
    for s in range(count + 2):
        if s < count:
            run.own_line(s)
        if 0 <= s - 1 < count:
            run.first_line(s - 1)
            run.second_line(s - 1)
        if 0 <= s - 2 < count:
            run.far_line(s - 2)
    for t in range(count):
        run.twin_lines(t)
    run.out.drain()


def gather(shards, collective_id):
    count = len(shards)
    wholes = pl.pallas_call(
        functools.partial(gather_body, count),
        in_specs=[pl.BlockSpec(memory_space=pltpu.VMEM)] * count,
        out_specs=[pl.BlockSpec(memory_space=pl.ANY)] * count,
        out_shape=[spread_shape(a) for a in shards],
        scratch_shapes=gather_sems(count),
        compiler_params=pltpu.CompilerParams(
            collective_id=collective_id, has_side_effects=True, vmem_limit_bytes=vmem_bytes
        ),
        name="gather",
    )(*shards)
    return [joined_shards(w) for w in wholes]


attend_plan = {
    (0, 2): ["O0"],
    (1, 1): ["O1 F0 S0"],
    (2, 0): ["O2 F1 S1 R0"],
    (2, 2): ["O3 F2 S2 R1"],
    (3, 1): ["R2"],
    (3, 2): ["O4 F3 S3"],
    (3, 3): ["F4 S4 R3 R4"],
}


def pump(run, step, plan, steps):
    def go(part):
        for g in range(steps):
            if (g, part) in plan:

                @pl.when(step == g)
                def _():
                    run.perform(plan[g, part])

    return go


def attend_gather_body(slot, question, *refs):
    ins, shards = refs[:8], refs[8:10]
    outs, wholes = refs[10:15], refs[15:17]
    step = pl.program_id(0)
    place = Place()
    width = shards[1].shape[1] // 4
    cuts = [slice(j * width, (j + 1) * width) for j in range(4)]
    units = [shards[0]] + [shards[1].at[:, cut] for cut in cuts]
    places = [wholes[0]] + [(wholes[1], (slice(None), cut)) for cut in cuts]
    run = Gather(place, units, places, *refs[17:])

    @pl.when(step == 0)
    def _():
        place.greet()
        for t in range(len(units)):
            run.begin(t)

    go = pump(run, step, attend_plan, 4)
    attend_step(slot, question, *ins, *outs, go=go)

    @pl.when(step == 3)
    def _():
        run.perform(attend_plan[3, 3])
        for t in range(len(units)):
            run.twin_lines(t)
        run.out.drain()


def attend_gather(length, tokens, wq, wk, wv, biases, cosine, sine, slot, question, shards):
    total, width = tokens.shape
    groups = width // (4 * HEAD)
    once = pl.Buffered(1)

    def kept(shape):
        return pl.BlockSpec(shape, lambda i: (0,) * len(shape), pipeline_mode=once)

    *outs, first, second = pl.pallas_call(
        functools.partial(attend_gather_body, slot, question),
        grid=(groups,),
        in_specs=[
            pl.BlockSpec(memory_space=pltpu.SMEM),
            kept((total, width)),
            group_spec(width),
            group_spec(width),
            group_spec(width),
            group_spec(8),
            kept((total, 2 * HEAD)),
            kept((total, 2 * HEAD)),
        ]
        + [kept(a.shape) for a in shards],
        out_specs=[group_spec(total)] * 4 + [mass_spec(total)] + [pl.BlockSpec(memory_space=pl.ANY)] * 2,
        out_shape=[jax.ShapeDtypeStruct((total, width), bf16)] * 4
        + [jax.ShapeDtypeStruct((groups, 8, total), f32)]
        + [spread_shape(a) for a in shards],
        scratch_shapes=gather_sems(5),
        compiler_params=pltpu.CompilerParams(collective_id=5, has_side_effects=True, vmem_limit_bytes=vmem_bytes),
        name="attend_forward",
    )(length, tokens, wq, wk, wv, biases, cosine, sine, *shards)
    return outs, [joined_shards(first), joined_shards(second)]


inner_plan = {
    (0, 3): ["O0"],
    (2, 0): ["O1 F0 S0"],
    (4, 0): ["F1 S1 R0"],
    (5, 0): ["O2"],
    (6, 0): ["R1"],
    (7, 0): ["O3 F2 S2 O4"],
    (8, 0): ["R2"],
    (8, 1): ["F3 S3 F4 S4", "R3 R4"],
}


def inner_body(refs):
    (tokens_ref, mixed_ref, wo_ref, wi_ref, vec_ref, bias_ref, outer_ref, proj_ref) = refs[:8]
    (normal_ref, inverse_ref, low_ref, act_ref, slope_ref, outer_whole, proj_whole) = refs[8:15]
    step = pl.program_id(0)
    place = Place()
    rows = outer_ref.shape[0] // 4
    cuts = [slice(j * rows, (j + 1) * rows) for j in range(4)]
    units = [outer_ref.at[cut] for cut in cuts] + [proj_ref]
    places = [(outer_whole, (cut,)) for cut in cuts] + [proj_whole]
    run = Gather(place, units, places, *refs[15:])
    total = tokens_ref.shape[0]

    @pl.when(step == 0)
    def _():
        place.greet()
        for t in range(len(units)):
            run.begin(t)
        part = total // 4
        for j in range(4):
            these = slice(j * part, (j + 1) * part)
            attended = nn(mixed_ref[these, :], wo_ref[...]) + vec_ref[0:1, :]
            normal, inverse = normalize_rows(tokens_ref[these, :].astype(f32) + attended)
            normal_ref[these, :] = normal
            inverse_ref[these, :] = jnp.broadcast_to(inverse, (part, inverse_ref.shape[1]))
            low_ref[these, :] = (normal * vec_ref[1:2, :] + vec_ref[2:3, :]).astype(bf16)
            if (0, j) in inner_plan:
                run.perform(inner_plan[0, j])

    @pl.when(step > 0)
    def _():
        part = total // 4

        def some(j, carry):
            these = pl.ds(pl.multiple_of(j * part, 16), part)
            hidden = nn(low_ref[these, :], wi_ref[...]) + bias_ref[...].astype(f32)
            activated, slope = gelu_both(hidden)
            act_ref[these, :] = activated.astype(bf16)
            slope_ref[these, :] = slope.astype(bf16)
            return carry

        lax.fori_loop(0, 4, some, 0)

    for g in range(1, 9):
        if (g, 0) in inner_plan:

            @pl.when(step == g)
            def _():
                run.perform(inner_plan[g, 0])

    @pl.when(step == 8)
    def _():
        run.perform(inner_plan[8, 1])
        for t in range(len(units)):
            run.twin_lines(t)
        run.out.drain()


def inner_forward(tokens, mixed, wo, wi, vectors, bias, shards):
    total, width = tokens.shape
    hidden = wi.shape[1]
    chunk = hidden // 8
    once = pl.Buffered(1)

    def kept(shape):
        return pl.BlockSpec(shape, lambda i: (0,) * len(shape), pipeline_mode=once)

    def chunked(rows):
        return pl.BlockSpec((rows, chunk), lambda i: (0, jnp.maximum(i - 1, 0)))

    *outs, outer, proj = pl.pallas_call(
        lambda *refs: inner_body(refs),
        grid=(9,),
        in_specs=[kept((total, width)), kept((total, width)), kept((width, width)), chunked(width), kept(vectors.shape)]
        + [chunked(1)]
        + [kept(a.shape) for a in shards],
        out_specs=[kept((total, width)), kept((total, 128)), kept((total, width)), chunked(total), chunked(total)]
        + [pl.BlockSpec(memory_space=pl.ANY)] * 2,
        out_shape=[
            jax.ShapeDtypeStruct((total, width), f32),
            jax.ShapeDtypeStruct((total, 128), f32),
            jax.ShapeDtypeStruct((total, width), bf16),
            jax.ShapeDtypeStruct((total, hidden), bf16),
            jax.ShapeDtypeStruct((total, hidden), bf16),
        ]
        + [spread_shape(a) for a in shards],
        scratch_shapes=gather_sems(5),
        compiler_params=pltpu.CompilerParams(collective_id=6, has_side_effects=True, vmem_limit_bytes=vmem_bytes),
        name="inner_forward",
    )(tokens, mixed, wo, wi, vectors, bias, *shards)
    return outs, [joined_shards(outer), joined_shards(proj)]


class Scatter:
    twin_slot = (0, 2, 1, 3)

    def __init__(self, place, parts, outs, buffers, send_sem, recv_sem, own_sem):
        self.at, self.parts, self.outs, self.buffers = place, parts, outs, buffers
        self.send_sem, self.recv_sem, self.own_sem = send_sem, recv_sem, own_sem
        self.out = Sender()

    def own(self, t, k):
        y, x = self.at.lines[k]
        return pltpu.make_async_copy(
            self.parts[t].at[y, :, x, self.at.c], self.buffers[t][0].at[k], self.own_sem.at[t, k]
        )

    def begin(self, t):
        at = self.at
        for k in (3, 2, 1, 0):
            y, x = at.lines[k]
            slot = self.twin_slot[k]
            self.out.go(
                self.parts[t].at[y, :, x, 1 - at.c],
                self.buffers[t][1].at[slot],
                self.send_sem.at[t, k],
                self.recv_sem.at[t, slot],
                at.twin,
            )
            self.own(t, k).start()

    def join_twin(self, t, k):
        total, twin = self.buffers[t][:2]
        self.own(t, k).wait()
        arrived(twin.at[k], self.recv_sem.at[t, k])
        total[k] = total[k] + twin[k]

    def to_second(self, t):
        total, second = self.buffers[t][0], self.buffers[t][2]
        self.join_twin(t, 3)
        self.out.go(total.at[3], second.at[1], self.send_sem.at[t, 4], self.recv_sem.at[t, 5], self.at.second)
        self.join_twin(t, 2)
        self.out.go(total.at[2], second.at[0], self.send_sem.at[t, 5], self.recv_sem.at[t, 4], self.at.second)
        self.join_twin(t, 1)
        self.join_twin(t, 0)

    def to_first(self, t):
        total, second, first = self.buffers[t][0], self.buffers[t][2], self.buffers[t][3]
        arrived(second.at[1], self.recv_sem.at[t, 5])
        total[1] = total[1] + second[1]
        self.out.go(total.at[1], first, self.send_sem.at[t, 6], self.recv_sem.at[t, 6], self.at.first)
        arrived(second.at[0], self.recv_sem.at[t, 4])
        total[0] = total[0] + second[0]

    def to_line(self, t):
        total, first, last = self.buffers[t][0], self.buffers[t][3], self.buffers[t][4]
        arrived(first, self.recv_sem.at[t, 6])
        total[0] = total[0] + first[...]
        for k, peer in enumerate(self.at.along):
            self.out.go(
                total.at[0, (self.at.z + k + 1) % 4],
                last.at[k],
                self.send_sem.at[t, 7 + k],
                self.recv_sem.at[t, 7 + k],
                peer,
            )

    def finish(self, t):
        total, last = self.buffers[t][0], self.buffers[t][4]
        for k in range(3):
            arrived(last.at[k], self.recv_sem.at[t, 7 + k])
        self.outs[t][...] = (total[0, self.at.z].astype(f32) + last[0].astype(f32)) + (
            last[1].astype(f32) + last[2].astype(f32)
        )


def scatter_buffers(shape, dtype):
    return [
        pltpu.VMEM((4, 4) + shape, dtype),
        pltpu.VMEM((4, 4) + shape, dtype),
        pltpu.VMEM((2, 4) + shape, dtype),
        pltpu.VMEM((4,) + shape, dtype),
        pltpu.VMEM((3,) + shape, dtype),
    ]


def scatter_body(count, *refs):
    parts, outs = refs[:count], refs[count : 2 * count]
    flat = refs[2 * count : 7 * count]
    buffers = [flat[5 * t : 5 * t + 5] for t in range(count)]
    place = Place()
    place.greet()
    run = Scatter(place, parts, outs, buffers, *refs[7 * count :])
    for t in range(count):
        run.begin(t)
    for s in range(count + 3):
        if s < count:
            run.to_second(s)
        if 0 <= s - 1 < count:
            run.to_first(s - 1)
        if 0 <= s - 2 < count:
            run.to_line(s - 2)
        if 0 <= s - 3 < count:
            run.finish(s - 3)
    run.out.drain()


def scatter(parts, collective_id):
    count = len(parts)
    shapes = [(p.shape[0] // 32, p.shape[1]) for p in parts]
    scratch = []
    for p, shape in zip(parts, shapes):
        scratch += scatter_buffers(shape, p.dtype)
    return pl.pallas_call(
        functools.partial(scatter_body, count),
        in_specs=[pl.BlockSpec(memory_space=pl.ANY)] * count,
        out_specs=[pl.BlockSpec(memory_space=pltpu.VMEM)] * count,
        out_shape=[jax.ShapeDtypeStruct(shape, f32) for shape in shapes],
        scratch_shapes=scratch
        + [
            pltpu.SemaphoreType.DMA((count, 10)),
            pltpu.SemaphoreType.DMA((count, 10)),
            pltpu.SemaphoreType.DMA((count, 4)),
        ],
        compiler_params=pltpu.CompilerParams(
            collective_id=collective_id, has_side_effects=True, vmem_limit_bytes=vmem_bytes
        ),
        name="scatter",
    )(*[p.reshape((2, 4, 2, 2) + shape) for p, shape in zip(parts, shapes)])


class Unit:
    twin_slot = (0, 2, 1, 3)

    def __init__(self, place, out, mine, twins, buffers, send_sem, recv_sem, own_sem=None):
        self.at, self.out, self.mine, self.twins = place, out, mine, twins
        self.total, self.twin, self.second, self.first, self.last = buffers
        self.send_sem, self.recv_sem, self.own_sem = send_sem, recv_sem, own_sem
        self.sender = LateSender()

    def to_twin(self, k):
        slot = self.twin_slot[k]
        return lambda: (self.twins(k), self.twin.at[slot], self.send_sem.at[k], self.recv_sem.at[slot], self.at.twin)

    def begin(self):
        for k in (3, 2, 1, 0):
            self.sender.copy(self.to_twin(k)).start()
            if self.own_sem is not None:
                self.own(k).start()

    def own(self, k):
        return pltpu.make_async_copy(self.mine(k), self.total.at[k], self.own_sem.at[k])

    def join_twin(self, k):
        if self.own_sem is not None:
            self.own(k).wait()
        arrived(self.twin.at[k], self.recv_sem.at[k])
        if self.own_sem is not None:
            self.total[k] = self.total[k] + self.twin[k]
        else:
            self.total[k] = self.mine(k)[...] + self.twin[k]

    def to_second(self):
        self.join_twin(3)
        self.sender.go(lambda: (self.total.at[3], self.second.at[1], self.send_sem.at[4], self.recv_sem.at[5], self.at.second))
        self.join_twin(2)
        self.sender.go(lambda: (self.total.at[2], self.second.at[0], self.send_sem.at[5], self.recv_sem.at[4], self.at.second))
        self.join_twin(1)
        self.join_twin(0)

    def to_first(self):
        arrived(self.second.at[1], self.recv_sem.at[5])
        self.total[1] = self.total[1] + self.second[1]
        self.sender.go(lambda: (self.total.at[1], self.first, self.send_sem.at[6], self.recv_sem.at[6], self.at.first))
        arrived(self.second.at[0], self.recv_sem.at[4])
        self.total[0] = self.total[0] + self.second[0]

    def to_line(self):
        arrived(self.first, self.recv_sem.at[6])
        self.total[0] = self.total[0] + self.first[...]
        for k, peer in enumerate(self.at.along):
            self.sender.go(lambda k=k, peer=peer: (self.total.at[0, self.at.ahead[k]], self.last.at[k], self.send_sem.at[7 + k], self.recv_sem.at[7 + k], peer))

    def finish(self):
        for k in range(3):
            arrived(self.last.at[k], self.recv_sem.at[7 + k])
        self.out(
            (self.total[0, self.at.z].astype(f32) + self.last[0].astype(f32))
            + (self.last[1].astype(f32) + self.last[2].astype(f32))
        )

    def drain_twin(self):
        for k in range(4):
            self.sender.copy(self.to_twin(k)).wait_send()

    def drain(self):
        self.sender.drain()


class VectorSum:
    def __init__(self, place, value, sums, heard, out, send_sem, recv_sem):
        self.at, self.value, self.sums, self.heard, self.out = place, value, sums, heard, out
        self.send_sem, self.recv_sem = send_sem, recv_sem
        self.sender = LateSender()

    def tell(self, source, slot, peer):
        self.sender.go(lambda: (source(), self.heard.at[slot], self.send_sem.at[slot], self.recv_sem.at[slot], peer))

    def hear(self, slot):
        arrived(self.heard.at[slot], self.recv_sem.at[slot])
        return self.heard[slot]

    def twin(self):
        self.tell(lambda: self.value, 0, self.at.twin)

    def second(self):
        self.sums[0] = self.value[...] + self.hear(0)
        self.tell(lambda: self.sums.at[0], 1, self.at.second)

    def first(self):
        self.sums[1] = self.sums[0] + self.hear(1)
        self.tell(lambda: self.sums.at[1], 2, self.at.first)

    def line(self):
        self.sums[2] = self.sums[1] + self.hear(2)
        for k, peer in enumerate(self.at.along):
            self.tell(lambda: self.sums.at[2], 3 + k, peer)

    def finish(self):
        self.out[...] = (self.sums[2] + self.hear(3)) + (self.hear(4) + self.hear(5))


def back_pair(slot, p, length, q_ref, k_ref, v_ref, mixed_ref, grad_ref, mass_ref, cos_ref, sin_ref, dq_ref, dk_ref, dv_ref):
    pair = (slot, 2 * HEAD)
    lane = lane_of(pair)
    mask = jnp.where(row_of(pair) < length, 0.0, masked_value).astype(bf16)
    cosine = cos_ref[0:slot, :]
    sine = sin_ref[0:slot, :]
    cols = slice(p * 2 * HEAD, (p + 1) * 2 * HEAD)
    query = q_ref[0:slot, cols]
    key = k_ref[0:slot, cols]
    value = v_ref[0:slot, cols]
    grad = grad_ref[0:slot, cols]
    key_turned = key.T
    product = (grad.astype(f32) * mixed_ref[0:slot, cols].astype(f32)).T
    dq = []
    dk = []
    dv = []
    for h in range(2):
        mine = (lane // HEAD) == h
        spare = (1 - h) * HEAD
        query_h = jnp.where(mine, query, jnp.where(lane == spare, 1.0, 0.0).astype(bf16))
        key_h = jnp.where(lane == spare, mask, key)
        value_h = jnp.where(mine, value, jnp.zeros_like(value))
        row_dot = jnp.sum(product[h * HEAD : (h + 1) * HEAD], axis=0, keepdims=True)
        mass = mass_ref[0, 2 * p + h : 2 * p + h + 1, 0:slot]
        probs = jnp.exp2(nt(key_h, query_h) * score_scale - mass)
        slope = (probs * (nt(value_h, grad) - row_dot)).astype(bf16)
        dv.append(nn(probs.astype(bf16), grad))
        dk.append(nn(slope, query))
        dq.append(nn(key_turned[h * HEAD : (h + 1) * HEAD], slope))
    dq_all = jnp.concatenate(dq, axis=0).T * 0.125
    dk_all = jnp.where(lane < HEAD, dk[0], dk[1]) * 0.125
    dq_ref[0:slot, cols] = rope_back(dq_all, cosine, sine).astype(bf16)
    dk_ref[0:slot, cols] = rope_back(dk_all, cosine, sine).astype(bf16)
    dv_ref[0:slot, cols] = jnp.where(lane < HEAD, dv[0], dv[1]).astype(bf16)


def back_questions(slot, question, q_ref, k_ref, v_ref, grad_ref, cos_ref, sin_ref, dq_ref, dk_ref, dv_ref):
    rest = slice(slot, q_ref.shape[0])
    cosine = wide(cos_ref[rest, :])
    sine = wide(sin_ref[rest, :])
    apart = heads_apart(q_ref[rest, :], 4)
    grad_apart = heads_apart(grad_ref[rest, :], 4)
    key = k_ref[rest, :]
    probs = question_probs(apart, key, question)
    grad_prob = nt(grad_apart, v_ref[rest, :])
    row_dot = jnp.sum(probs * grad_prob, axis=1, keepdims=True)
    slope = (probs * (grad_prob - row_dot) * 0.125).astype(bf16)
    dq_ref[rest, :] = rope_back(heads_joined(nn(slope, key), 4), cosine, sine).astype(bf16)
    dk_ref[rest, :] = rope_back(tn(slope, apart), cosine, sine).astype(bf16)
    dv_ref[rest, :] = tn(probs.astype(bf16), grad_apart).astype(bf16)


def attend_back_step(slot, question, length_ref, q_ref, k_ref, v_ref, mixed_ref, grad_ref, mass_ref, cos_ref, sin_ref, dq_ref, dk_ref, dv_ref):
    ins = (q_ref, k_ref, v_ref, mixed_ref, grad_ref, mass_ref, cos_ref, sin_ref)
    for p in range(2):
        back_pair(slot, p, length_ref[0], *ins, dq_ref, dk_ref, dv_ref)
    back_questions(slot, question, q_ref, k_ref, v_ref, grad_ref, cos_ref, sin_ref, dq_ref, dk_ref, dv_ref)


def attend_backward(length, q, k, v, mixed, grad, mass, cosine, sine, slot, question):
    total, width = q.shape
    groups = width // (4 * HEAD)
    return pl.pallas_call(
        functools.partial(attend_back_step, slot, question),
        grid=(groups,),
        in_specs=[pl.BlockSpec(memory_space=pltpu.SMEM)]
        + [group_spec(total)] * 5
        + [mass_spec(total), whole_spec((total, 2 * HEAD)), whole_spec((total, 2 * HEAD))],
        out_specs=[group_spec(total)] * 3,
        out_shape=[jax.ShapeDtypeStruct((total, width), bf16)] * 3,
        compiler_params=pltpu.CompilerParams(vmem_limit_bytes=vmem_bytes),
        name="attend_backward",
    )(length, q, k, v, mixed, grad, mass, cosine, sine)


back_plan = {
    (0, 0): ["B0 B1 B2 B3", "B4 B5 B6 B7", "B8 B9 S0"],
    (0, 1): ["S1 S2 S3"],
    (0, 2): ["S4 S5"],
    (0, 3): ["B10 S6 S7 F0"],
    (1, 1): ["S8 S9 S10 F1"],
    (1, 2): ["F2 L0"],
    (1, 3): ["B11 F3 L1"],
    (2, 1): ["S11 F4 L2"],
    (2, 2): ["F5 L3 E0"],
    (2, 3): ["B12 F6 L4 E1"],
    (3, 1): ["S12 F7 L5 E2"],
    (3, 2): ["F8 F9 F10 L6", "E3"],
    (3, 3): ["B13 Vt F11 L7", "S13 L8 L9 F12", "L10 Vs E4 E5", "L11 Vf F13 E6", "E7 L12 E8 E9", "Vl E10 E11 L13", "E12 Ve E13"],
}


def back_body(slot, question, *refs):
    (length_ref, q_ref, k_ref, v_ref, mixed_ref, grad_ref, mass_ref, cos_ref, sin_ref) = refs[:9]
    (wq_ref, wk_ref, wv_ref, turned_ref, vec_ref, first_ref, outer_ref, inner_ref, output_ref, proj_ref) = refs[9:19]
    (doc_ref, query_ref, outer_out, inner_out, output_out, proj_out, dwq_out, dwk_out, dwv_out, vec_out) = refs[19:29]
    (grads, token_grad, stage, value, sums, heard) = refs[29:35]
    flat = refs[35 : 35 + 14 * 5]
    send_sem, recv_sem, own_sem, vec_send, vec_recv, copy_sem = refs[35 + 14 * 5 :]
    step = pl.program_id(0)
    place = Place()
    group = 4 * HEAD

    def lines(ref, core, *tail):
        return lambda k: ref.at[(place.lines[k][0], slice(None), place.lines[k][1], core) + tail]

    def matrix(u, ref, out, *tail):
        return Unit(
            place,
            out,
            lines(ref, place.c, *tail),
            lines(ref, place.other, *tail),
            flat[5 * u : 5 * u + 5],
            send_sem.at[u],
            recv_sem.at[u],
            own_sem.at[u],
        )

    def into(ref, *where):
        def put(block):
            ref[where] = block

        return put

    everything = slice(None)
    units = []
    rows = outer_out.shape[0] // 4
    for j in range(4):
        part = slice(j * rows, (j + 1) * rows)
        units.append(matrix(j, outer_ref, into(outer_out, part, everything), part))
    columns = inner_out.shape[1] // 4
    for j in range(4):
        part = slice(j * columns, (j + 1) * columns)
        units.append(matrix(4 + j, inner_ref, into(inner_out, everything, part), everything, part))
    units.append(matrix(8, output_ref, into(output_out, everything, everything)))
    units.append(matrix(9, proj_ref, into(proj_out, everything, everything)))

    def heads_out(g):
        part = slice(g * group, (g + 1) * group)

        def put(block):
            for i, ref in enumerate((dwq_out, dwk_out, dwv_out)):
                ref[:, part] = block[:, i * group : (i + 1) * group]

        return put

    for g in range(4):
        here = stage.at[g % 2]
        u = 10 + g
        units.append(
            Unit(
                place,
                heads_out(g),
                lines(here, place.c),
                lines(here, place.other),
                flat[5 * u : 5 * u + 5],
                send_sem.at[u],
                recv_sem.at[u],
            )
        )
    vectors = VectorSum(place, value, sums, heard, vec_out, vec_send, vec_recv)
    moves = {"B": "begin", "S": "to_second", "F": "to_first", "L": "to_line", "E": "finish"}
    tells = {"t": "twin", "s": "second", "f": "first", "l": "line", "e": "finish"}

    def pump(spot):
        for g in range(4):
            todo = [name for some in back_plan.get((g, spot), []) for name in some.split()]
            if todo:

                @pl.when(step == g)
                def _():
                    for name in todo:
                        if name[0] == "V":
                            getattr(vectors, tells[name[1]])()
                        else:
                            getattr(units[int(name[1:])], moves[name[0]])()

    seed = pltpu.make_async_copy(first_ref, token_grad, copy_sem.at[0])

    @pl.when(step == 0)
    def _():
        place.greet()
        seed.start()
        value[...] = vec_ref[...]

    ins = (q_ref, k_ref, v_ref, mixed_ref, grad_ref, mass_ref, cos_ref, sin_ref)
    dq, dk, dv = [grads.at[:, i * group : (i + 1) * group] for i in range(3)]
    pump(0)
    for p in range(2):
        back_pair(slot, p, length_ref[0], *ins, dq, dk, dv)
        pump(1 + p)
    back_questions(slot, question, q_ref, k_ref, v_ref, grad_ref, cos_ref, sin_ref, dq, dk, dv)
    for g in range(2, 4):

        @pl.when(step == g)
        def _():
            units[8 + g].drain_twin()

    weight = nn(turned_ref[...], grads[...]).astype(bf16)
    stage[lax.rem(step, 2)] = weight.reshape(stage.shape[1:])
    column_sums = jnp.sum(grads[...].astype(f32), axis=0, keepdims=True)
    for g in range(4):

        @pl.when(step == g)
        def _():
            for i in range(3):
                value[10 + i : 11 + i, g * group : (g + 1) * group] = column_sums[:, i * group : (i + 1) * group]

    @pl.when(step == 0)
    def _():
        seed.wait()

    token_grad[...] += nt(dq[...], wq_ref[...]) + nt(dk[...], wk_ref[...]) + nt(dv[...], wv_ref[...])
    docs = pltpu.make_async_copy(token_grad.at[0:slot], doc_ref, copy_sem.at[1])
    asked = pltpu.make_async_copy(token_grad.at[slot:], query_ref, copy_sem.at[2])

    @pl.when(step == 3)
    def _():
        docs.start()
        asked.start()

    pump(3)

    @pl.when(step == 3)
    def _():
        for u in range(14):
            if u not in (10, 11):
                units[u].drain_twin()
            units[u].drain()
        vectors.sender.drain()
        docs.wait()
        asked.wait()


def unit_buffers(shape, dtype):
    return [
        pltpu.VMEM((4, 4) + shape, dtype),
        pltpu.VMEM((4, 4) + shape, dtype),
        pltpu.VMEM((2, 4) + shape, dtype),
        pltpu.VMEM((4,) + shape, dtype),
        pltpu.VMEM((3,) + shape, dtype),
    ]


def back_close(length, q, k, v, mixed, grad, mass, cosine, sine, slot, question, tokens, weights, vectors, first_grad, parts):
    total, width = q.shape
    group = 4 * HEAD
    shapes = [(p.shape[0] // 32, p.shape[1]) for p in parts]
    outer, inner, output, proj = shapes
    unit_shapes = [(outer[0] // 4, outer[1])] * 4 + [(inner[0], inner[1] // 4)] * 4 + [output, proj]
    unit_shapes += [(width // 32, 3 * group)] * 4
    scratch = []
    for shape in unit_shapes:
        scratch += unit_buffers(shape, bf16)
    once = pl.Buffered(1)
    hbm = pl.BlockSpec(memory_space=pl.ANY)

    def kept(shape):
        return pl.BlockSpec(shape, lambda i: (0,) * len(shape), pipeline_mode=once)

    shard = (width // 32, width)
    outs = [outer, inner, output, proj, shard, shard, shard, vectors.shape]
    return pl.pallas_call(
        functools.partial(back_body, slot, question),
        grid=(width // group,),
        in_specs=[pl.BlockSpec(memory_space=pltpu.SMEM)]
        + [group_spec(total)] * 3
        + [pl.BlockSpec((total, group), lambda i: (0, i), pipeline_mode=once)] * 2
        + [mass_spec(total), kept((total, 2 * HEAD)), kept((total, 2 * HEAD))]
        + [pl.BlockSpec((width, group), lambda i: (0, i), pipeline_mode=once)] * 3
        + [kept((width, total)), kept(vectors.shape)]
        + [hbm] * 5,
        out_specs=[hbm, hbm] + [kept(shape) for shape in outs],
        out_shape=[jax.ShapeDtypeStruct((slot, width), f32), jax.ShapeDtypeStruct((total - slot, width), f32)]
        + [jax.ShapeDtypeStruct(shape, f32) for shape in outs],
        scratch_shapes=[
            pltpu.VMEM((total, 3 * group), bf16),
            pltpu.VMEM((total, width), f32),
            pltpu.VMEM((2, 2, 4, 2, 2, width // 32, 3 * group), bf16),
            pltpu.VMEM(vectors.shape, f32),
            pltpu.VMEM((3,) + vectors.shape, f32),
            pltpu.VMEM((6,) + vectors.shape, f32),
        ]
        + scratch
        + [
            pltpu.SemaphoreType.DMA((14, 10)),
            pltpu.SemaphoreType.DMA((14, 10)),
            pltpu.SemaphoreType.DMA((14, 4)),
            pltpu.SemaphoreType.DMA((6,)),
            pltpu.SemaphoreType.DMA((6,)),
            pltpu.SemaphoreType.DMA((3,)),
        ],
        compiler_params=pltpu.CompilerParams(collective_id=4, has_side_effects=True, vmem_limit_bytes=67043328),
        name="back",
    )(
        length, q, k, v, mixed, grad, mass, cosine, sine, *weights, tokens.T, vectors, first_grad,
        *[p.reshape((2, 4, 2, 2) + shape) for p, shape in zip(parts, shapes)],
    )


def rotary_tables(slot, question, count):
    place = np.concatenate([np.arange(slot)] + [np.arange(question)] * count)
    channel = np.arange(HEAD // 2, dtype=np.float32)[None, :]
    rate = np.exp(channel * np.float32(-2.0 * math.log(10000.0) / HEAD))
    angle = place.astype(np.float32)[:, None] * rate
    cosine, sine = np.cos(angle), np.sin(angle)
    return (
        jnp.asarray(np.concatenate([cosine] * 4, axis=1)),
        jnp.asarray(np.concatenate([-sine, sine] * 2, axis=1)),
    )


def dense(operand, matrix):
    return jnp.einsum("ld,de->le", operand, matrix, preferred_element_type=f32)


def dense_back(gradient, matrix):
    return jnp.einsum("le,de->ld", gradient, matrix, preferred_element_type=f32)


def weight_grad(operand, gradient):
    return jnp.einsum("ld,le->de", operand, gradient, preferred_element_type=f32).astype(bf16)


def row_sum(values):
    return jnp.sum(values.astype(f32), axis=0)


def normalize_rows(values):
    center = jnp.mean(values, axis=-1, keepdims=True)
    centered = values - center
    variance = jnp.mean(centered * centered, axis=-1, keepdims=True)
    inverse_std = lax.rsqrt(variance + norm_eps)
    return (centered * inverse_std, inverse_std)


def norm_back(gradient, normal, inverse_std):
    return inverse_std * (
        gradient
        - jnp.mean(gradient, axis=-1, keepdims=True)
        - normal * jnp.mean(gradient * normal, axis=-1, keepdims=True)
    )


def gelu_both(values):
    half = 0.5 * (1.0 + lax.erf(values * math.sqrt(0.5)))
    bell = jnp.exp(-0.5 * values * values) * (1.0 / math.sqrt(2.0 * math.pi))
    return (values * half, half + values * bell)


def padded(rows, lanes):
    return jnp.pad(rows, ((0, 0), (0, lanes - rows.shape[1])))


class Close:
    def weights(self, matrices, vectors, wide_vector, positives):
        lanes = wide_vector.shape[0]
        rows = jnp.concatenate(
            [wide_vector[None], padded(jnp.stack(vectors), lanes), padded(positives.astype(bf16)[None], lanes)]
        )
        pack = jnp.pad(rows, ((0, 16 - rows.shape[0]), (0, 0)))
        *wholes, packs = gather(list(matrices) + [pack], 0)
        packs = packs.reshape(32, 16, lanes)
        count, size = len(vectors), vectors[0].shape[0]
        small = packs[:, 1 : 1 + count, :size].transpose(1, 0, 2).reshape(count, 32 * size)
        chosen = packs[:, 1 + count, : positives.shape[0]].reshape(-1).astype(jnp.int32)
        return wholes, small, packs[:, 0].reshape(-1), chosen

    def forward(self, attend, shards, row_vectors, inner_bias):
        tokens = attend[1]
        output_shard, inner_shard, outer_shard, proj_shard = shards
        outs, (w_output, w_inner) = attend_gather(*attend, [output_shard, inner_shard])
        mixed = outs[3]
        (normal, inverse, low, activated, slope), (w_outer, w_proj) = inner_forward(
            tokens, mixed, w_output, w_inner, jnp.stack(row_vectors), inner_bias[None], [outer_shard, proj_shard]
        )
        return outs, normal, inverse[:, :1], low, activated, slope, (w_output, w_inner, w_outer, w_proj)

    def rows(self, rows):
        return gather([rows], 1)[0]

    def totals(self, totals):
        block = jnp.broadcast_to(padded(totals[None], 128), (8, 128))
        return gather([block], 2)[0].reshape(32, 8, 128)[:, 0, : totals.shape[0]]

    def row_grads(self, grads):
        return scatter([grads], 3)[0]

    def back(self, attend, tokens, weights, vectors, inner_bias_grad, first_grad, parts):
        width = tokens.shape[1]
        slot = attend[-2]
        rows = jnp.concatenate([inner_bias_grad.reshape(4, width), jnp.stack(vectors)])
        rows = jnp.pad(rows, ((0, 16 - rows.shape[0]), (0, 0)))
        docs, asked, *shards, sums = back_close(*attend, tokens, weights, rows, first_grad, parts)
        index = lax.axis_index(AXES)
        small = lax.dynamic_slice_in_dim(sums[4:13], index * (width // 32), width // 32, 1)
        inner_bias_shard = lax.dynamic_slice_in_dim(sums[:4].reshape(-1), index * (width // 8), width // 8, 0)
        return docs, asked, shards, [small[i] for i in range(9)], inner_bias_shard


class Far:
    def one(self, value):
        return lax.all_gather(value, AXES, axis=0, tiled=True)

    def weights(self, matrices, vectors, wide_vector, positives):
        return (
            [self.one(m) for m in matrices],
            jnp.stack([self.one(v) for v in vectors]),
            self.one(wide_vector),
            self.one(positives),
        )

    def forward(self, attend, shards, row_vectors, inner_bias):
        tokens = attend[1]
        weights = [self.one(m) for m in shards]
        outs = attend_forward(*attend)
        bias, gain, shift = row_vectors
        normal, inverse = normalize_rows(tokens.astype(f32) + dense(outs[3], weights[0]) + bias)
        low = (normal * gain + shift).astype(bf16)
        activated, slope = gelu_both(dense(low, weights[1]) + inner_bias.astype(f32))
        return outs, normal, inverse, low, activated.astype(bf16), slope.astype(bf16), weights

    def rows(self, rows):
        return self.one(rows)

    def totals(self, totals):
        return self.one(totals[None])

    def row_grads(self, grads):
        return self.spread(grads)

    def spread(self, value):
        return lax.psum_scatter(value.astype(f32), AXES, scatter_dimension=0, tiled=True)

    def back(self, attend, tokens, weights, vectors, inner_bias_grad, first_grad, parts):
        slot = attend[-2]
        grads = attend_backward(*attend)
        total = first_grad
        for grad, weight in zip(grads, weights):
            total = total + dense_back(grad, weight)
        parts = list(parts) + [weight_grad(tokens, grad) for grad in grads]
        vectors = list(vectors) + [row_sum(grad) for grad in grads]
        return (
            total[:slot],
            total[slot:],
            [self.spread(part) for part in parts],
            [self.spread(vector) for vector in vectors],
            self.spread(inner_bias_grad),
        )


def local(
    link,
    doc_tokens,
    query_tokens,
    doc_lengths,
    positives,
    query_weight,
    key_weight,
    value_weight,
    output_weight,
    query_bias,
    key_bias,
    value_bias,
    output_bias,
    attn_gain,
    attn_shift,
    inner_weight,
    inner_bias,
    outer_weight,
    outer_bias,
    final_gain,
    final_shift,
    proj_weight,
):
    slot, width = doc_tokens.shape[1:]
    count, question = query_tokens.shape[:2]
    tokens = jnp.concatenate([doc_tokens[0], query_tokens.reshape(count * question, width)])
    cosine, sine = rotary_tables(slot, question, count)

    matrices, vectors, b_inner, chosen = link.weights(
        [query_weight, key_weight, value_weight],
        [
            query_bias,
            key_bias,
            value_bias,
            output_bias,
            attn_gain,
            attn_shift,
            outer_bias,
            final_gain,
            final_shift,
        ],
        inner_bias,
        positives,
    )
    w_query, w_key, w_value = matrices
    b_output, g_attn, s_attn, b_outer, g_final, s_final = [vectors[i].astype(f32) for i in range(3, 9)]

    outs, first_normal, first_inverse, normed_low, activated, slope, matrices = link.forward(
        (doc_lengths, tokens, w_query, w_key, w_value, vectors[0:8], cosine, sine, slot, question),
        [output_weight, inner_weight, outer_weight, proj_weight],
        [b_output, g_attn, s_attn],
        b_inner,
    )
    query_rot, key_rot, value_low, mixed, mass = outs
    w_output, w_inner, w_outer, w_proj = matrices
    normed = first_normal * g_attn + s_attn
    outer_branch = dense(activated, w_outer) + b_outer
    second_normal, second_inverse = normalize_rows(normed + outer_branch)
    states_low = (second_normal * g_final + s_final).astype(bf16)
    projected = dense(states_low, w_proj)
    inverse_norm = lax.rsqrt(jnp.sum(projected * projected, axis=-1, keepdims=True) + unit_eps)
    encoded = (projected * inverse_norm).astype(bf16)

    doc_rows = encoded[:slot]
    all_rows = link.rows(encoded[slot:])
    key_mask = jnp.arange(slot)[None, :] < doc_lengths[0]
    vector_width = encoded.shape[1]
    block_rows = 32 * question
    row_blocks = all_rows.reshape(-1, block_rows, vector_width)

    def block_scores(rows_block):
        scores = jnp.einsum("qe,ke->qk", rows_block, doc_rows, preferred_element_type=f32)
        return jnp.where(key_mask, scores / sharpness_divisor, masked_value)

    def smooth_block(unused, rows_block):
        scores = block_scores(rows_block)
        peak = jnp.max(scores, axis=1, keepdims=True)
        return unused, sharpness_divisor * (
            peak[:, 0] + jnp.log(jnp.sum(jnp.exp(scores - peak), axis=1))
        )

    unused, smooth = lax.scan(smooth_block, jnp.zeros((), f32), row_blocks)
    totals = smooth.reshape(-1, question).sum(axis=1)
    doc_index = lax.axis_index(AXES)
    all_totals = link.totals(totals)
    peak = jnp.max(all_totals, axis=0)
    log_total = peak + jnp.log(jnp.sum(jnp.exp(all_totals - peak), axis=0))
    hit = jnp.arange(all_totals.shape[0])[:, None] == chosen[None, :]
    losses = log_total - jnp.sum(jnp.where(hit, all_totals, 0.0), axis=0)
    query_loss = lax.dynamic_slice_in_dim(losses, doc_index * count, count, 0)
    coefficient = loss_scale * (jnp.exp(totals - log_total) - (chosen == doc_index).astype(f32))
    token_coefficient = jnp.broadcast_to(coefficient[:, None], (coefficient.shape[0], question))
    token_coefficient = token_coefficient.reshape(row_blocks.shape[0], block_rows)

    def grad_block(doc_grad, inputs):
        rows_block, smooth_rows, coefficient_rows = inputs
        weight = jnp.exp(block_scores(rows_block) - (smooth_rows / sharpness_divisor)[:, None])
        score_grad = (weight * coefficient_rows[:, None]).astype(bf16)
        row_grad = jnp.einsum("qk,ke->qe", score_grad, doc_rows, preferred_element_type=f32)
        doc_grad = doc_grad + jnp.einsum("qk,qe->ke", score_grad, rows_block, preferred_element_type=f32)
        return doc_grad, row_grad

    doc_vector_grad, row_grads = lax.scan(
        grad_block, jnp.zeros(doc_rows.shape, f32), (row_blocks, smooth, token_coefficient)
    )
    query_vector_grad = link.row_grads(row_grads.reshape(-1, vector_width))
    vector_grad = jnp.concatenate([doc_vector_grad, query_vector_grad])

    radial = jnp.sum(vector_grad * projected, axis=-1, keepdims=True)
    proj_grad = (
        vector_grad * inverse_norm - projected * (inverse_norm * inverse_norm * inverse_norm) * radial
    ).astype(bf16)
    proj_weight_grad = weight_grad(states_low, proj_grad)
    states_grad = dense_back(proj_grad, w_proj)
    final_gain_grad = row_sum(states_grad * second_normal)
    final_shift_grad = row_sum(states_grad)
    second_grad = norm_back(states_grad * g_final, second_normal, second_inverse)
    outer_grad = second_grad.astype(bf16)
    outer_weight_grad = weight_grad(activated, outer_grad)
    outer_bias_grad = row_sum(outer_grad)
    hidden_grad = (dense_back(outer_grad, w_outer) * slope.astype(f32)).astype(bf16)
    inner_weight_grad = weight_grad(normed_low, hidden_grad)
    inner_bias_grad = row_sum(hidden_grad)
    normed_grad = second_grad + dense_back(hidden_grad, w_inner)
    attn_gain_grad = row_sum(normed_grad * first_normal)
    attn_shift_grad = row_sum(normed_grad)
    first_grad = norm_back(normed_grad * g_attn, first_normal, first_inverse)
    attended_grad = first_grad.astype(bf16)
    output_weight_grad = weight_grad(mixed, attended_grad)
    output_bias_grad = row_sum(attended_grad)
    mixed_grad = dense_back(attended_grad, w_output).astype(bf16)
    attend = (
        doc_lengths, query_rot, key_rot, value_low, mixed, mixed_grad, mass, cosine, sine, slot, question,
    )
    docs_grad, asked_grad, shards, small, inner_bias_shard = link.back(
        attend,
        tokens,
        (w_query, w_key, w_value),
        [outer_bias_grad, final_gain_grad, final_shift_grad, attn_gain_grad, attn_shift_grad, output_bias_grad],
        inner_bias_grad,
        first_grad,
        [outer_weight_grad, inner_weight_grad, output_weight_grad, proj_weight_grad],
    )
    outer_shard, inner_shard, output_shard, proj_shard, query_shard, key_shard, value_shard = shards
    b_outer_shard, gain_shard, shift_shard, attn_gain_shard, attn_shift_shard, b_output_shard, *b_heads = small
    return (
        query_loss,
        states_low[None, :slot],
        states_low[slot:].reshape(count, question, width),
        docs_grad[None],
        asked_grad.reshape(count, question, width),
        query_shard,
        key_shard,
        value_shard,
        output_shard,
        *b_heads,
        b_output_shard,
        attn_gain_shard,
        attn_shift_shard,
        inner_shard,
        inner_bias_shard,
        outer_shard,
        b_outer_shard,
        gain_shard,
        shift_shard,
        proj_shard,
    )


def solution(mesh):
    row = P(AXES)
    flat = P(AXES, None)
    deep = P(AXES, None, None)
    in_specs = (deep, deep, row, row) + (flat,) * 4 + (row,) * 6 + (flat, row, flat, row, row, row, flat)
    out_specs = (row, deep, deep, deep, deep) + (flat,) * 4 + (row,) * 6 + (flat, row, flat, row, row, row, flat)
    link = Close() if (mesh.shape["fsdp"], mesh.shape["dp"]) == (2, 16) else Far()
    return jax.shard_map(
        functools.partial(local, link), mesh=mesh, in_specs=in_specs, out_specs=out_specs, check_vma=False
    )
```

```python
import functools
import math

import jax
import jax.numpy as jnp
import numpy as np
from jax import lax
from jax.experimental import pallas as pl
from jax.experimental.pallas import tpu as pltpu
from jax.sharding import PartitionSpec as P

HEADS = 16
HEAD = 64
AXES = ("fsdp", "dp")
MESH = pl.DeviceIdType.MESH
f32 = jnp.float32
bf16 = jnp.bfloat16
norm_eps = 1e-05
unit_eps = 1e-06
sharpness_divisor = 0.0625
loss_scale = 256.0
masked_value = -1e30
score_scale = 0.125 * math.log2(math.e)
vmem_bytes = 62 * 1024 * 1024


def nt(a, b):
    return lax.dot_general(a, b, (((1,), (1,)), ((), ())), preferred_element_type=f32)


def nn(a, b):
    return lax.dot_general(a, b, (((1,), (0,)), ((), ())), preferred_element_type=f32)


def tn(a, b):
    return lax.dot_general(a, b, (((0,), (0,)), ((), ())), preferred_element_type=f32)


def lane_of(shape):
    return lax.broadcasted_iota(jnp.int32, shape, 1)


def row_of(shape):
    return lax.broadcasted_iota(jnp.int32, shape, 0)


def wide(table):
    return jnp.concatenate([table, table], axis=1)


def rope(values, cosine, signed_sine):
    width = values.shape[1]
    turned = jnp.where(
        lane_of(values.shape) % HEAD < HEAD // 2,
        pltpu.roll(values, width - HEAD // 2, 1),
        pltpu.roll(values, HEAD // 2, 1),
    )
    return values * cosine + turned * signed_sine


def rope_back(gradient, cosine, signed_sine):
    width = gradient.shape[1]
    scaled = gradient * signed_sine
    turned = jnp.where(
        lane_of(gradient.shape) % HEAD < HEAD // 2,
        pltpu.roll(scaled, width - HEAD // 2, 1),
        pltpu.roll(scaled, HEAD // 2, 1),
    )
    return gradient * cosine + turned


def heads_apart(values, heads):
    rows = values.shape[0]
    tall = jnp.concatenate([values] * heads, axis=0)
    keep = (row_of(tall.shape) // rows) == (lane_of(tall.shape) // HEAD)
    return jnp.where(keep, tall, jnp.zeros_like(tall))


def heads_joined(values, heads):
    rows = values.shape[0] // heads
    keep = (row_of(values.shape) // rows) == (lane_of(values.shape) // HEAD)
    values = jnp.where(keep, values, 0.0)
    total = values[0:rows]
    for h in range(1, heads):
        total = total + values[h * rows : (h + 1) * rows]
    return total


def question_probs(apart, key, question):
    rows = key.shape[0]
    scores = nt(apart, key) * 0.125
    same = (row_of(scores.shape) % rows) // question == lane_of(scores.shape) // question
    scores = jnp.where(same, scores, masked_value)
    weight = jnp.exp(scores - jnp.max(scores, axis=1, keepdims=True))
    return weight / jnp.sum(weight, axis=1, keepdims=True)


def attend_step(slot, question, length_ref, tokens_ref, wq_ref, wk_ref, wv_ref, bias_ref, cos_ref, sin_ref, q_ref, k_ref, v_ref, mixed_ref, mass_ref, go=lambda part: None):
    tokens = tokens_ref[...]
    cosine = wide(cos_ref[...])
    sine = wide(sin_ref[...])
    q_ref[...] = rope(nn(tokens, wq_ref[...]) + bias_ref[0:1, :].astype(f32), cosine, sine).astype(bf16)
    k_ref[...] = rope(nn(tokens, wk_ref[...]) + bias_ref[1:2, :].astype(f32), cosine, sine).astype(bf16)
    v_ref[...] = (nn(tokens, wv_ref[...]) + bias_ref[2:3, :].astype(f32)).astype(bf16)
    go(0)
    total = tokens.shape[0]
    length = length_ref[0]
    pair = (slot, 2 * HEAD)
    lane = lane_of(pair)
    mask = jnp.where(row_of(pair) < length, 0.0, masked_value).astype(bf16)
    for p in range(2):
        cols = slice(p * 2 * HEAD, (p + 1) * 2 * HEAD)
        query = q_ref[0:slot, cols]
        key = k_ref[0:slot, cols]
        value = v_ref[0:slot, cols]
        parts = []
        masses = []
        for h in range(2):
            mine = (lane // HEAD) == h
            spare = (1 - h) * HEAD
            query_h = jnp.where(mine, query, jnp.where(lane == spare, 1.0, 0.0).astype(bf16))
            key_h = jnp.where(lane == spare, mask, key)
            value_h = jnp.where(mine, value, jnp.ones_like(value))
            scores = nt(query_h, key_h)
            peak = jnp.max(scores, axis=1, keepdims=True)
            weight = jnp.exp2((scores - peak) * score_scale).astype(bf16)
            mixed = nn(weight, value_h)
            parts.append(mixed / pltpu.roll(mixed, HEAD, 1))
            masses.append(peak * score_scale + jnp.log2(mixed))
        mixed_ref[0:slot, cols] = jnp.where(lane < HEAD, parts[0], parts[1]).astype(bf16)
        turned = jnp.where(lane < HEAD, masses[1], masses[0]).T
        mass_ref[0, 2 * p : 2 * p + 1, 0:slot] = turned[HEAD : HEAD + 1, :]
        mass_ref[0, 2 * p + 1 : 2 * p + 2, 0:slot] = turned[0:1, :]
        if p == 0:
            go(1)
    rest = slice(slot, total)
    weight = question_probs(heads_apart(q_ref[rest, :], 4), k_ref[rest, :], question)
    mixed_ref[rest, :] = heads_joined(nn(weight.astype(bf16), v_ref[rest, :]), 4).astype(bf16)
    go(2)


def group_spec(rows):
    return pl.BlockSpec((rows, 4 * HEAD), lambda i: (0, i))


def whole_spec(shape):
    return pl.BlockSpec(shape, lambda i: (0,) * len(shape))


def mass_spec(total):
    return pl.BlockSpec((1, 8, total), lambda i: (i, 0, 0))


def attend_forward(length, tokens, wq, wk, wv, biases, cosine, sine, slot, question):
    total, width = tokens.shape
    groups = width // (4 * HEAD)
    return pl.pallas_call(
        functools.partial(attend_step, slot, question),
        grid=(groups,),
        in_specs=[
            pl.BlockSpec(memory_space=pltpu.SMEM),
            whole_spec((total, width)),
            group_spec(width),
            group_spec(width),
            group_spec(width),
            group_spec(8),
            whole_spec((total, 2 * HEAD)),
            whole_spec((total, 2 * HEAD)),
        ],
        out_specs=[group_spec(total)] * 4 + [mass_spec(total)],
        out_shape=[jax.ShapeDtypeStruct((total, width), bf16)] * 4
        + [jax.ShapeDtypeStruct((groups, 8, total), f32)],
        compiler_params=pltpu.CompilerParams(vmem_limit_bytes=vmem_bytes),
        name="attend_forward",
    )(length, tokens, wq, wk, wv, biases, cosine, sine)


class Place:
    def __init__(self):
        y = lax.axis_index("fsdp")
        d = lax.axis_index("dp")
        z, x, c = d // 4, (d // 2) % 2, d % 2
        self.y, self.z, self.x, self.c = y, z, x, c
        x1, y1 = (1 - c) * (1 - x) + c * x, c * (1 - y) + (1 - c) * y
        x2, y2 = c * (1 - x) + (1 - c) * x, (1 - c) * (1 - y) + c * y
        self.first = (y1, z * 4 + x1 * 2 + c)
        self.second = (y2, z * 4 + x2 * 2 + c)
        self.twin = (y, z * 4 + x * 2 + (1 - c))
        self.along = [(y, ((z + k) % 4) * 4 + x * 2 + c) for k in (1, 2, 3)]
        self.lines = [(y, x), (y1, x1), (y2, x2), (1 - y, 1 - x)]
        self.ahead = [(z + k) % 4 for k in (1, 2, 3)]
        self.other = 1 - c

    def greet(self):
        barrier = pltpu.get_barrier_semaphore()
        peers = [self.first, self.second, self.twin] + self.along
        for peer in peers:
            pl.semaphore_signal(barrier, inc=1, device_id=peer, device_id_type=MESH)
        pl.semaphore_wait(barrier, len(peers))


class Sender:
    def __init__(self):
        self.sent = []

    def go(self, src, dst, send_sem, recv_sem, device):
        copy = pltpu.make_async_remote_copy(
            src_ref=src,
            dst_ref=dst,
            send_sem=send_sem,
            recv_sem=recv_sem,
            device_id=device,
            device_id_type=MESH,
        )
        copy.start()
        self.sent.append(copy)

    def drain(self):
        for copy in self.sent:
            copy.wait_send()


def arrived(ref, sem):
    pltpu.make_async_copy(ref, ref, sem).wait()


class LateSender:
    def __init__(self):
        self.sent = []

    def copy(self, parts):
        src, dst, send_sem, recv_sem, device = parts()
        return pltpu.make_async_remote_copy(
            src_ref=src, dst_ref=dst, send_sem=send_sem, recv_sem=recv_sem, device_id=device, device_id_type=MESH
        )

    def go(self, parts):
        self.copy(parts).start()
        self.sent.append(parts)

    def drain(self):
        for parts in self.sent:
            self.copy(parts).wait_send()


class Gather:
    def __init__(self, place, shards, wholes, send_sem, recv_sem, own_sem):
        self.at, self.shards = place, shards
        self.wholes = [w if isinstance(w, tuple) else (w, ()) for w in wholes]
        self.send_sem, self.recv_sem, self.own_sem = send_sem, recv_sem, own_sem
        self.out = LateSender()

    def block(self, t, *where):
        whole, tail = self.wholes[t]
        return whole.at[where + tail]

    def line(self, t, k, core):
        y, x = self.at.lines[k]
        return self.block(t, y, slice(None), x, core)

    def mine(self, t):
        at = self.at
        return self.block(t, at.y, at.z, at.x, at.c)

    def own(self, t):
        return pltpu.make_async_copy(self.shards[t], self.mine(t), self.own_sem.at[t])

    def begin(self, t):
        at = self.at
        targets = [(k, 0, peer) for k, peer in enumerate(at.along)]
        targets += [(3, 1, at.first), (4, 2, at.second), (5, 4, at.twin)]
        for send, recv, peer in targets:
            self.out.go(
                lambda send=send, recv=recv, peer=peer: (
                    self.shards[t], self.mine(t), self.send_sem.at[t, send], self.recv_sem.at[t, recv], peer,
                )
            )
        self.own(t).start()

    def pass_line(self, t, k, targets):
        for send, recv, peer in targets:
            self.out.go(
                lambda send=send, recv=recv, peer=peer: (
                    self.line(t, k, self.at.c),
                    self.line(t, k, self.at.c),
                    self.send_sem.at[t, send],
                    self.recv_sem.at[t, recv],
                    peer,
                )
            )

    def own_line(self, t):
        at = self.at
        arrived(self.block(t, at.y, slice(0, 3), at.x, at.c), self.recv_sem.at[t, 0])
        for j, (recv, peer) in enumerate([(1, at.first), (2, at.second), (4, at.twin)]):
            for k in range(3):
                self.out.go(
                    lambda send=10 + 3 * j + k, recv=recv, peer=peer, z=at.ahead[k]: (
                        self.block(t, at.y, z, at.x, at.c),
                        self.block(t, at.y, z, at.x, at.c),
                        self.send_sem.at[t, send],
                        self.recv_sem.at[t, recv],
                        peer,
                    )
                )

    def first_line(self, t):
        at = self.at
        arrived(self.line(t, 1, at.c), self.recv_sem.at[t, 1])
        self.pass_line(t, 1, [(6, 3, at.second), (7, 5, at.twin)])

    def second_line(self, t):
        arrived(self.line(t, 2, self.at.c), self.recv_sem.at[t, 2])
        self.pass_line(t, 2, [(8, 6, self.at.twin)])

    def far_line(self, t):
        arrived(self.line(t, 3, self.at.c), self.recv_sem.at[t, 3])
        self.pass_line(t, 3, [(9, 7, self.at.twin)])

    def twin_lines(self, t):
        self.own(t).wait()
        for k in range(4):
            arrived(self.line(t, k, self.at.other), self.recv_sem.at[t, 4 + k])

    def perform(self, names):
        moves = {
            "B": self.begin, "O": self.own_line, "F": self.first_line, "S": self.second_line,
            "R": self.far_line, "T": self.twin_lines,
        }
        for some in names:
            for name in some.split():
                moves[name[0]](int(name[1:]))


def gather_sems(count):
    return [
        pltpu.SemaphoreType.DMA((count, 19)),
        pltpu.SemaphoreType.DMA((count, 8)),
        pltpu.SemaphoreType.DMA((count,)),
    ]


def spread_shape(shard):
    return jax.ShapeDtypeStruct((2, 4, 2, 2) + shard.shape, shard.dtype)


def joined_shards(whole):
    return whole.reshape((32 * whole.shape[4],) + whole.shape[5:])


def gather_body(count, *refs):
    shards, wholes = refs[:count], refs[count : 2 * count]
    place = Place()
    place.greet()
    run = Gather(place, shards, wholes, *refs[2 * count :])
    for t in range(count):
        run.begin(t)
    for s in range(count + 2):
        if s < count:
            run.own_line(s)
        if 0 <= s - 1 < count:
            run.first_line(s - 1)
            run.second_line(s - 1)
        if 0 <= s - 2 < count:
            run.far_line(s - 2)
    for t in range(count):
        run.twin_lines(t)
    run.out.drain()


def gather(shards, collective_id):
    count = len(shards)
    wholes = pl.pallas_call(
        functools.partial(gather_body, count),
        in_specs=[pl.BlockSpec(memory_space=pltpu.VMEM)] * count,
        out_specs=[pl.BlockSpec(memory_space=pl.ANY)] * count,
        out_shape=[spread_shape(a) for a in shards],
        scratch_shapes=gather_sems(count),
        compiler_params=pltpu.CompilerParams(
            collective_id=collective_id, has_side_effects=True, vmem_limit_bytes=vmem_bytes
        ),
        name="gather",
    )(*shards)
    return [joined_shards(w) for w in wholes]


attend_plan = {
    (0, 2): ["O0"],
    (1, 1): ["O1"],
    (1, 2): ["F0 S0"],
    (2, 0): ["O2"],
    (2, 1): ["F1 S1"],
    (2, 2): ["R0 O3"],
    (3, 0): ["F2 S2"],
    (3, 1): ["R1 O4"],
    (3, 2): ["F3 S3 R2"],
    (3, 3): ["F4 S4 R3 R4"],
}


def pump(run, step, plan, steps):
    def go(part):
        for g in range(steps):
            if (g, part) in plan:

                @pl.when(step == g)
                def _():
                    run.perform(plan[g, part])

    return go


def attend_gather_body(slot, question, *refs):
    ins, shards = refs[:8], refs[8:10]
    outs, turned_ref, wholes = refs[10:15], refs[15], refs[16:18]
    step = pl.program_id(0)
    place = Place()
    width = shards[1].shape[1] // 4
    cuts = [slice(j * width, (j + 1) * width) for j in range(4)]
    units = [shards[0]] + [shards[1].at[:, cut] for cut in cuts]
    places = [wholes[0]] + [(wholes[1], (slice(None), cut)) for cut in cuts]
    run = Gather(place, units, places, *refs[18:])

    @pl.when(step == 0)
    def _():
        place.greet()
        for t in range(len(units)):
            run.begin(t)

    columns = pl.ds(pl.multiple_of(step * 4 * HEAD, 4 * HEAD), 4 * HEAD)
    turned_ref[:, 0:slot] = ins[1][0:slot, columns].T
    turned_ref[:, slot:] = ins[1][slot:, columns].T
    go = pump(run, step, attend_plan, 4)
    attend_step(slot, question, *ins, *outs, go=go)

    @pl.when(step == 3)
    def _():
        run.perform(attend_plan[3, 3])
        for t in range(len(units)):
            run.twin_lines(t)
        run.out.drain()


def attend_gather(length, tokens, wq, wk, wv, biases, cosine, sine, slot, question, shards):
    total, width = tokens.shape
    groups = width // (4 * HEAD)
    once = pl.Buffered(1)

    def kept(shape):
        return pl.BlockSpec(shape, lambda i: (0,) * len(shape), pipeline_mode=once)

    *outs, turned, first, second = pl.pallas_call(
        functools.partial(attend_gather_body, slot, question),
        grid=(groups,),
        in_specs=[
            pl.BlockSpec(memory_space=pltpu.SMEM),
            kept((total, width)),
            group_spec(width),
            group_spec(width),
            group_spec(width),
            group_spec(8),
            kept((total, 2 * HEAD)),
            kept((total, 2 * HEAD)),
        ]
        + [kept(a.shape) for a in shards],
        out_specs=[group_spec(total)] * 4
        + [mass_spec(total), pl.BlockSpec((4 * HEAD, total), lambda i: (i, 0))]
        + [pl.BlockSpec(memory_space=pl.ANY)] * 2,
        out_shape=[jax.ShapeDtypeStruct((total, width), bf16)] * 4
        + [jax.ShapeDtypeStruct((groups, 8, total), f32), jax.ShapeDtypeStruct((width, total), bf16)]
        + [spread_shape(a) for a in shards],
        scratch_shapes=gather_sems(5),
        compiler_params=pltpu.CompilerParams(collective_id=5, has_side_effects=True, vmem_limit_bytes=vmem_bytes),
        name="attend_forward",
    )(length, tokens, wq, wk, wv, biases, cosine, sine, *shards)
    return outs, turned, [joined_shards(first), joined_shards(second)]


inner_plan = {
    (0, 3): ["O0"],
    (2, 0): ["O1 F0 S0"],
    (4, 0): ["F1 S1 R0"],
    (5, 0): ["O2"],
    (6, 0): ["R1"],
    (7, 0): ["O3 F2 S2 O4"],
    (8, 0): ["R2"],
    (8, 1): ["F3 S3 F4 S4", "R3 R4"],
}


def inner_body(slot, refs):
    (tokens_ref, mixed_ref, wo_ref, wi_ref, vec_ref, bias_ref, outer_ref, proj_ref) = refs[:8]
    (normal_ref, inverse_ref, low_ref, act_ref, slope_ref, turned_ref, outer_whole, proj_whole) = refs[8:16]
    step = pl.program_id(0)
    place = Place()
    rows = outer_ref.shape[0] // 4
    cuts = [slice(j * rows, (j + 1) * rows) for j in range(4)]
    units = [outer_ref.at[cut] for cut in cuts] + [proj_ref]
    places = [(outer_whole, (cut,)) for cut in cuts] + [proj_whole]
    run = Gather(place, units, places, *refs[16:])
    total = tokens_ref.shape[0]

    @pl.when(step == 0)
    def _():
        place.greet()
        for t in range(len(units)):
            run.begin(t)
        part = total // 4
        for j in range(4):
            these = slice(j * part, (j + 1) * part)
            attended = nn(mixed_ref[these, :], wo_ref[...]) + vec_ref[0:1, :]
            normal, inverse = normalize_rows(tokens_ref[these, :].astype(f32) + attended)
            normal_ref[these, :] = normal
            inverse_ref[these, :] = jnp.broadcast_to(inverse, (part, inverse_ref.shape[1]))
            low_ref[these, :] = (normal * vec_ref[1:2, :] + vec_ref[2:3, :]).astype(bf16)
            if (0, j) in inner_plan:
                run.perform(inner_plan[0, j])

    @pl.when(step > 0)
    def _():
        part = total // 4

        def some(j, carry):
            these = pl.ds(pl.multiple_of(j * part, 16), part)
            hidden = nn(low_ref[these, :], wi_ref[...]) + bias_ref[...].astype(f32)
            activated, slope = gelu_both(hidden)
            act_ref[these, :] = activated.astype(bf16)
            slope_ref[these, :] = slope.astype(bf16)
            return carry

        lax.fori_loop(0, 4, some, 0)
        slab = turned_ref.shape[0]
        columns = pl.ds(pl.multiple_of((step - 1) * slab, slab), slab)
        turned_ref[:, 0:slot] = low_ref[0:slot, columns].T
        turned_ref[:, slot:] = low_ref[slot:, columns].T

    for g in range(1, 9):
        if (g, 0) in inner_plan:

            @pl.when(step == g)
            def _():
                run.perform(inner_plan[g, 0])

    @pl.when(step == 8)
    def _():
        run.perform(inner_plan[8, 1])
        for t in range(len(units)):
            run.twin_lines(t)
        run.out.drain()


def inner_forward(tokens, mixed, wo, wi, vectors, bias, slot, shards):
    total, width = tokens.shape
    hidden = wi.shape[1]
    chunk = hidden // 8
    once = pl.Buffered(1)

    def kept(shape):
        return pl.BlockSpec(shape, lambda i: (0,) * len(shape), pipeline_mode=once)

    def chunked(rows):
        return pl.BlockSpec((rows, chunk), lambda i: (0, jnp.maximum(i - 1, 0)))

    *outs, outer, proj = pl.pallas_call(
        lambda *refs: inner_body(slot, refs),
        grid=(9,),
        in_specs=[kept((total, width)), kept((total, width)), kept((width, width)), chunked(width), kept(vectors.shape)]
        + [chunked(1)]
        + [kept(a.shape) for a in shards],
        out_specs=[kept((total, width)), kept((total, 128)), kept((total, width)), chunked(total), chunked(total)]
        + [pl.BlockSpec((width // 8, total), lambda i: (jnp.maximum(i - 1, 0), 0))]
        + [pl.BlockSpec(memory_space=pl.ANY)] * 2,
        out_shape=[
            jax.ShapeDtypeStruct((total, width), f32),
            jax.ShapeDtypeStruct((total, 128), f32),
            jax.ShapeDtypeStruct((total, width), bf16),
            jax.ShapeDtypeStruct((total, hidden), bf16),
            jax.ShapeDtypeStruct((total, hidden), bf16),
            jax.ShapeDtypeStruct((width, total), bf16),
        ]
        + [spread_shape(a) for a in shards],
        scratch_shapes=gather_sems(5),
        compiler_params=pltpu.CompilerParams(collective_id=6, has_side_effects=True, vmem_limit_bytes=vmem_bytes),
        name="inner_forward",
    )(tokens, mixed, wo, wi, vectors, bias, *shards)
    return outs, [joined_shards(outer), joined_shards(proj)]


class Scatter:
    twin_slot = (0, 2, 1, 3)

    def __init__(self, place, parts, outs, buffers, send_sem, recv_sem, own_sem):
        self.at, self.parts, self.outs, self.buffers = place, parts, outs, buffers
        self.send_sem, self.recv_sem, self.own_sem = send_sem, recv_sem, own_sem
        self.out = Sender()

    def own(self, t, k):
        y, x = self.at.lines[k]
        return pltpu.make_async_copy(
            self.parts[t].at[y, :, x, self.at.c], self.buffers[t][0].at[k], self.own_sem.at[t, k]
        )

    def begin(self, t):
        at = self.at
        for k in (3, 2, 1, 0):
            y, x = at.lines[k]
            slot = self.twin_slot[k]
            self.out.go(
                self.parts[t].at[y, :, x, 1 - at.c],
                self.buffers[t][1].at[slot],
                self.send_sem.at[t, k],
                self.recv_sem.at[t, slot],
                at.twin,
            )
            self.own(t, k).start()

    def join_twin(self, t, k):
        total, twin = self.buffers[t][:2]
        self.own(t, k).wait()
        arrived(twin.at[k], self.recv_sem.at[t, k])
        total[k] = total[k] + twin[k]

    def to_second(self, t):
        total, second = self.buffers[t][0], self.buffers[t][2]
        self.join_twin(t, 3)
        self.out.go(total.at[3], second.at[1], self.send_sem.at[t, 4], self.recv_sem.at[t, 5], self.at.second)
        self.join_twin(t, 2)
        self.out.go(total.at[2], second.at[0], self.send_sem.at[t, 5], self.recv_sem.at[t, 4], self.at.second)
        self.join_twin(t, 1)
        self.join_twin(t, 0)

    def to_first(self, t):
        total, second, first = self.buffers[t][0], self.buffers[t][2], self.buffers[t][3]
        arrived(second.at[1], self.recv_sem.at[t, 5])
        total[1] = total[1] + second[1]
        self.out.go(total.at[1], first, self.send_sem.at[t, 6], self.recv_sem.at[t, 6], self.at.first)
        arrived(second.at[0], self.recv_sem.at[t, 4])
        total[0] = total[0] + second[0]

    def to_line(self, t):
        total, first, last = self.buffers[t][0], self.buffers[t][3], self.buffers[t][4]
        arrived(first, self.recv_sem.at[t, 6])
        total[0] = total[0] + first[...]
        for k, peer in enumerate(self.at.along):
            self.out.go(
                total.at[0, (self.at.z + k + 1) % 4],
                last.at[k],
                self.send_sem.at[t, 7 + k],
                self.recv_sem.at[t, 7 + k],
                peer,
            )

    def finish(self, t):
        total, last = self.buffers[t][0], self.buffers[t][4]
        for k in range(3):
            arrived(last.at[k], self.recv_sem.at[t, 7 + k])
        self.outs[t][...] = (total[0, self.at.z].astype(f32) + last[0].astype(f32)) + (
            last[1].astype(f32) + last[2].astype(f32)
        )


def scatter_buffers(shape, dtype):
    return [
        pltpu.VMEM((4, 4) + shape, dtype),
        pltpu.VMEM((4, 4) + shape, dtype),
        pltpu.VMEM((2, 4) + shape, dtype),
        pltpu.VMEM((4,) + shape, dtype),
        pltpu.VMEM((3,) + shape, dtype),
    ]


def scatter_body(count, *refs):
    parts, outs = refs[:count], refs[count : 2 * count]
    flat = refs[2 * count : 7 * count]
    buffers = [flat[5 * t : 5 * t + 5] for t in range(count)]
    place = Place()
    place.greet()
    run = Scatter(place, parts, outs, buffers, *refs[7 * count :])
    for t in range(count):
        run.begin(t)
    for s in range(count + 3):
        if s < count:
            run.to_second(s)
        if 0 <= s - 1 < count:
            run.to_first(s - 1)
        if 0 <= s - 2 < count:
            run.to_line(s - 2)
        if 0 <= s - 3 < count:
            run.finish(s - 3)
    run.out.drain()


def scatter(parts, collective_id):
    count = len(parts)
    shapes = [(p.shape[0] // 32, p.shape[1]) for p in parts]
    scratch = []
    for p, shape in zip(parts, shapes):
        scratch += scatter_buffers(shape, p.dtype)
    return pl.pallas_call(
        functools.partial(scatter_body, count),
        in_specs=[pl.BlockSpec(memory_space=pl.ANY)] * count,
        out_specs=[pl.BlockSpec(memory_space=pltpu.VMEM)] * count,
        out_shape=[jax.ShapeDtypeStruct(shape, f32) for shape in shapes],
        scratch_shapes=scratch
        + [
            pltpu.SemaphoreType.DMA((count, 10)),
            pltpu.SemaphoreType.DMA((count, 10)),
            pltpu.SemaphoreType.DMA((count, 4)),
        ],
        compiler_params=pltpu.CompilerParams(
            collective_id=collective_id, has_side_effects=True, vmem_limit_bytes=vmem_bytes
        ),
        name="scatter",
    )(*[p.reshape((2, 4, 2, 2) + shape) for p, shape in zip(parts, shapes)])


def add_blocks(out, left, right):
    def one(z, carry):
        out[z] = left[z] + right[z]
        return carry

    lax.fori_loop(0, out.shape[0], one, 0)


class Unit:
    twin_slot = (0, 2, 1, 3)

    def __init__(self, place, out, mine, twins, buffers, send_sem, recv_sem, own_sem=None):
        self.at, self.out, self.mine, self.twins = place, out, mine, twins
        self.total, self.twin, self.second, self.first, self.last = buffers
        self.send_sem, self.recv_sem, self.own_sem = send_sem, recv_sem, own_sem
        self.sender = LateSender()

    def to_twin(self, k):
        slot = self.twin_slot[k]
        return lambda: (self.twins(k), self.twin.at[slot], self.send_sem.at[k], self.recv_sem.at[slot], self.at.twin)

    def begin(self):
        for k in (3, 2, 1, 0):
            self.sender.copy(self.to_twin(k)).start()
            if self.own_sem is not None:
                self.own(k).start()

    def own(self, k):
        return pltpu.make_async_copy(self.mine(k), self.total.at[k], self.own_sem.at[k])

    def join_twin(self, k):
        if self.own_sem is not None:
            self.own(k).wait()
        arrived(self.twin.at[k], self.recv_sem.at[k])
        base = self.total.at[k] if self.own_sem is not None else self.mine(k)
        add_blocks(self.total.at[k], base, self.twin.at[k])

    def to_second(self):
        self.join_twin(3)
        self.sender.go(lambda: (self.total.at[3], self.second.at[1], self.send_sem.at[4], self.recv_sem.at[5], self.at.second))
        self.join_twin(2)
        self.sender.go(lambda: (self.total.at[2], self.second.at[0], self.send_sem.at[5], self.recv_sem.at[4], self.at.second))
        self.join_twin(1)
        self.join_twin(0)

    def to_first(self):
        arrived(self.second.at[1], self.recv_sem.at[5])
        add_blocks(self.total.at[1], self.total.at[1], self.second.at[1])
        self.sender.go(lambda: (self.total.at[1], self.first, self.send_sem.at[6], self.recv_sem.at[6], self.at.first))
        arrived(self.second.at[0], self.recv_sem.at[4])
        add_blocks(self.total.at[0], self.total.at[0], self.second.at[0])

    def to_line(self):
        arrived(self.first, self.recv_sem.at[6])
        add_blocks(self.total.at[0], self.total.at[0], self.first)
        for k, peer in enumerate(self.at.along):
            self.sender.go(lambda k=k, peer=peer: (self.total.at[0, self.at.ahead[k]], self.last.at[k], self.send_sem.at[7 + k], self.recv_sem.at[7 + k], peer))

    def finish(self):
        for k in range(3):
            arrived(self.last.at[k], self.recv_sem.at[7 + k])
        self.out(
            (self.total[0, self.at.z].astype(f32) + self.last[0].astype(f32))
            + (self.last[1].astype(f32) + self.last[2].astype(f32))
        )

    def drain_twin(self):
        for k in range(4):
            self.sender.copy(self.to_twin(k)).wait_send()

    def drain(self):
        self.sender.drain()


class VectorSum:
    def __init__(self, place, value, sums, heard, out, send_sem, recv_sem):
        self.at, self.value, self.sums, self.heard, self.out = place, value, sums, heard, out
        self.send_sem, self.recv_sem = send_sem, recv_sem
        self.sender = LateSender()

    def tell(self, source, slot, peer):
        self.sender.go(lambda: (source(), self.heard.at[slot], self.send_sem.at[slot], self.recv_sem.at[slot], peer))

    def hear(self, slot):
        arrived(self.heard.at[slot], self.recv_sem.at[slot])
        return self.heard[slot]

    def twin(self):
        self.tell(lambda: self.value, 0, self.at.twin)

    def second(self):
        self.sums[0] = self.value[...] + self.hear(0)
        self.tell(lambda: self.sums.at[0], 1, self.at.second)

    def first(self):
        self.sums[1] = self.sums[0] + self.hear(1)
        self.tell(lambda: self.sums.at[1], 2, self.at.first)

    def line(self):
        self.sums[2] = self.sums[1] + self.hear(2)
        for k, peer in enumerate(self.at.along):
            self.tell(lambda: self.sums.at[2], 3 + k, peer)

    def finish(self):
        self.out[...] = (self.sums[2] + self.hear(3)) + (self.hear(4) + self.hear(5))


def back_pair(slot, p, length, q_ref, k_ref, v_ref, mixed_ref, grad_ref, mass_ref, cos_ref, sin_ref, dq_ref, dk_ref, dv_ref):
    pair = (slot, 2 * HEAD)
    lane = lane_of(pair)
    mask = jnp.where(row_of(pair) < length, 0.0, masked_value).astype(bf16)
    cosine = cos_ref[0:slot, :]
    sine = sin_ref[0:slot, :]
    cols = slice(p * 2 * HEAD, (p + 1) * 2 * HEAD)
    query = q_ref[0:slot, cols]
    key = k_ref[0:slot, cols]
    value = v_ref[0:slot, cols]
    grad = grad_ref[0:slot, cols]
    key_turned = key.T
    product = (grad.astype(f32) * mixed_ref[0:slot, cols].astype(f32)).T
    dq = []
    dk = []
    dv = []
    for h in range(2):
        mine = (lane // HEAD) == h
        spare = (1 - h) * HEAD
        query_h = jnp.where(mine, query, jnp.where(lane == spare, 1.0, 0.0).astype(bf16))
        key_h = jnp.where(lane == spare, mask, key)
        value_h = jnp.where(mine, value, jnp.zeros_like(value))
        row_dot = jnp.sum(product[h * HEAD : (h + 1) * HEAD], axis=0, keepdims=True)
        mass = mass_ref[0, 2 * p + h : 2 * p + h + 1, 0:slot]
        probs = jnp.exp2(nt(key_h, query_h) * score_scale - mass)
        slope = (probs * (nt(value_h, grad) - row_dot)).astype(bf16)
        dv.append(nn(probs.astype(bf16), grad))
        dk.append(nn(slope, query))
        dq.append(nn(key_turned[h * HEAD : (h + 1) * HEAD], slope))
    dq_all = jnp.concatenate(dq, axis=0).T * 0.125
    dk_all = jnp.where(lane < HEAD, dk[0], dk[1]) * 0.125
    dq_ref[0:slot, cols] = rope_back(dq_all, cosine, sine).astype(bf16)
    dk_ref[0:slot, cols] = rope_back(dk_all, cosine, sine).astype(bf16)
    dv_ref[0:slot, cols] = jnp.where(lane < HEAD, dv[0], dv[1]).astype(bf16)


def back_questions(slot, question, q_ref, k_ref, v_ref, grad_ref, cos_ref, sin_ref, dq_ref, dk_ref, dv_ref):
    rest = slice(slot, q_ref.shape[0])
    cosine = wide(cos_ref[rest, :])
    sine = wide(sin_ref[rest, :])
    apart = heads_apart(q_ref[rest, :], 4)
    grad_apart = heads_apart(grad_ref[rest, :], 4)
    key = k_ref[rest, :]
    probs = question_probs(apart, key, question)
    grad_prob = nt(grad_apart, v_ref[rest, :])
    row_dot = jnp.sum(probs * grad_prob, axis=1, keepdims=True)
    slope = (probs * (grad_prob - row_dot) * 0.125).astype(bf16)
    dq_ref[rest, :] = rope_back(heads_joined(nn(slope, key), 4), cosine, sine).astype(bf16)
    dk_ref[rest, :] = rope_back(tn(slope, apart), cosine, sine).astype(bf16)
    dv_ref[rest, :] = tn(probs.astype(bf16), grad_apart).astype(bf16)


def attend_back_step(slot, question, length_ref, q_ref, k_ref, v_ref, mixed_ref, grad_ref, mass_ref, cos_ref, sin_ref, dq_ref, dk_ref, dv_ref):
    ins = (q_ref, k_ref, v_ref, mixed_ref, grad_ref, mass_ref, cos_ref, sin_ref)
    for p in range(2):
        back_pair(slot, p, length_ref[0], *ins, dq_ref, dk_ref, dv_ref)
    back_questions(slot, question, q_ref, k_ref, v_ref, grad_ref, cos_ref, sin_ref, dq_ref, dk_ref, dv_ref)


def attend_backward(length, q, k, v, mixed, grad, mass, cosine, sine, slot, question):
    total, width = q.shape
    groups = width // (4 * HEAD)
    return pl.pallas_call(
        functools.partial(attend_back_step, slot, question),
        grid=(groups,),
        in_specs=[pl.BlockSpec(memory_space=pltpu.SMEM)]
        + [group_spec(total)] * 5
        + [mass_spec(total), whole_spec((total, 2 * HEAD)), whole_spec((total, 2 * HEAD))],
        out_specs=[group_spec(total)] * 3,
        out_shape=[jax.ShapeDtypeStruct((total, width), bf16)] * 3,
        compiler_params=pltpu.CompilerParams(vmem_limit_bytes=vmem_bytes),
        name="attend_backward",
    )(length, q, k, v, mixed, grad, mass, cosine, sine)


middle_plan = {
    (1, 0): ["S0"],
    (2, 0): ["S1"],
    (2, 1): ["F0"],
    (3, 0): ["S2 L0"],
    (3, 1): ["F1"],
    (4, 0): ["S3 L1"],
    (4, 1): ["F2"],
    (5, 0): ["E0 L2"],
    (5, 1): ["F3"],
    (6, 0): ["E1"],
    (6, 1): ["L3"],
    (7, 0): ["E2"],
    (7, 1): ["E3"],
}
scatter_moves = {"B": "begin", "S": "to_second", "F": "to_first", "L": "to_line", "E": "finish"}


def middle_body(refs):
    (grad_ref, second_ref, turned_ref, wo_ref, wi_ref, slope_ref, part_ref) = refs[:7]
    (normed_ref, inner_ref, bias_ref, out_ref) = refs[7:11]
    hidden_ref, seed_ref = refs[11:13]
    flat = refs[13:33]
    send_sem, recv_sem, own_sem, seed_sem = refs[33:]
    step = pl.program_id(0)
    place = Place()
    rows = out_ref.shape[0] // 4

    def lines(core, part):
        return lambda k: part_ref.at[place.lines[k][0], :, place.lines[k][1], core, part]

    def put(part):
        def write(block):
            out_ref[part, :] = block

        return write

    units = []
    for u in range(4):
        part = slice(u * rows, (u + 1) * rows)
        units.append(
            Unit(
                place,
                put(part),
                lines(place.c, part),
                lines(place.other, part),
                flat[5 * u : 5 * u + 5],
                send_sem.at[u],
                recv_sem.at[u],
                own_sem.at[u],
            )
        )

    def go(part):
        for g in range(8):
            if (g, part) in middle_plan:

                @pl.when(step == g)
                def _():
                    for some in middle_plan[g, part]:
                        for name in some.split():
                            getattr(units[int(name[1:])], scatter_moves[name[0]])()

    @pl.when(step == 0)
    def _():
        place.greet()
        for unit in units:
            unit.begin()
        pltpu.make_async_copy(second_ref, seed_ref, seed_sem.at[0]).start()
        normed_ref[...] = jnp.zeros_like(normed_ref)

    half = grad_ref.shape[0] // 2

    def some_rows(j, sums):
        these = pl.ds(pl.multiple_of(j * half, 16), half)
        hidden = (nt(grad_ref[these, :], wo_ref[...]) * slope_ref[these, :].astype(f32)).astype(bf16)
        hidden_ref[these, :] = hidden
        normed_ref[these, :] += nt(hidden, wi_ref[...])
        return sums + jnp.sum(hidden.astype(f32), axis=0, keepdims=True)

    sums = lax.fori_loop(0, 2, some_rows, jnp.zeros((1, hidden_ref.shape[1]), f32))
    bias_ref[...] = jnp.broadcast_to(sums, bias_ref.shape)
    go(0)
    quarter = turned_ref.shape[0] // 2

    def some_columns(j, carry):
        these = pl.ds(pl.multiple_of(j * quarter, 16), quarter)
        inner_ref[these, :] = nn(turned_ref[these, :], hidden_ref[...]).astype(bf16)
        return carry

    lax.fori_loop(0, 2, some_columns, 0)
    go(1)

    @pl.when(step == 7)
    def _():
        pltpu.make_async_copy(second_ref, seed_ref, seed_sem.at[0]).wait()
        normed_ref[...] += seed_ref[...]
        for unit in units:
            unit.drain_twin()
            unit.drain()


def middle_back(grad, second, turned, wo, wi, slope, part):
    total, width = grad.shape
    hidden = wi.shape[1]
    chunk = hidden // 8
    shard = part.shape[0] // 32
    once = pl.Buffered(1)

    def kept(shape):
        return pl.BlockSpec(shape, lambda i: (0,) * len(shape), pipeline_mode=once)

    def chunked(rows):
        return pl.BlockSpec((rows, chunk), lambda i: (0, i))

    scratch = [pltpu.VMEM((total, chunk), bf16), pltpu.VMEM((total, width), f32)]
    for u in range(4):
        scratch += unit_buffers((shard // 4, width), bf16)
    return pl.pallas_call(
        lambda *refs: middle_body(refs),
        grid=(8,),
        in_specs=[
            kept((total, width)),
            pl.BlockSpec(memory_space=pl.ANY),
            kept((width, total)),
            pl.BlockSpec((chunk, width), lambda i: (i, 0)),
            chunked(width),
            chunked(total),
            pl.BlockSpec(memory_space=pl.ANY),
        ],
        out_specs=[kept((total, width)), chunked(width), chunked(8), kept((shard, width))],
        out_shape=[
            jax.ShapeDtypeStruct((total, width), f32),
            jax.ShapeDtypeStruct((width, hidden), bf16),
            jax.ShapeDtypeStruct((8, hidden), f32),
            jax.ShapeDtypeStruct((shard, width), f32),
        ],
        scratch_shapes=scratch
        + [
            pltpu.SemaphoreType.DMA((4, 10)),
            pltpu.SemaphoreType.DMA((4, 10)),
            pltpu.SemaphoreType.DMA((4, 4)),
            pltpu.SemaphoreType.DMA((1,)),
        ],
        compiler_params=pltpu.CompilerParams(collective_id=7, has_side_effects=True, vmem_limit_bytes=vmem_bytes),
        name="middle",
    )(grad, second, turned, wo, wi, slope, part.reshape((2, 4, 2, 2, shard, width)))


back_plan = {
    (0, 0): ["B0 B1 B2 B3", "B4 B5"],
    (0, 2): ["S0"],
    (0, 3): ["S1"],
    (0, 4): ["B6"],
    (1, 1): ["S2 F0"],
    (1, 2): ["S3 F1 L0"],
    (1, 3): ["S4 S5 F2 L1"],
    (1, 4): ["B7"],
    (2, 1): ["S6 F3 L2 E0"],
    (2, 2): ["S7 F4 F5 L3", "E1"],
    (2, 3): ["F6 L4 L5 E2"],
    (2, 4): ["B8"],
    (3, 1): ["S8 F7 L6 E3"],
    (3, 2): ["F8 L7 E4 E5"],
    (3, 3): ["S9 Vt L8 E6", "F9 Vs E7 L9", "Vf E8 Vl E9", "Ve"],
    (3, 4): ["B9"],
}


def back_body(slot, question, *refs):
    (length_ref, q_ref, k_ref, v_ref, mixed_ref, grad_ref, mass_ref, cos_ref, sin_ref) = refs[:9]
    (wq_ref, wk_ref, wv_ref, turned_ref, vec_ref, first_ref, inner_ref, output_ref, proj_ref) = refs[9:18]
    (doc_ref, query_ref, inner_out, output_out, proj_out, dwq_out, dwk_out, dwv_out, vec_out) = refs[18:27]
    (grads, token_grad, stage, value, sums, heard) = refs[27:33]
    flat = refs[33 : 33 + 10 * 5]
    send_sem, recv_sem, own_sem, vec_send, vec_recv, copy_sem = refs[33 + 10 * 5 :]
    step = pl.program_id(0)
    place = Place()
    group = 4 * HEAD

    def lines(ref, core, *tail):
        return lambda k: ref.at[(place.lines[k][0], slice(None), place.lines[k][1], core) + tail]

    def matrix(u, ref, out, *tail):
        return Unit(
            place,
            out,
            lines(ref, place.c, *tail),
            lines(ref, place.other, *tail),
            flat[5 * u : 5 * u + 5],
            send_sem.at[u],
            recv_sem.at[u],
            own_sem.at[u],
        )

    def into(ref, *where):
        def put(block):
            ref[where] = block

        return put

    everything = slice(None)
    units = []
    columns = inner_out.shape[1] // 4
    for j in range(4):
        part = slice(j * columns, (j + 1) * columns)
        units.append(matrix(j, inner_ref, into(inner_out, everything, part), everything, part))
    units.append(matrix(4, output_ref, into(output_out, everything, everything)))
    units.append(matrix(5, proj_ref, into(proj_out, everything, everything)))

    def heads_out(g):
        part = slice(g * group, (g + 1) * group)

        def put(block):
            for i, ref in enumerate((dwq_out, dwk_out, dwv_out)):
                ref[:, part] = block[:, i * group : (i + 1) * group]

        return put

    for g in range(4):
        here = stage.at[g % 2]
        u = 6 + g
        units.append(
            Unit(
                place,
                heads_out(g),
                lines(here, place.c),
                lines(here, place.other),
                flat[5 * u : 5 * u + 5],
                send_sem.at[u],
                recv_sem.at[u],
            )
        )
    vectors = VectorSum(place, value, sums, heard, vec_out, vec_send, vec_recv)
    tells = {"t": "twin", "s": "second", "f": "first", "l": "line", "e": "finish"}

    def pump(spot):
        for g in range(4):
            todo = [name for some in back_plan.get((g, spot), []) for name in some.split()]
            if todo:

                @pl.when(step == g)
                def _():
                    for name in todo:
                        if name[0] == "V":
                            getattr(vectors, tells[name[1]])()
                        else:
                            getattr(units[int(name[1:])], scatter_moves[name[0]])()

    seed = pltpu.make_async_copy(first_ref, token_grad, copy_sem.at[0])

    @pl.when(step == 0)
    def _():
        place.greet()
        seed.start()
        value[...] = vec_ref[...]

    ins = (q_ref, k_ref, v_ref, mixed_ref, grad_ref, mass_ref, cos_ref, sin_ref)
    dq, dk, dv = [grads.at[:, i * group : (i + 1) * group] for i in range(3)]
    pump(0)
    for p in range(2):
        back_pair(slot, p, length_ref[0], *ins, dq, dk, dv)
        pump(1 + p)
    back_questions(slot, question, q_ref, k_ref, v_ref, grad_ref, cos_ref, sin_ref, dq, dk, dv)
    for g in range(2, 4):

        @pl.when(step == g)
        def _():
            units[4 + g].drain_twin()

    weight = nn(turned_ref[...], grads[...]).astype(bf16)
    stage[lax.rem(step, 2)] = weight.reshape(stage.shape[1:])
    column_sums = jnp.sum(grads[...].astype(f32), axis=0, keepdims=True)
    for g in range(4):

        @pl.when(step == g)
        def _():
            for i in range(3):
                value[10 + i : 11 + i, g * group : (g + 1) * group] = column_sums[:, i * group : (i + 1) * group]

    pump(4)

    @pl.when(step == 0)
    def _():
        seed.wait()

    token_grad[...] += nt(dq[...], wq_ref[...]) + nt(dk[...], wk_ref[...]) + nt(dv[...], wv_ref[...])
    docs = pltpu.make_async_copy(token_grad.at[0:slot], doc_ref, copy_sem.at[1])
    asked = pltpu.make_async_copy(token_grad.at[slot:], query_ref, copy_sem.at[2])

    @pl.when(step == 3)
    def _():
        docs.start()
        asked.start()

    pump(3)

    @pl.when(step == 3)
    def _():
        for u in range(10):
            if u not in (6, 7):
                units[u].drain_twin()
            units[u].drain()
        vectors.sender.drain()
        docs.wait()
        asked.wait()


def unit_buffers(shape, dtype):
    return [
        pltpu.VMEM((4, 4) + shape, dtype),
        pltpu.VMEM((4, 4) + shape, dtype),
        pltpu.VMEM((2, 4) + shape, dtype),
        pltpu.VMEM((4,) + shape, dtype),
        pltpu.VMEM((3,) + shape, dtype),
    ]


def back_close(length, q, k, v, mixed, grad, mass, cosine, sine, slot, question, tokens, weights, vectors, first_grad, parts):
    total, width = q.shape
    group = 4 * HEAD
    shapes = [(p.shape[0] // 32, p.shape[1]) for p in parts]
    inner, output, proj = shapes
    unit_shapes = [(inner[0], inner[1] // 4)] * 4 + [output, proj]
    unit_shapes += [(width // 32, 3 * group)] * 4
    scratch = []
    for shape in unit_shapes:
        scratch += unit_buffers(shape, bf16)
    once = pl.Buffered(1)
    hbm = pl.BlockSpec(memory_space=pl.ANY)

    def kept(shape):
        return pl.BlockSpec(shape, lambda i: (0,) * len(shape), pipeline_mode=once)

    shard = (width // 32, width)
    outs = [inner, output, proj, shard, shard, shard, vectors.shape]
    return pl.pallas_call(
        functools.partial(back_body, slot, question),
        grid=(width // group,),
        in_specs=[pl.BlockSpec(memory_space=pltpu.SMEM)]
        + [group_spec(total)] * 3
        + [pl.BlockSpec((total, group), lambda i: (0, i), pipeline_mode=once)] * 2
        + [mass_spec(total), kept((total, 2 * HEAD)), kept((total, 2 * HEAD))]
        + [pl.BlockSpec((width, group), lambda i: (0, i), pipeline_mode=once)] * 3
        + [kept((width, total)), kept(vectors.shape)]
        + [hbm] * 4,
        out_specs=[hbm, hbm] + [kept(shape) for shape in outs],
        out_shape=[jax.ShapeDtypeStruct((slot, width), f32), jax.ShapeDtypeStruct((total - slot, width), f32)]
        + [jax.ShapeDtypeStruct(shape, f32) for shape in outs],
        scratch_shapes=[
            pltpu.VMEM((total, 3 * group), bf16),
            pltpu.VMEM((total, width), f32),
            pltpu.VMEM((2, 2, 4, 2, 2, width // 32, 3 * group), bf16),
            pltpu.VMEM(vectors.shape, f32),
            pltpu.VMEM((3,) + vectors.shape, f32),
            pltpu.VMEM((6,) + vectors.shape, f32),
        ]
        + scratch
        + [
            pltpu.SemaphoreType.DMA((10, 10)),
            pltpu.SemaphoreType.DMA((10, 10)),
            pltpu.SemaphoreType.DMA((10, 4)),
            pltpu.SemaphoreType.DMA((6,)),
            pltpu.SemaphoreType.DMA((6,)),
            pltpu.SemaphoreType.DMA((3,)),
        ],
        compiler_params=pltpu.CompilerParams(collective_id=4, has_side_effects=True, vmem_limit_bytes=67043328),
        name="back",
    )(
        length, q, k, v, mixed, grad, mass, cosine, sine, *weights, tokens, vectors, first_grad,
        *[p.reshape((2, 4, 2, 2) + shape) for p, shape in zip(parts, shapes)],
    )


def rotary_tables(slot, question, count):
    place = np.concatenate([np.arange(slot)] + [np.arange(question)] * count)
    channel = np.arange(HEAD // 2, dtype=np.float32)[None, :]
    rate = np.exp(channel * np.float32(-2.0 * math.log(10000.0) / HEAD))
    angle = place.astype(np.float32)[:, None] * rate
    cosine, sine = np.cos(angle), np.sin(angle)
    return (
        jnp.asarray(np.concatenate([cosine] * 4, axis=1)),
        jnp.asarray(np.concatenate([-sine, sine] * 2, axis=1)),
    )


def dense(operand, matrix):
    return jnp.einsum("ld,de->le", operand, matrix, preferred_element_type=f32)


def dense_back(gradient, matrix):
    return jnp.einsum("le,de->ld", gradient, matrix, preferred_element_type=f32)


def weight_grad(operand, gradient):
    return jnp.einsum("ld,le->de", operand, gradient, preferred_element_type=f32).astype(bf16)


def row_sum(values):
    return jnp.sum(values.astype(f32), axis=0)


def normalize_rows(values):
    center = jnp.mean(values, axis=-1, keepdims=True)
    centered = values - center
    variance = jnp.mean(centered * centered, axis=-1, keepdims=True)
    inverse_std = lax.rsqrt(variance + norm_eps)
    return (centered * inverse_std, inverse_std)


def norm_back(gradient, normal, inverse_std):
    return inverse_std * (
        gradient
        - jnp.mean(gradient, axis=-1, keepdims=True)
        - normal * jnp.mean(gradient * normal, axis=-1, keepdims=True)
    )


def gelu_both(values):
    half = 0.5 * (1.0 + lax.erf(values * math.sqrt(0.5)))
    bell = jnp.exp(-0.5 * values * values) * (1.0 / math.sqrt(2.0 * math.pi))
    return (values * half, half + values * bell)


def padded(rows, lanes):
    return jnp.pad(rows, ((0, 0), (0, lanes - rows.shape[1])))


class Close:
    def weights(self, matrices, vectors, wide_vector, positives):
        lanes = wide_vector.shape[0]
        rows = jnp.concatenate(
            [wide_vector[None], padded(jnp.stack(vectors), lanes), padded(positives.astype(bf16)[None], lanes)]
        )
        pack = jnp.pad(rows, ((0, 16 - rows.shape[0]), (0, 0)))
        *wholes, packs = gather(list(matrices) + [pack], 0)
        packs = packs.reshape(32, 16, lanes)
        count, size = len(vectors), vectors[0].shape[0]
        small = packs[:, 1 : 1 + count, :size].transpose(1, 0, 2).reshape(count, 32 * size)
        chosen = packs[:, 1 + count, : positives.shape[0]].reshape(-1).astype(jnp.int32)
        return wholes, small, packs[:, 0].reshape(-1), chosen

    def forward(self, attend, shards, row_vectors, inner_bias):
        tokens = attend[1]
        output_shard, inner_shard, outer_shard, proj_shard = shards
        slot = attend[-2]
        outs, turned, (w_output, w_inner) = attend_gather(*attend, [output_shard, inner_shard])
        mixed = outs[3]
        (normal, inverse, low, activated, slope, low_turned), (w_outer, w_proj) = inner_forward(
            tokens, mixed, w_output, w_inner, jnp.stack(row_vectors), inner_bias[None], slot, [outer_shard, proj_shard]
        )
        return outs, normal, inverse[:, :1], (low_turned, turned), activated, slope, (w_output, w_inner, w_outer, w_proj)

    def rows(self, rows):
        return gather([rows], 1)[0]

    def totals(self, totals):
        block = jnp.broadcast_to(padded(totals[None], 128), (8, 128))
        return gather([block], 2)[0].reshape(32, 8, 128)[:, 0, : totals.shape[0]]

    def row_grads(self, grads):
        return scatter([grads], 3)[0]

    def middle(self, grad, second, low, w_outer, w_inner, slope, part):
        normed_grad, inner_grad, bias, shard = middle_back(grad, second, low, w_outer, w_inner, slope, part)
        return normed_grad, inner_grad, bias[0], shard

    def back(self, attend, tokens, weights, vectors, inner_bias_grad, first_grad, parts):
        width = tokens.shape[0]
        slot = attend[-2]
        rows = jnp.concatenate([inner_bias_grad.reshape(4, width), jnp.stack(vectors)])
        rows = jnp.pad(rows, ((0, 16 - rows.shape[0]), (0, 0)))
        docs, asked, *shards, sums = back_close(*attend, tokens, weights, rows, first_grad, parts)
        index = lax.axis_index(AXES)
        small = lax.dynamic_slice_in_dim(sums[4:13], index * (width // 32), width // 32, 1)
        inner_bias_shard = lax.dynamic_slice_in_dim(sums[:4].reshape(-1), index * (width // 8), width // 8, 0)
        return docs, asked, shards, [small[i] for i in range(9)], inner_bias_shard


class Far:
    def one(self, value):
        return lax.all_gather(value, AXES, axis=0, tiled=True)

    def weights(self, matrices, vectors, wide_vector, positives):
        return (
            [self.one(m) for m in matrices],
            jnp.stack([self.one(v) for v in vectors]),
            self.one(wide_vector),
            self.one(positives),
        )

    def forward(self, attend, shards, row_vectors, inner_bias):
        tokens = attend[1]
        weights = [self.one(m) for m in shards]
        outs = attend_forward(*attend)
        bias, gain, shift = row_vectors
        normal, inverse = normalize_rows(tokens.astype(f32) + dense(outs[3], weights[0]) + bias)
        low = (normal * gain + shift).astype(bf16)
        activated, slope = gelu_both(dense(low, weights[1]) + inner_bias.astype(f32))
        return outs, normal, inverse, (low, tokens), activated.astype(bf16), slope.astype(bf16), weights

    def rows(self, rows):
        return self.one(rows)

    def totals(self, totals):
        return self.one(totals[None])

    def row_grads(self, grads):
        return self.spread(grads)

    def spread(self, value):
        return lax.psum_scatter(value.astype(f32), AXES, scatter_dimension=0, tiled=True)

    def middle(self, grad, second, low, w_outer, w_inner, slope, part):
        hidden = (dense_back(grad, w_outer) * slope.astype(f32)).astype(bf16)
        return second + dense_back(hidden, w_inner), weight_grad(low, hidden), row_sum(hidden), self.spread(part)

    def back(self, attend, tokens, weights, vectors, inner_bias_grad, first_grad, parts):
        slot = attend[-2]
        grads = attend_backward(*attend)
        total = first_grad
        for grad, weight in zip(grads, weights):
            total = total + dense_back(grad, weight)
        parts = list(parts) + [weight_grad(tokens, grad) for grad in grads]
        vectors = list(vectors) + [row_sum(grad) for grad in grads]
        return (
            total[:slot],
            total[slot:],
            [self.spread(part) for part in parts],
            [self.spread(vector) for vector in vectors],
            self.spread(inner_bias_grad),
        )


def local(
    link,
    doc_tokens,
    query_tokens,
    doc_lengths,
    positives,
    query_weight,
    key_weight,
    value_weight,
    output_weight,
    query_bias,
    key_bias,
    value_bias,
    output_bias,
    attn_gain,
    attn_shift,
    inner_weight,
    inner_bias,
    outer_weight,
    outer_bias,
    final_gain,
    final_shift,
    proj_weight,
):
    slot, width = doc_tokens.shape[1:]
    count, question = query_tokens.shape[:2]
    tokens = jnp.concatenate([doc_tokens[0], query_tokens.reshape(count * question, width)])
    cosine, sine = rotary_tables(slot, question, count)

    matrices, vectors, b_inner, chosen = link.weights(
        [query_weight, key_weight, value_weight],
        [
            query_bias,
            key_bias,
            value_bias,
            output_bias,
            attn_gain,
            attn_shift,
            outer_bias,
            final_gain,
            final_shift,
        ],
        inner_bias,
        positives,
    )
    w_query, w_key, w_value = matrices
    b_output, g_attn, s_attn, b_outer, g_final, s_final = [vectors[i].astype(f32) for i in range(3, 9)]

    outs, first_normal, first_inverse, (normed_low, tokens_kept), activated, slope, matrices = link.forward(
        (doc_lengths, tokens, w_query, w_key, w_value, vectors[0:8], cosine, sine, slot, question),
        [output_weight, inner_weight, outer_weight, proj_weight],
        [b_output, g_attn, s_attn],
        b_inner,
    )
    query_rot, key_rot, value_low, mixed, mass = outs
    w_output, w_inner, w_outer, w_proj = matrices
    normed = first_normal * g_attn + s_attn
    outer_branch = dense(activated, w_outer) + b_outer
    second_normal, second_inverse = normalize_rows(normed + outer_branch)
    states_low = (second_normal * g_final + s_final).astype(bf16)
    projected = dense(states_low, w_proj)
    inverse_norm = lax.rsqrt(jnp.sum(projected * projected, axis=-1, keepdims=True) + unit_eps)
    encoded = (projected * inverse_norm).astype(bf16)

    doc_rows = encoded[:slot]
    all_rows = link.rows(encoded[slot:])
    key_mask = jnp.arange(slot)[None, :] < doc_lengths[0]
    vector_width = encoded.shape[1]
    block_rows = 32 * question
    row_blocks = all_rows.reshape(-1, block_rows, vector_width)

    def block_scores(rows_block):
        scores = jnp.einsum("qe,ke->qk", rows_block, doc_rows, preferred_element_type=f32)
        return jnp.where(key_mask, scores / sharpness_divisor, masked_value)

    def smooth_block(unused, rows_block):
        scores = block_scores(rows_block)
        peak = jnp.max(scores, axis=1, keepdims=True)
        return unused, sharpness_divisor * (
            peak[:, 0] + jnp.log(jnp.sum(jnp.exp(scores - peak), axis=1))
        )

    unused, smooth = lax.scan(smooth_block, jnp.zeros((), f32), row_blocks)
    totals = smooth.reshape(-1, question).sum(axis=1)
    doc_index = lax.axis_index(AXES)
    all_totals = link.totals(totals)
    peak = jnp.max(all_totals, axis=0)
    log_total = peak + jnp.log(jnp.sum(jnp.exp(all_totals - peak), axis=0))
    hit = jnp.arange(all_totals.shape[0])[:, None] == chosen[None, :]
    losses = log_total - jnp.sum(jnp.where(hit, all_totals, 0.0), axis=0)
    query_loss = lax.dynamic_slice_in_dim(losses, doc_index * count, count, 0)
    coefficient = loss_scale * (jnp.exp(totals - log_total) - (chosen == doc_index).astype(f32))
    token_coefficient = jnp.broadcast_to(coefficient[:, None], (coefficient.shape[0], question))
    token_coefficient = token_coefficient.reshape(row_blocks.shape[0], block_rows)

    def grad_block(doc_grad, inputs):
        rows_block, smooth_rows, coefficient_rows = inputs
        weight = jnp.exp(block_scores(rows_block) - (smooth_rows / sharpness_divisor)[:, None])
        score_grad = (weight * coefficient_rows[:, None]).astype(bf16)
        row_grad = jnp.einsum("qk,ke->qe", score_grad, doc_rows, preferred_element_type=f32)
        doc_grad = doc_grad + jnp.einsum("qk,qe->ke", score_grad, rows_block, preferred_element_type=f32)
        return doc_grad, row_grad

    doc_vector_grad, row_grads = lax.scan(
        grad_block, jnp.zeros(doc_rows.shape, f32), (row_blocks, smooth, token_coefficient)
    )
    query_vector_grad = link.row_grads(row_grads.reshape(-1, vector_width))
    vector_grad = jnp.concatenate([doc_vector_grad, query_vector_grad])

    radial = jnp.sum(vector_grad * projected, axis=-1, keepdims=True)
    proj_grad = (
        vector_grad * inverse_norm - projected * (inverse_norm * inverse_norm * inverse_norm) * radial
    ).astype(bf16)
    proj_weight_grad = weight_grad(states_low, proj_grad)
    states_grad = dense_back(proj_grad, w_proj)
    final_gain_grad = row_sum(states_grad * second_normal)
    final_shift_grad = row_sum(states_grad)
    second_grad = norm_back(states_grad * g_final, second_normal, second_inverse)
    outer_grad = second_grad.astype(bf16)
    outer_weight_grad = weight_grad(activated, outer_grad)
    outer_bias_grad = row_sum(outer_grad)
    normed_grad, inner_weight_grad, inner_bias_grad, outer_shard = link.middle(
        outer_grad, second_grad, normed_low, w_outer, w_inner, slope, outer_weight_grad
    )
    attn_gain_grad = row_sum(normed_grad * first_normal)
    attn_shift_grad = row_sum(normed_grad)
    first_grad = norm_back(normed_grad * g_attn, first_normal, first_inverse)
    attended_grad = first_grad.astype(bf16)
    output_weight_grad = weight_grad(mixed, attended_grad)
    output_bias_grad = row_sum(attended_grad)
    mixed_grad = dense_back(attended_grad, w_output).astype(bf16)
    attend = (
        doc_lengths, query_rot, key_rot, value_low, mixed, mixed_grad, mass, cosine, sine, slot, question,
    )
    docs_grad, asked_grad, shards, small, inner_bias_shard = link.back(
        attend,
        tokens_kept,
        (w_query, w_key, w_value),
        [outer_bias_grad, final_gain_grad, final_shift_grad, attn_gain_grad, attn_shift_grad, output_bias_grad],
        inner_bias_grad,
        first_grad,
        [inner_weight_grad, output_weight_grad, proj_weight_grad],
    )
    inner_shard, output_shard, proj_shard, query_shard, key_shard, value_shard = shards
    b_outer_shard, gain_shard, shift_shard, attn_gain_shard, attn_shift_shard, b_output_shard, *b_heads = small
    return (
        query_loss,
        states_low[None, :slot],
        states_low[slot:].reshape(count, question, width),
        docs_grad[None],
        asked_grad.reshape(count, question, width),
        query_shard,
        key_shard,
        value_shard,
        output_shard,
        *b_heads,
        b_output_shard,
        attn_gain_shard,
        attn_shift_shard,
        inner_shard,
        inner_bias_shard,
        outer_shard,
        b_outer_shard,
        gain_shard,
        shift_shard,
        proj_shard,
    )


def solution(mesh):
    row = P(AXES)
    flat = P(AXES, None)
    deep = P(AXES, None, None)
    in_specs = (deep, deep, row, row) + (flat,) * 4 + (row,) * 6 + (flat, row, flat, row, row, row, flat)
    out_specs = (row, deep, deep, deep, deep) + (flat,) * 4 + (row,) * 6 + (flat, row, flat, row, row, row, flat)
    link = Close() if (mesh.shape["fsdp"], mesh.shape["dp"]) == (2, 16) else Far()
    return jax.shard_map(
        functools.partial(local, link), mesh=mesh, in_specs=in_specs, out_specs=out_specs, check_vma=False
    )
```

```python
import functools
import math

import jax
import jax.numpy as jnp
import numpy as np
from jax import lax
from jax.experimental import pallas as pl
from jax.experimental.pallas import tpu as pltpu
from jax.sharding import PartitionSpec as P

HEADS = 16
HEAD = 64
AXES = ("fsdp", "dp")
MESH = pl.DeviceIdType.MESH
f32 = jnp.float32
bf16 = jnp.bfloat16
norm_eps = 1e-05
unit_eps = 1e-06
sharpness_divisor = 0.0625
loss_scale = 256.0
masked_value = -1e30
score_scale = 0.125 * math.log2(math.e)
vmem_bytes = 62 * 1024 * 1024
small_room = 6 * 1024 * 1024


def nt(a, b):
    return lax.dot_general(a, b, (((1,), (1,)), ((), ())), preferred_element_type=f32)


def nn(a, b):
    return lax.dot_general(a, b, (((1,), (0,)), ((), ())), preferred_element_type=f32)


def tn(a, b):
    return lax.dot_general(a, b, (((0,), (0,)), ((), ())), preferred_element_type=f32)


def lane_of(shape):
    return lax.broadcasted_iota(jnp.int32, shape, 1)


def row_of(shape):
    return lax.broadcasted_iota(jnp.int32, shape, 0)


def wide(table):
    return jnp.concatenate([table, table], axis=1)


def rope(values, cosine, signed_sine):
    width = values.shape[1]
    turned = jnp.where(
        lane_of(values.shape) % HEAD < HEAD // 2,
        pltpu.roll(values, width - HEAD // 2, 1),
        pltpu.roll(values, HEAD // 2, 1),
    )
    return values * cosine + turned * signed_sine


def rope_back(gradient, cosine, signed_sine):
    width = gradient.shape[1]
    scaled = gradient * signed_sine
    turned = jnp.where(
        lane_of(gradient.shape) % HEAD < HEAD // 2,
        pltpu.roll(scaled, width - HEAD // 2, 1),
        pltpu.roll(scaled, HEAD // 2, 1),
    )
    return gradient * cosine + turned


def heads_apart(values, heads):
    rows = values.shape[0]
    tall = jnp.concatenate([values] * heads, axis=0)
    keep = (row_of(tall.shape) // rows) == (lane_of(tall.shape) // HEAD)
    return jnp.where(keep, tall, jnp.zeros_like(tall))


def heads_joined(values, heads):
    rows = values.shape[0] // heads
    keep = (row_of(values.shape) // rows) == (lane_of(values.shape) // HEAD)
    values = jnp.where(keep, values, 0.0)
    total = values[0:rows]
    for h in range(1, heads):
        total = total + values[h * rows : (h + 1) * rows]
    return total


def question_probs(apart, key, question):
    rows = key.shape[0]
    scores = nt(apart, key) * 0.125
    same = (row_of(scores.shape) % rows) // question == lane_of(scores.shape) // question
    scores = jnp.where(same, scores, masked_value)
    weight = jnp.exp(scores - jnp.max(scores, axis=1, keepdims=True))
    return weight / jnp.sum(weight, axis=1, keepdims=True)


def attend_step(slot, question, length_ref, tokens_ref, wq_ref, wk_ref, wv_ref, bias_ref, cos_ref, sin_ref, q_ref, k_ref, v_ref, mixed_ref, mass_ref, go=lambda part: None):
    tokens = tokens_ref[...]
    cosine = wide(cos_ref[...])
    sine = wide(sin_ref[...])
    q_ref[...] = rope(nn(tokens, wq_ref[...]) + bias_ref[0:1, :].astype(f32), cosine, sine).astype(bf16)
    k_ref[...] = rope(nn(tokens, wk_ref[...]) + bias_ref[1:2, :].astype(f32), cosine, sine).astype(bf16)
    v_ref[...] = (nn(tokens, wv_ref[...]) + bias_ref[2:3, :].astype(f32)).astype(bf16)
    go(0)
    total = tokens.shape[0]
    length = length_ref[0]
    pair = (slot, 2 * HEAD)
    lane = lane_of(pair)
    mask = jnp.where(row_of(pair) < length, 0.0, masked_value).astype(bf16)
    for p in range(2):
        cols = slice(p * 2 * HEAD, (p + 1) * 2 * HEAD)
        query = q_ref[0:slot, cols]
        key = k_ref[0:slot, cols]
        value = v_ref[0:slot, cols]
        parts = []
        masses = []
        for h in range(2):
            mine = (lane // HEAD) == h
            spare = (1 - h) * HEAD
            query_h = jnp.where(mine, query, jnp.where(lane == spare, 1.0, 0.0).astype(bf16))
            key_h = jnp.where(lane == spare, mask, key)
            value_h = jnp.where(mine, value, jnp.ones_like(value))
            scores = nt(query_h, key_h)
            peak = jnp.max(scores, axis=1, keepdims=True)
            weight = jnp.exp2((scores - peak) * score_scale).astype(bf16)
            mixed = nn(weight, value_h)
            parts.append(mixed / pltpu.roll(mixed, HEAD, 1))
            masses.append(peak * score_scale + jnp.log2(mixed))
        mixed_ref[0:slot, cols] = jnp.where(lane < HEAD, parts[0], parts[1]).astype(bf16)
        turned = jnp.where(lane < HEAD, masses[1], masses[0]).T
        mass_ref[0, 2 * p : 2 * p + 1, 0:slot] = turned[HEAD : HEAD + 1, :]
        mass_ref[0, 2 * p + 1 : 2 * p + 2, 0:slot] = turned[0:1, :]
        if p == 0:
            go(1)
    rest = slice(slot, total)
    weight = question_probs(heads_apart(q_ref[rest, :], 4), k_ref[rest, :], question)
    mixed_ref[rest, :] = heads_joined(nn(weight.astype(bf16), v_ref[rest, :]), 4).astype(bf16)
    go(2)


def group_spec(rows):
    return pl.BlockSpec((rows, 4 * HEAD), lambda i: (0, i))


def whole_spec(shape):
    return pl.BlockSpec(shape, lambda i: (0,) * len(shape))


def mass_spec(total):
    return pl.BlockSpec((1, 8, total), lambda i: (i, 0, 0))


def attend_forward(length, tokens, wq, wk, wv, biases, cosine, sine, slot, question):
    total, width = tokens.shape
    groups = width // (4 * HEAD)
    return pl.pallas_call(
        functools.partial(attend_step, slot, question),
        grid=(groups,),
        in_specs=[
            pl.BlockSpec(memory_space=pltpu.SMEM),
            whole_spec((total, width)),
            group_spec(width),
            group_spec(width),
            group_spec(width),
            group_spec(8),
            whole_spec((total, 2 * HEAD)),
            whole_spec((total, 2 * HEAD)),
        ],
        out_specs=[group_spec(total)] * 4 + [mass_spec(total)],
        out_shape=[jax.ShapeDtypeStruct((total, width), bf16)] * 4
        + [jax.ShapeDtypeStruct((groups, 8, total), f32)],
        compiler_params=pltpu.CompilerParams(vmem_limit_bytes=vmem_bytes),
        name="attend_forward",
    )(length, tokens, wq, wk, wv, biases, cosine, sine)


class Place:
    def __init__(self):
        y = lax.axis_index("fsdp")
        d = lax.axis_index("dp")
        z, x, c = d // 4, (d // 2) % 2, d % 2
        self.y, self.z, self.x, self.c = y, z, x, c
        x1, y1 = (1 - c) * (1 - x) + c * x, c * (1 - y) + (1 - c) * y
        x2, y2 = c * (1 - x) + (1 - c) * x, (1 - c) * (1 - y) + c * y
        self.first = (y1, z * 4 + x1 * 2 + c)
        self.second = (y2, z * 4 + x2 * 2 + c)
        self.twin = (y, z * 4 + x * 2 + (1 - c))
        self.along = [(y, ((z + k) % 4) * 4 + x * 2 + c) for k in (1, 2, 3)]
        self.lines = [(y, x), (y1, x1), (y2, x2), (1 - y, 1 - x)]
        self.ahead = [(z + k) % 4 for k in (1, 2, 3)]
        self.other = 1 - c

    def greet(self):
        barrier = pltpu.get_barrier_semaphore()
        peers = [self.first, self.second, self.twin] + self.along
        for peer in peers:
            pl.semaphore_signal(barrier, inc=1, device_id=peer, device_id_type=MESH)
        pl.semaphore_wait(barrier, len(peers))


class Sender:
    def __init__(self):
        self.sent = []

    def go(self, src, dst, send_sem, recv_sem, device):
        copy = pltpu.make_async_remote_copy(
            src_ref=src,
            dst_ref=dst,
            send_sem=send_sem,
            recv_sem=recv_sem,
            device_id=device,
            device_id_type=MESH,
        )
        copy.start()
        self.sent.append(copy)

    def drain(self):
        for copy in self.sent:
            copy.wait_send()


def arrived(ref, sem):
    pltpu.make_async_copy(ref, ref, sem).wait()


class LateSender:
    def __init__(self):
        self.sent = []

    def copy(self, parts):
        src, dst, send_sem, recv_sem, device = parts()
        return pltpu.make_async_remote_copy(
            src_ref=src, dst_ref=dst, send_sem=send_sem, recv_sem=recv_sem, device_id=device, device_id_type=MESH
        )

    def go(self, parts):
        self.copy(parts).start()
        self.sent.append(parts)

    def drain(self):
        for parts in self.sent:
            self.copy(parts).wait_send()


class Gather:
    def __init__(self, place, shards, wholes, send_sem, recv_sem, own_sem):
        self.at, self.shards = place, shards
        self.wholes = [w if isinstance(w, tuple) else (w, ()) for w in wholes]
        self.send_sem, self.recv_sem, self.own_sem = send_sem, recv_sem, own_sem
        self.out = LateSender()

    def block(self, t, *where):
        whole, tail = self.wholes[t]
        return whole.at[where + tail]

    def line(self, t, k, core):
        y, x = self.at.lines[k]
        return self.block(t, y, slice(None), x, core)

    def mine(self, t):
        at = self.at
        return self.block(t, at.y, at.z, at.x, at.c)

    def own(self, t):
        return pltpu.make_async_copy(self.shards[t], self.mine(t), self.own_sem.at[t])

    def begin(self, t):
        at = self.at
        targets = [(k, 0, peer) for k, peer in enumerate(at.along)]
        targets += [(3, 1, at.first), (4, 2, at.second), (5, 4, at.twin)]
        for send, recv, peer in targets:
            self.out.go(
                lambda send=send, recv=recv, peer=peer: (
                    self.shards[t], self.mine(t), self.send_sem.at[t, send], self.recv_sem.at[t, recv], peer,
                )
            )
        self.own(t).start()

    def pass_line(self, t, k, targets):
        for send, recv, peer in targets:
            self.out.go(
                lambda send=send, recv=recv, peer=peer: (
                    self.line(t, k, self.at.c),
                    self.line(t, k, self.at.c),
                    self.send_sem.at[t, send],
                    self.recv_sem.at[t, recv],
                    peer,
                )
            )

    def own_line(self, t):
        at = self.at
        arrived(self.block(t, at.y, slice(0, 3), at.x, at.c), self.recv_sem.at[t, 0])
        for j, (recv, peer) in enumerate([(1, at.first), (2, at.second), (4, at.twin)]):
            for k in range(3):
                self.out.go(
                    lambda send=10 + 3 * j + k, recv=recv, peer=peer, z=at.ahead[k]: (
                        self.block(t, at.y, z, at.x, at.c),
                        self.block(t, at.y, z, at.x, at.c),
                        self.send_sem.at[t, send],
                        self.recv_sem.at[t, recv],
                        peer,
                    )
                )

    def first_line(self, t):
        at = self.at
        arrived(self.line(t, 1, at.c), self.recv_sem.at[t, 1])
        self.pass_line(t, 1, [(6, 3, at.second), (7, 5, at.twin)])

    def second_line(self, t):
        arrived(self.line(t, 2, self.at.c), self.recv_sem.at[t, 2])
        self.pass_line(t, 2, [(8, 6, self.at.twin)])

    def far_line(self, t):
        arrived(self.line(t, 3, self.at.c), self.recv_sem.at[t, 3])
        self.pass_line(t, 3, [(9, 7, self.at.twin)])

    def twin_lines(self, t):
        self.own(t).wait()
        for k in range(4):
            arrived(self.line(t, k, self.at.other), self.recv_sem.at[t, 4 + k])

    def perform(self, names):
        moves = {
            "B": self.begin, "O": self.own_line, "F": self.first_line, "S": self.second_line,
            "R": self.far_line, "T": self.twin_lines,
        }
        for some in names:
            for name in some.split():
                moves[name[0]](int(name[1:]))


def gather_sems(count):
    return [
        pltpu.SemaphoreType.DMA((count, 19)),
        pltpu.SemaphoreType.DMA((count, 8)),
        pltpu.SemaphoreType.DMA((count,)),
    ]


def spread_shape(shard):
    return jax.ShapeDtypeStruct((2, 4, 2, 2) + shard.shape, shard.dtype)


def joined_shards(whole):
    return whole.reshape((32 * whole.shape[4],) + whole.shape[5:])


def gather_body(count, *refs):
    shards, wholes = refs[:count], refs[count : 2 * count]
    place = Place()
    place.greet()
    run = Gather(place, shards, wholes, *refs[2 * count :])
    for t in range(count):
        run.begin(t)
    for s in range(count + 2):
        if s < count:
            run.own_line(s)
        if 0 <= s - 1 < count:
            run.first_line(s - 1)
            run.second_line(s - 1)
        if 0 <= s - 2 < count:
            run.far_line(s - 2)
    for t in range(count):
        run.twin_lines(t)
    run.out.drain()


def gather(shards, collective_id, room=vmem_bytes):
    count = len(shards)
    wholes = pl.pallas_call(
        functools.partial(gather_body, count),
        in_specs=[pl.BlockSpec(memory_space=pltpu.VMEM)] * count,
        out_specs=[pl.BlockSpec(memory_space=pl.ANY)] * count,
        out_shape=[spread_shape(a) for a in shards],
        scratch_shapes=gather_sems(count),
        compiler_params=pltpu.CompilerParams(
            collective_id=collective_id, has_side_effects=True, vmem_limit_bytes=room
        ),
        name="gather",
    )(*shards)
    return [joined_shards(w) for w in wholes]


def exchange_body(block_ref, whole, send_sem, recv_sem, own_sem):
    place = Place()
    y, z, x, c = place.y, place.z, place.x, place.c
    near = []
    for flip in range(1, 8):
        there = ((1 - y) if flip & 4 else y, (1 - x) if flip & 2 else x, (1 - c) if flip & 1 else c)
        near.append((there, (there[0], z * 4 + there[1] * 2 + there[2])))
    peers = [device for _, device in near] + place.along
    barrier = pltpu.get_barrier_semaphore()
    for peer in peers:
        pl.semaphore_signal(barrier, inc=1, device_id=peer, device_id_type=MESH)
    pl.semaphore_wait(barrier, len(peers))
    out = Sender()
    mine = whole.at[y, z, x, c]
    for i, (_, device) in enumerate(near):
        out.go(block_ref, mine, send_sem.at[i], recv_sem.at[i], device)
    own = pltpu.make_async_copy(block_ref, mine, own_sem.at[0])
    own.start()
    own.wait()
    for i, (there, _) in enumerate(near):
        arrived(whole.at[there[0], z, there[1], there[2]], recv_sem.at[i])
    for k, device in enumerate(place.along):
        out.go(whole.at[:, z], whole.at[:, z], send_sem.at[7 + k], recv_sem.at[7 + k], device)
    for k in range(3):
        arrived(whole.at[:, place.ahead[2 - k]], recv_sem.at[7 + k])
    out.drain()


def exchange(block, collective_id):
    return pl.pallas_call(
        exchange_body,
        in_specs=[pl.BlockSpec(memory_space=pltpu.VMEM)],
        out_specs=pl.BlockSpec(memory_space=pltpu.VMEM),
        out_shape=spread_shape(block),
        scratch_shapes=[
            pltpu.SemaphoreType.DMA((10,)),
            pltpu.SemaphoreType.DMA((10,)),
            pltpu.SemaphoreType.DMA((1,)),
        ],
        compiler_params=pltpu.CompilerParams(collective_id=collective_id, has_side_effects=True, vmem_limit_bytes=small_room),
        name="exchange",
    )(block)


attend_plan = {
    (0, 2): ["O0"],
    (1, 1): ["O1"],
    (1, 2): ["F0 S0"],
    (2, 0): ["O2"],
    (2, 1): ["F1 S1"],
    (2, 2): ["R0 O3"],
    (3, 0): ["F2 S2"],
    (3, 1): ["R1 O4"],
    (3, 2): ["F3 S3 R2"],
    (3, 3): ["F4 S4 R3 R4"],
}


def pump(run, step, plan, steps):
    def go(part):
        for g in range(steps):
            if (g, part) in plan:

                @pl.when(step == g)
                def _():
                    run.perform(plan[g, part])

    return go


def attend_gather_body(slot, question, *refs):
    ins, shards = refs[:8], refs[8:10]
    outs, turned_ref, wholes = refs[10:15], refs[15], refs[16:18]
    step = pl.program_id(0)
    place = Place()
    width = shards[1].shape[1] // 4
    cuts = [slice(j * width, (j + 1) * width) for j in range(4)]
    units = [shards[0]] + [shards[1].at[:, cut] for cut in cuts]
    places = [wholes[0]] + [(wholes[1], (slice(None), cut)) for cut in cuts]
    run = Gather(place, units, places, *refs[18:])

    @pl.when(step == 0)
    def _():
        place.greet()
        for t in range(len(units)):
            run.begin(t)

    columns = pl.ds(pl.multiple_of(step * 4 * HEAD, 4 * HEAD), 4 * HEAD)
    turned_ref[:, 0:slot] = ins[1][0:slot, columns].T
    turned_ref[:, slot:] = ins[1][slot:, columns].T
    go = pump(run, step, attend_plan, 4)
    attend_step(slot, question, *ins, *outs, go=go)

    @pl.when(step == 3)
    def _():
        run.perform(attend_plan[3, 3])
        for t in range(len(units)):
            run.twin_lines(t)
        run.out.drain()


def attend_gather(length, tokens, wq, wk, wv, biases, cosine, sine, slot, question, shards):
    total, width = tokens.shape
    groups = width // (4 * HEAD)
    once = pl.Buffered(1)

    def kept(shape):
        return pl.BlockSpec(shape, lambda i: (0,) * len(shape), pipeline_mode=once)

    *outs, turned, first, second = pl.pallas_call(
        functools.partial(attend_gather_body, slot, question),
        grid=(groups,),
        in_specs=[
            pl.BlockSpec(memory_space=pltpu.SMEM),
            kept((total, width)),
            group_spec(width),
            group_spec(width),
            group_spec(width),
            group_spec(8),
            kept((total, 2 * HEAD)),
            kept((total, 2 * HEAD)),
        ]
        + [kept(a.shape) for a in shards],
        out_specs=[group_spec(total)] * 4
        + [mass_spec(total), pl.BlockSpec((4 * HEAD, total), lambda i: (i, 0))]
        + [pl.BlockSpec(memory_space=pl.ANY)] * 2,
        out_shape=[jax.ShapeDtypeStruct((total, width), bf16)] * 4
        + [jax.ShapeDtypeStruct((groups, 8, total), f32), jax.ShapeDtypeStruct((width, total), bf16)]
        + [spread_shape(a) for a in shards],
        scratch_shapes=gather_sems(5),
        compiler_params=pltpu.CompilerParams(collective_id=5, has_side_effects=True, vmem_limit_bytes=vmem_bytes),
        name="attend_forward",
    )(length, tokens, wq, wk, wv, biases, cosine, sine, *shards)
    return outs, turned, [joined_shards(first), joined_shards(second)]


inner_plan = {
    (0, 3): ["O0"],
    (2, 0): ["O1 F0 S0"],
    (4, 0): ["F1 S1 R0"],
    (5, 0): ["O2"],
    (6, 0): ["R1"],
    (7, 0): ["O3 F2 S2 O4"],
    (8, 0): ["R2"],
    (8, 1): ["F3 S3 F4 S4", "R3 R4"],
}


def inner_body(slot, refs):
    (tokens_ref, mixed_ref, wo_ref, wi_ref, vec_ref, bias_ref, outer_ref, proj_ref) = refs[:8]
    (normal_ref, inverse_ref, low_ref, act_ref, slope_ref, turned_ref, outer_whole, proj_whole) = refs[8:16]
    step = pl.program_id(0)
    place = Place()
    rows = outer_ref.shape[0] // 4
    cuts = [slice(j * rows, (j + 1) * rows) for j in range(4)]
    units = [outer_ref.at[cut] for cut in cuts] + [proj_ref]
    places = [(outer_whole, (cut,)) for cut in cuts] + [proj_whole]
    run = Gather(place, units, places, *refs[16:])
    total = tokens_ref.shape[0]

    @pl.when(step == 0)
    def _():
        place.greet()
        for t in range(len(units)):
            run.begin(t)
        part = total // 4
        for j in range(4):
            these = slice(j * part, (j + 1) * part)
            attended = nn(mixed_ref[these, :], wo_ref[...]) + vec_ref[0:1, :]
            normal, inverse = normalize_rows(tokens_ref[these, :].astype(f32) + attended)
            normal_ref[these, :] = normal
            inverse_ref[these, :] = jnp.broadcast_to(inverse, (part, inverse_ref.shape[1]))
            low_ref[these, :] = (normal * vec_ref[1:2, :] + vec_ref[2:3, :]).astype(bf16)
            if (0, j) in inner_plan:
                run.perform(inner_plan[0, j])

    @pl.when(step > 0)
    def _():
        part = total // 4

        def some(j, carry):
            these = pl.ds(pl.multiple_of(j * part, 16), part)
            hidden = nn(low_ref[these, :], wi_ref[...]) + bias_ref[...].astype(f32)
            activated, slope = gelu_both(hidden)
            act_ref[these, :] = activated.astype(bf16)
            slope_ref[these, :] = slope.astype(bf16)
            return carry

        lax.fori_loop(0, 4, some, 0)
        slab = turned_ref.shape[0]
        columns = pl.ds(pl.multiple_of((step - 1) * slab, slab), slab)
        turned_ref[:, 0:slot] = low_ref[0:slot, columns].T
        turned_ref[:, slot:] = low_ref[slot:, columns].T

    for g in range(1, 9):
        if (g, 0) in inner_plan:

            @pl.when(step == g)
            def _():
                run.perform(inner_plan[g, 0])

    @pl.when(step == 8)
    def _():
        run.perform(inner_plan[8, 1])
        for t in range(len(units)):
            run.twin_lines(t)
        run.out.drain()


def inner_forward(tokens, mixed, wo, wi, vectors, bias, slot, shards):
    total, width = tokens.shape
    hidden = wi.shape[1]
    chunk = hidden // 8
    once = pl.Buffered(1)

    def kept(shape):
        return pl.BlockSpec(shape, lambda i: (0,) * len(shape), pipeline_mode=once)

    def chunked(rows):
        return pl.BlockSpec((rows, chunk), lambda i: (0, jnp.maximum(i - 1, 0)))

    *outs, outer, proj = pl.pallas_call(
        lambda *refs: inner_body(slot, refs),
        grid=(9,),
        in_specs=[kept((total, width)), kept((total, width)), kept((width, width)), chunked(width), kept(vectors.shape)]
        + [chunked(1)]
        + [kept(a.shape) for a in shards],
        out_specs=[kept((total, width)), kept((total, 128)), kept((total, width)), chunked(total), chunked(total)]
        + [pl.BlockSpec((width // 8, total), lambda i: (jnp.maximum(i - 1, 0), 0))]
        + [pl.BlockSpec(memory_space=pl.ANY)] * 2,
        out_shape=[
            jax.ShapeDtypeStruct((total, width), f32),
            jax.ShapeDtypeStruct((total, 128), f32),
            jax.ShapeDtypeStruct((total, width), bf16),
            jax.ShapeDtypeStruct((total, hidden), bf16),
            jax.ShapeDtypeStruct((total, hidden), bf16),
            jax.ShapeDtypeStruct((width, total), bf16),
        ]
        + [spread_shape(a) for a in shards],
        scratch_shapes=gather_sems(5),
        compiler_params=pltpu.CompilerParams(collective_id=6, has_side_effects=True, vmem_limit_bytes=vmem_bytes),
        name="inner_forward",
    )(tokens, mixed, wo, wi, vectors, bias, *shards)
    return outs, [joined_shards(outer), joined_shards(proj)]


class Scatter:
    twin_slot = (0, 2, 1, 3)

    def __init__(self, place, parts, outs, buffers, send_sem, recv_sem, own_sem):
        self.at, self.parts, self.outs, self.buffers = place, parts, outs, buffers
        self.send_sem, self.recv_sem, self.own_sem = send_sem, recv_sem, own_sem
        self.out = Sender()

    def own(self, t, k):
        y, x = self.at.lines[k]
        return pltpu.make_async_copy(
            self.parts[t].at[y, :, x, self.at.c], self.buffers[t][0].at[k], self.own_sem.at[t, k]
        )

    def begin(self, t):
        at = self.at
        for k in (3, 2, 1, 0):
            y, x = at.lines[k]
            slot = self.twin_slot[k]
            self.out.go(
                self.parts[t].at[y, :, x, 1 - at.c],
                self.buffers[t][1].at[slot],
                self.send_sem.at[t, k],
                self.recv_sem.at[t, slot],
                at.twin,
            )
            self.own(t, k).start()

    def join_twin(self, t, k):
        total, twin = self.buffers[t][:2]
        self.own(t, k).wait()
        arrived(twin.at[k], self.recv_sem.at[t, k])
        total[k] = total[k] + twin[k]

    def to_second(self, t):
        total, second = self.buffers[t][0], self.buffers[t][2]
        self.join_twin(t, 3)
        self.out.go(total.at[3], second.at[1], self.send_sem.at[t, 4], self.recv_sem.at[t, 5], self.at.second)
        self.join_twin(t, 2)
        self.out.go(total.at[2], second.at[0], self.send_sem.at[t, 5], self.recv_sem.at[t, 4], self.at.second)
        self.join_twin(t, 1)
        self.join_twin(t, 0)

    def to_first(self, t):
        total, second, first = self.buffers[t][0], self.buffers[t][2], self.buffers[t][3]
        arrived(second.at[1], self.recv_sem.at[t, 5])
        total[1] = total[1] + second[1]
        self.out.go(total.at[1], first, self.send_sem.at[t, 6], self.recv_sem.at[t, 6], self.at.first)
        arrived(second.at[0], self.recv_sem.at[t, 4])
        total[0] = total[0] + second[0]

    def to_line(self, t):
        total, first, last = self.buffers[t][0], self.buffers[t][3], self.buffers[t][4]
        arrived(first, self.recv_sem.at[t, 6])
        total[0] = total[0] + first[...]
        for k, peer in enumerate(self.at.along):
            self.out.go(
                total.at[0, (self.at.z + k + 1) % 4],
                last.at[k],
                self.send_sem.at[t, 7 + k],
                self.recv_sem.at[t, 7 + k],
                peer,
            )

    def finish(self, t):
        total, last = self.buffers[t][0], self.buffers[t][4]
        for k in range(3):
            arrived(last.at[k], self.recv_sem.at[t, 7 + k])
        self.outs[t][...] = (total[0, self.at.z].astype(f32) + last[0].astype(f32)) + (
            last[1].astype(f32) + last[2].astype(f32)
        )


def scatter_buffers(shape, dtype):
    return [
        pltpu.VMEM((4, 4) + shape, dtype),
        pltpu.VMEM((4, 4) + shape, dtype),
        pltpu.VMEM((2, 4) + shape, dtype),
        pltpu.VMEM((4,) + shape, dtype),
        pltpu.VMEM((3,) + shape, dtype),
    ]


def scatter_body(count, *refs):
    parts, outs = refs[:count], refs[count : 2 * count]
    flat = refs[2 * count : 7 * count]
    buffers = [flat[5 * t : 5 * t + 5] for t in range(count)]
    place = Place()
    place.greet()
    run = Scatter(place, parts, outs, buffers, *refs[7 * count :])
    for t in range(count):
        run.begin(t)
    for s in range(count + 3):
        if s < count:
            run.to_second(s)
        if 0 <= s - 1 < count:
            run.to_first(s - 1)
        if 0 <= s - 2 < count:
            run.to_line(s - 2)
        if 0 <= s - 3 < count:
            run.finish(s - 3)
    run.out.drain()


def scatter(parts, collective_id):
    count = len(parts)
    shapes = [(p.shape[0] // 32, p.shape[1]) for p in parts]
    scratch = []
    for p, shape in zip(parts, shapes):
        scratch += scatter_buffers(shape, p.dtype)
    return pl.pallas_call(
        functools.partial(scatter_body, count),
        in_specs=[pl.BlockSpec(memory_space=pl.ANY)] * count,
        out_specs=[pl.BlockSpec(memory_space=pltpu.VMEM)] * count,
        out_shape=[jax.ShapeDtypeStruct(shape, f32) for shape in shapes],
        scratch_shapes=scratch
        + [
            pltpu.SemaphoreType.DMA((count, 10)),
            pltpu.SemaphoreType.DMA((count, 10)),
            pltpu.SemaphoreType.DMA((count, 4)),
        ],
        compiler_params=pltpu.CompilerParams(
            collective_id=collective_id, has_side_effects=True, vmem_limit_bytes=small_room
        ),
        name="scatter",
    )(*[p.reshape((2, 4, 2, 2) + shape) for p, shape in zip(parts, shapes)])


def add_blocks(out, left, right):
    def one(z, carry):
        out[z] = left[z] + right[z]
        return carry

    lax.fori_loop(0, out.shape[0], one, 0)


class Unit:
    twin_slot = (0, 2, 1, 3)

    def __init__(self, place, out, mine, twins, buffers, send_sem, recv_sem, own_sem=None):
        self.at, self.out, self.mine, self.twins = place, out, mine, twins
        self.total, self.twin, self.second, self.first, self.last = buffers
        self.send_sem, self.recv_sem, self.own_sem = send_sem, recv_sem, own_sem
        self.sender = LateSender()

    def to_twin(self, k):
        slot = self.twin_slot[k]
        return lambda: (self.twins(k), self.twin.at[slot], self.send_sem.at[k], self.recv_sem.at[slot], self.at.twin)

    def begin(self):
        for k in (3, 2, 1, 0):
            self.sender.copy(self.to_twin(k)).start()
            if self.own_sem is not None:
                self.own(k).start()

    def own(self, k):
        return pltpu.make_async_copy(self.mine(k), self.total.at[k], self.own_sem.at[k])

    def join_twin(self, k):
        if self.own_sem is not None:
            self.own(k).wait()
        arrived(self.twin.at[k], self.recv_sem.at[k])
        base = self.total.at[k] if self.own_sem is not None else self.mine(k)
        add_blocks(self.total.at[k], base, self.twin.at[k])

    def to_second(self):
        self.join_twin(3)
        self.sender.go(lambda: (self.total.at[3], self.second.at[1], self.send_sem.at[4], self.recv_sem.at[5], self.at.second))
        self.join_twin(2)
        self.sender.go(lambda: (self.total.at[2], self.second.at[0], self.send_sem.at[5], self.recv_sem.at[4], self.at.second))
        self.join_twin(1)
        self.join_twin(0)

    def to_first(self):
        arrived(self.second.at[1], self.recv_sem.at[5])
        add_blocks(self.total.at[1], self.total.at[1], self.second.at[1])
        self.sender.go(lambda: (self.total.at[1], self.first, self.send_sem.at[6], self.recv_sem.at[6], self.at.first))
        arrived(self.second.at[0], self.recv_sem.at[4])
        add_blocks(self.total.at[0], self.total.at[0], self.second.at[0])

    def to_line(self):
        arrived(self.first, self.recv_sem.at[6])
        add_blocks(self.total.at[0], self.total.at[0], self.first)
        for k, peer in enumerate(self.at.along):
            self.sender.go(lambda k=k, peer=peer: (self.total.at[0, self.at.ahead[k]], self.last.at[k], self.send_sem.at[7 + k], self.recv_sem.at[7 + k], peer))

    def finish(self):
        for k in range(3):
            arrived(self.last.at[k], self.recv_sem.at[7 + k])
        self.out(
            (self.total[0, self.at.z].astype(f32) + self.last[0].astype(f32))
            + (self.last[1].astype(f32) + self.last[2].astype(f32))
        )

    def drain_twin(self):
        for k in range(4):
            self.sender.copy(self.to_twin(k)).wait_send()

    def drain(self):
        self.sender.drain()


class VectorSum:
    def __init__(self, place, value, sums, heard, out, send_sem, recv_sem):
        self.at, self.value, self.sums, self.heard, self.out = place, value, sums, heard, out
        self.send_sem, self.recv_sem = send_sem, recv_sem
        self.sender = LateSender()

    def tell(self, source, slot, peer):
        self.sender.go(lambda: (source(), self.heard.at[slot], self.send_sem.at[slot], self.recv_sem.at[slot], peer))

    def hear(self, slot):
        arrived(self.heard.at[slot], self.recv_sem.at[slot])
        return self.heard[slot]

    def twin(self):
        self.tell(lambda: self.value, 0, self.at.twin)

    def second(self):
        self.sums[0] = self.value[...] + self.hear(0)
        self.tell(lambda: self.sums.at[0], 1, self.at.second)

    def first(self):
        self.sums[1] = self.sums[0] + self.hear(1)
        self.tell(lambda: self.sums.at[1], 2, self.at.first)

    def line(self):
        self.sums[2] = self.sums[1] + self.hear(2)
        for k, peer in enumerate(self.at.along):
            self.tell(lambda: self.sums.at[2], 3 + k, peer)

    def finish(self):
        self.out[...] = (self.sums[2] + self.hear(3)) + (self.hear(4) + self.hear(5))


def back_pair(slot, p, length, q_ref, k_ref, v_ref, mixed_ref, grad_ref, mass_ref, cos_ref, sin_ref, dq_ref, dk_ref, dv_ref):
    pair = (slot, 2 * HEAD)
    lane = lane_of(pair)
    mask = jnp.where(row_of(pair) < length, 0.0, masked_value).astype(bf16)
    cosine = cos_ref[0:slot, :]
    sine = sin_ref[0:slot, :]
    cols = slice(p * 2 * HEAD, (p + 1) * 2 * HEAD)
    query = q_ref[0:slot, cols]
    key = k_ref[0:slot, cols]
    value = v_ref[0:slot, cols]
    grad = grad_ref[0:slot, cols]
    key_turned = key.T
    product = (grad.astype(f32) * mixed_ref[0:slot, cols].astype(f32)).T
    dq = []
    dk = []
    dv = []
    for h in range(2):
        mine = (lane // HEAD) == h
        spare = (1 - h) * HEAD
        query_h = jnp.where(mine, query, jnp.where(lane == spare, 1.0, 0.0).astype(bf16))
        key_h = jnp.where(lane == spare, mask, key)
        value_h = jnp.where(mine, value, jnp.zeros_like(value))
        row_dot = jnp.sum(product[h * HEAD : (h + 1) * HEAD], axis=0, keepdims=True)
        mass = mass_ref[0, 2 * p + h : 2 * p + h + 1, 0:slot]
        probs = jnp.exp2(nt(key_h, query_h) * score_scale - mass)
        slope = (probs * (nt(value_h, grad) - row_dot)).astype(bf16)
        dv.append(nn(probs.astype(bf16), grad))
        dk.append(nn(slope, query))
        dq.append(nn(key_turned[h * HEAD : (h + 1) * HEAD], slope))
    dq_all = jnp.concatenate(dq, axis=0).T * 0.125
    dk_all = jnp.where(lane < HEAD, dk[0], dk[1]) * 0.125
    dq_ref[0:slot, cols] = rope_back(dq_all, cosine, sine).astype(bf16)
    dk_ref[0:slot, cols] = rope_back(dk_all, cosine, sine).astype(bf16)
    dv_ref[0:slot, cols] = jnp.where(lane < HEAD, dv[0], dv[1]).astype(bf16)


def back_questions(slot, question, q_ref, k_ref, v_ref, grad_ref, cos_ref, sin_ref, dq_ref, dk_ref, dv_ref):
    rest = slice(slot, q_ref.shape[0])
    cosine = wide(cos_ref[rest, :])
    sine = wide(sin_ref[rest, :])
    apart = heads_apart(q_ref[rest, :], 4)
    grad_apart = heads_apart(grad_ref[rest, :], 4)
    key = k_ref[rest, :]
    probs = question_probs(apart, key, question)
    grad_prob = nt(grad_apart, v_ref[rest, :])
    row_dot = jnp.sum(probs * grad_prob, axis=1, keepdims=True)
    slope = (probs * (grad_prob - row_dot) * 0.125).astype(bf16)
    dq_ref[rest, :] = rope_back(heads_joined(nn(slope, key), 4), cosine, sine).astype(bf16)
    dk_ref[rest, :] = rope_back(tn(slope, apart), cosine, sine).astype(bf16)
    dv_ref[rest, :] = tn(probs.astype(bf16), grad_apart).astype(bf16)


def attend_back_step(slot, question, length_ref, q_ref, k_ref, v_ref, mixed_ref, grad_ref, mass_ref, cos_ref, sin_ref, dq_ref, dk_ref, dv_ref):
    ins = (q_ref, k_ref, v_ref, mixed_ref, grad_ref, mass_ref, cos_ref, sin_ref)
    for p in range(2):
        back_pair(slot, p, length_ref[0], *ins, dq_ref, dk_ref, dv_ref)
    back_questions(slot, question, q_ref, k_ref, v_ref, grad_ref, cos_ref, sin_ref, dq_ref, dk_ref, dv_ref)


def attend_backward(length, q, k, v, mixed, grad, mass, cosine, sine, slot, question):
    total, width = q.shape
    groups = width // (4 * HEAD)
    return pl.pallas_call(
        functools.partial(attend_back_step, slot, question),
        grid=(groups,),
        in_specs=[pl.BlockSpec(memory_space=pltpu.SMEM)]
        + [group_spec(total)] * 5
        + [mass_spec(total), whole_spec((total, 2 * HEAD)), whole_spec((total, 2 * HEAD))],
        out_specs=[group_spec(total)] * 3,
        out_shape=[jax.ShapeDtypeStruct((total, width), bf16)] * 3,
        compiler_params=pltpu.CompilerParams(vmem_limit_bytes=vmem_bytes),
        name="attend_backward",
    )(length, q, k, v, mixed, grad, mass, cosine, sine)


middle_plan = {
    (1, 0): ["S0"],
    (2, 0): ["S1"],
    (2, 1): ["F0"],
    (3, 0): ["S2 L0"],
    (3, 1): ["F1"],
    (4, 0): ["S3 L1"],
    (4, 1): ["F2"],
    (5, 0): ["E0 L2"],
    (5, 1): ["F3"],
    (6, 0): ["E1"],
    (6, 1): ["L3"],
    (7, 0): ["E2"],
    (7, 1): ["E3"],
}
scatter_moves = {"B": "begin", "S": "to_second", "F": "to_first", "L": "to_line", "E": "finish"}


def middle_body(refs):
    (grad_ref, second_ref, turned_ref, wo_ref, wi_ref, slope_ref, part_ref) = refs[:7]
    (normed_ref, inner_ref, bias_ref, out_ref) = refs[7:11]
    hidden_ref, seed_ref = refs[11:13]
    flat = refs[13:33]
    send_sem, recv_sem, own_sem, seed_sem = refs[33:]
    step = pl.program_id(0)
    place = Place()
    rows = out_ref.shape[0] // 4

    def lines(core, part):
        return lambda k: part_ref.at[place.lines[k][0], :, place.lines[k][1], core, part]

    def put(part):
        def write(block):
            out_ref[part, :] = block

        return write

    units = []
    for u in range(4):
        part = slice(u * rows, (u + 1) * rows)
        units.append(
            Unit(
                place,
                put(part),
                lines(place.c, part),
                lines(place.other, part),
                flat[5 * u : 5 * u + 5],
                send_sem.at[u],
                recv_sem.at[u],
                own_sem.at[u],
            )
        )

    def go(part):
        for g in range(8):
            if (g, part) in middle_plan:

                @pl.when(step == g)
                def _():
                    for some in middle_plan[g, part]:
                        for name in some.split():
                            getattr(units[int(name[1:])], scatter_moves[name[0]])()

    @pl.when(step == 0)
    def _():
        place.greet()
        for unit in units:
            unit.begin()
        pltpu.make_async_copy(second_ref, seed_ref, seed_sem.at[0]).start()
        normed_ref[...] = jnp.zeros_like(normed_ref)

    half = grad_ref.shape[0] // 2

    def some_rows(j, sums):
        these = pl.ds(pl.multiple_of(j * half, 16), half)
        hidden = (nt(grad_ref[these, :], wo_ref[...]) * slope_ref[these, :].astype(f32)).astype(bf16)
        hidden_ref[these, :] = hidden
        normed_ref[these, :] += nt(hidden, wi_ref[...])
        return sums + jnp.sum(hidden.astype(f32), axis=0, keepdims=True)

    sums = lax.fori_loop(0, 2, some_rows, jnp.zeros((1, hidden_ref.shape[1]), f32))
    bias_ref[...] = jnp.broadcast_to(sums, bias_ref.shape)
    go(0)
    quarter = turned_ref.shape[0] // 2

    def some_columns(j, carry):
        these = pl.ds(pl.multiple_of(j * quarter, 16), quarter)
        inner_ref[these, :] = nn(turned_ref[these, :], hidden_ref[...]).astype(bf16)
        return carry

    lax.fori_loop(0, 2, some_columns, 0)
    go(1)

    @pl.when(step == 7)
    def _():
        pltpu.make_async_copy(second_ref, seed_ref, seed_sem.at[0]).wait()
        normed_ref[...] += seed_ref[...]
        for unit in units:
            unit.drain_twin()
            unit.drain()


def middle_back(grad, second, turned, wo, wi, slope, part):
    total, width = grad.shape
    hidden = wi.shape[1]
    chunk = hidden // 8
    shard = part.shape[0] // 32
    once = pl.Buffered(1)

    def kept(shape):
        return pl.BlockSpec(shape, lambda i: (0,) * len(shape), pipeline_mode=once)

    def chunked(rows):
        return pl.BlockSpec((rows, chunk), lambda i: (0, i))

    scratch = [pltpu.VMEM((total, chunk), bf16), pltpu.VMEM((total, width), f32)]
    for u in range(4):
        scratch += unit_buffers((shard // 4, width), bf16)
    return pl.pallas_call(
        lambda *refs: middle_body(refs),
        grid=(8,),
        in_specs=[
            kept((total, width)),
            pl.BlockSpec(memory_space=pl.ANY),
            kept((width, total)),
            pl.BlockSpec((chunk, width), lambda i: (i, 0)),
            chunked(width),
            chunked(total),
            pl.BlockSpec(memory_space=pl.ANY),
        ],
        out_specs=[kept((total, width)), chunked(width), chunked(8), kept((shard, width))],
        out_shape=[
            jax.ShapeDtypeStruct((total, width), f32),
            jax.ShapeDtypeStruct((width, hidden), bf16),
            jax.ShapeDtypeStruct((8, hidden), f32),
            jax.ShapeDtypeStruct((shard, width), f32),
        ],
        scratch_shapes=scratch
        + [
            pltpu.SemaphoreType.DMA((4, 10)),
            pltpu.SemaphoreType.DMA((4, 10)),
            pltpu.SemaphoreType.DMA((4, 4)),
            pltpu.SemaphoreType.DMA((1,)),
        ],
        compiler_params=pltpu.CompilerParams(collective_id=7, has_side_effects=True, vmem_limit_bytes=vmem_bytes),
        name="middle",
    )(grad, second, turned, wo, wi, slope, part.reshape((2, 4, 2, 2, shard, width)))


back_plan = {
    (0, 0): ["B0 B1 B2 B3", "B4 B5"],
    (0, 2): ["S0"],
    (0, 3): ["S1"],
    (0, 4): ["B6"],
    (1, 1): ["S2 F0"],
    (1, 2): ["S3 F1 L0"],
    (1, 3): ["S4 S5 F2 L1"],
    (1, 4): ["B7"],
    (2, 1): ["S6 F3 L2 E0"],
    (2, 2): ["S7 F4 F5 L3", "E1"],
    (2, 3): ["F6 L4 L5 E2"],
    (2, 4): ["B8"],
    (3, 1): ["S8 F7 L6 E3"],
    (3, 2): ["F8 L7 E4 E5"],
    (3, 3): ["S9 Vt L8 E6", "F9 Vs E7 L9", "Vf E8 Vl E9", "Ve"],
    (3, 4): ["B9"],
}


def back_body(slot, question, *refs):
    (length_ref, q_ref, k_ref, v_ref, mixed_ref, grad_ref, mass_ref, cos_ref, sin_ref) = refs[:9]
    (wq_ref, wk_ref, wv_ref, turned_ref, vec_ref, first_ref, inner_ref, output_ref, proj_ref) = refs[9:18]
    (doc_ref, query_ref, inner_out, output_out, proj_out, dwq_out, dwk_out, dwv_out, vec_out) = refs[18:27]
    (grads, token_grad, stage, value, sums, heard) = refs[27:33]
    flat = refs[33 : 33 + 10 * 5]
    send_sem, recv_sem, own_sem, vec_send, vec_recv, copy_sem = refs[33 + 10 * 5 :]
    step = pl.program_id(0)
    place = Place()
    group = 4 * HEAD

    def lines(ref, core, *tail):
        return lambda k: ref.at[(place.lines[k][0], slice(None), place.lines[k][1], core) + tail]

    def matrix(u, ref, out, *tail):
        return Unit(
            place,
            out,
            lines(ref, place.c, *tail),
            lines(ref, place.other, *tail),
            flat[5 * u : 5 * u + 5],
            send_sem.at[u],
            recv_sem.at[u],
            own_sem.at[u],
        )

    def into(ref, *where):
        def put(block):
            ref[where] = block

        return put

    everything = slice(None)
    units = []
    columns = inner_out.shape[1] // 4
    for j in range(4):
        part = slice(j * columns, (j + 1) * columns)
        units.append(matrix(j, inner_ref, into(inner_out, everything, part), everything, part))
    units.append(matrix(4, output_ref, into(output_out, everything, everything)))
    units.append(matrix(5, proj_ref, into(proj_out, everything, everything)))

    def heads_out(g):
        part = slice(g * group, (g + 1) * group)

        def put(block):
            for i, ref in enumerate((dwq_out, dwk_out, dwv_out)):
                ref[:, part] = block[:, i * group : (i + 1) * group]

        return put

    for g in range(4):
        here = stage.at[g % 2]
        u = 6 + g
        units.append(
            Unit(
                place,
                heads_out(g),
                lines(here, place.c),
                lines(here, place.other),
                flat[5 * u : 5 * u + 5],
                send_sem.at[u],
                recv_sem.at[u],
            )
        )
    vectors = VectorSum(place, value, sums, heard, vec_out, vec_send, vec_recv)
    tells = {"t": "twin", "s": "second", "f": "first", "l": "line", "e": "finish"}

    def pump(spot):
        for g in range(4):
            todo = [name for some in back_plan.get((g, spot), []) for name in some.split()]
            if todo:

                @pl.when(step == g)
                def _():
                    for name in todo:
                        if name[0] == "V":
                            getattr(vectors, tells[name[1]])()
                        else:
                            getattr(units[int(name[1:])], scatter_moves[name[0]])()

    seed = pltpu.make_async_copy(first_ref, token_grad, copy_sem.at[0])

    @pl.when(step == 0)
    def _():
        place.greet()
        seed.start()
        value[...] = vec_ref[...]

    ins = (q_ref, k_ref, v_ref, mixed_ref, grad_ref, mass_ref, cos_ref, sin_ref)
    dq, dk, dv = [grads.at[:, i * group : (i + 1) * group] for i in range(3)]
    pump(0)
    for p in range(2):
        back_pair(slot, p, length_ref[0], *ins, dq, dk, dv)
        pump(1 + p)
    back_questions(slot, question, q_ref, k_ref, v_ref, grad_ref, cos_ref, sin_ref, dq, dk, dv)
    for g in range(2, 4):

        @pl.when(step == g)
        def _():
            units[4 + g].drain_twin()

    weight = nn(turned_ref[...], grads[...]).astype(bf16)
    stage[lax.rem(step, 2)] = weight.reshape(stage.shape[1:])
    column_sums = jnp.sum(grads[...].astype(f32), axis=0, keepdims=True)
    for g in range(4):

        @pl.when(step == g)
        def _():
            for i in range(3):
                value[10 + i : 11 + i, g * group : (g + 1) * group] = column_sums[:, i * group : (i + 1) * group]

    pump(4)

    @pl.when(step == 0)
    def _():
        seed.wait()

    token_grad[...] += nt(dq[...], wq_ref[...]) + nt(dk[...], wk_ref[...]) + nt(dv[...], wv_ref[...])
    docs = pltpu.make_async_copy(token_grad.at[0:slot], doc_ref, copy_sem.at[1])
    asked = pltpu.make_async_copy(token_grad.at[slot:], query_ref, copy_sem.at[2])

    @pl.when(step == 3)
    def _():
        docs.start()
        asked.start()

    pump(3)

    @pl.when(step == 3)
    def _():
        for u in range(10):
            if u not in (6, 7):
                units[u].drain_twin()
            units[u].drain()
        vectors.sender.drain()
        docs.wait()
        asked.wait()


def unit_buffers(shape, dtype):
    return [
        pltpu.VMEM((4, 4) + shape, dtype),
        pltpu.VMEM((4, 4) + shape, dtype),
        pltpu.VMEM((2, 4) + shape, dtype),
        pltpu.VMEM((4,) + shape, dtype),
        pltpu.VMEM((3,) + shape, dtype),
    ]


def back_close(length, q, k, v, mixed, grad, mass, cosine, sine, slot, question, tokens, weights, vectors, first_grad, parts):
    total, width = q.shape
    group = 4 * HEAD
    shapes = [(p.shape[0] // 32, p.shape[1]) for p in parts]
    inner, output, proj = shapes
    unit_shapes = [(inner[0], inner[1] // 4)] * 4 + [output, proj]
    unit_shapes += [(width // 32, 3 * group)] * 4
    scratch = []
    for shape in unit_shapes:
        scratch += unit_buffers(shape, bf16)
    once = pl.Buffered(1)
    hbm = pl.BlockSpec(memory_space=pl.ANY)

    def kept(shape):
        return pl.BlockSpec(shape, lambda i: (0,) * len(shape), pipeline_mode=once)

    shard = (width // 32, width)
    outs = [inner, output, proj, shard, shard, shard, vectors.shape]
    return pl.pallas_call(
        functools.partial(back_body, slot, question),
        grid=(width // group,),
        in_specs=[pl.BlockSpec(memory_space=pltpu.SMEM)]
        + [group_spec(total)] * 3
        + [pl.BlockSpec((total, group), lambda i: (0, i), pipeline_mode=once)] * 2
        + [mass_spec(total), kept((total, 2 * HEAD)), kept((total, 2 * HEAD))]
        + [pl.BlockSpec((width, group), lambda i: (0, i), pipeline_mode=once)] * 3
        + [kept((width, total)), kept(vectors.shape)]
        + [hbm] * 4,
        out_specs=[hbm, hbm] + [kept(shape) for shape in outs],
        out_shape=[jax.ShapeDtypeStruct((slot, width), f32), jax.ShapeDtypeStruct((total - slot, width), f32)]
        + [jax.ShapeDtypeStruct(shape, f32) for shape in outs],
        scratch_shapes=[
            pltpu.VMEM((total, 3 * group), bf16),
            pltpu.VMEM((total, width), f32),
            pltpu.VMEM((2, 2, 4, 2, 2, width // 32, 3 * group), bf16),
            pltpu.VMEM(vectors.shape, f32),
            pltpu.VMEM((3,) + vectors.shape, f32),
            pltpu.VMEM((6,) + vectors.shape, f32),
        ]
        + scratch
        + [
            pltpu.SemaphoreType.DMA((10, 10)),
            pltpu.SemaphoreType.DMA((10, 10)),
            pltpu.SemaphoreType.DMA((10, 4)),
            pltpu.SemaphoreType.DMA((6,)),
            pltpu.SemaphoreType.DMA((6,)),
            pltpu.SemaphoreType.DMA((3,)),
        ],
        compiler_params=pltpu.CompilerParams(collective_id=4, has_side_effects=True, vmem_limit_bytes=67043328),
        name="back",
    )(
        length, q, k, v, mixed, grad, mass, cosine, sine, *weights, tokens, vectors, first_grad,
        *[p.reshape((2, 4, 2, 2) + shape) for p, shape in zip(parts, shapes)],
    )


def rotary_tables(slot, question, count):
    place = np.concatenate([np.arange(slot)] + [np.arange(question)] * count)
    channel = np.arange(HEAD // 2, dtype=np.float32)[None, :]
    rate = np.exp(channel * np.float32(-2.0 * math.log(10000.0) / HEAD))
    angle = place.astype(np.float32)[:, None] * rate
    cosine, sine = np.cos(angle), np.sin(angle)
    return (
        jnp.asarray(np.concatenate([cosine] * 4, axis=1)),
        jnp.asarray(np.concatenate([-sine, sine] * 2, axis=1)),
    )


def dense(operand, matrix):
    return jnp.einsum("ld,de->le", operand, matrix, preferred_element_type=f32)


def dense_back(gradient, matrix):
    return jnp.einsum("le,de->ld", gradient, matrix, preferred_element_type=f32)


def weight_grad(operand, gradient):
    return jnp.einsum("ld,le->de", operand, gradient, preferred_element_type=f32).astype(bf16)


def row_sum(values):
    return jnp.sum(values.astype(f32), axis=0)


def normalize_rows(values):
    center = jnp.mean(values, axis=-1, keepdims=True)
    centered = values - center
    variance = jnp.mean(centered * centered, axis=-1, keepdims=True)
    inverse_std = lax.rsqrt(variance + norm_eps)
    return (centered * inverse_std, inverse_std)


def norm_back(gradient, normal, inverse_std):
    return inverse_std * (
        gradient
        - jnp.mean(gradient, axis=-1, keepdims=True)
        - normal * jnp.mean(gradient * normal, axis=-1, keepdims=True)
    )


def gelu_both(values):
    half = 0.5 * (1.0 + lax.erf(values * math.sqrt(0.5)))
    bell = jnp.exp(-0.5 * values * values) * (1.0 / math.sqrt(2.0 * math.pi))
    return (values * half, half + values * bell)


def padded(rows, lanes):
    return jnp.pad(rows, ((0, 0), (0, lanes - rows.shape[1])))


class Close:
    def weights(self, matrices, vectors, wide_vector, positives):
        lanes = wide_vector.shape[0]
        rows = jnp.concatenate(
            [wide_vector[None], padded(jnp.stack(vectors), lanes), padded(positives.astype(bf16)[None], lanes)]
        )
        pack = jnp.pad(rows, ((0, 16 - rows.shape[0]), (0, 0)))
        *wholes, packs = gather(list(matrices) + [pack], 0)
        packs = packs.reshape(32, 16, lanes)
        count, size = len(vectors), vectors[0].shape[0]
        small = packs[:, 1 : 1 + count, :size].transpose(1, 0, 2).reshape(count, 32 * size)
        chosen = packs[:, 1 + count, : positives.shape[0]].reshape(-1).astype(jnp.int32)
        return wholes, small, packs[:, 0].reshape(-1), chosen

    def forward(self, attend, shards, row_vectors, inner_bias):
        tokens = attend[1]
        output_shard, inner_shard, outer_shard, proj_shard = shards
        slot = attend[-2]
        outs, turned, (w_output, w_inner) = attend_gather(*attend, [output_shard, inner_shard])
        mixed = outs[3]
        (normal, inverse, low, activated, slope, low_turned), (w_outer, w_proj) = inner_forward(
            tokens, mixed, w_output, w_inner, jnp.stack(row_vectors), inner_bias[None], slot, [outer_shard, proj_shard]
        )
        return outs, normal, inverse[:, :1], (low_turned, turned), activated, slope, (w_output, w_inner, w_outer, w_proj)

    def rows(self, rows):
        return gather([rows], 1, small_room)[0]

    def totals(self, totals):
        block = jnp.broadcast_to(padded(totals[None], 128), (8, 128))
        return exchange(block, 2).reshape(32, 8, 128)[:, 0, : totals.shape[0]]

    def row_grads(self, grads):
        return scatter([grads], 3)[0]

    def middle(self, grad, second, low, w_outer, w_inner, slope, part):
        normed_grad, inner_grad, bias, shard = middle_back(grad, second, low, w_outer, w_inner, slope, part)
        return normed_grad, inner_grad, bias[0], shard

    def back(self, attend, tokens, weights, vectors, inner_bias_grad, first_grad, parts):
        width = tokens.shape[0]
        slot = attend[-2]
        rows = jnp.concatenate([inner_bias_grad.reshape(4, width), jnp.stack(vectors)])
        rows = jnp.pad(rows, ((0, 16 - rows.shape[0]), (0, 0)))
        docs, asked, *shards, sums = back_close(*attend, tokens, weights, rows, first_grad, parts)
        index = lax.axis_index(AXES)
        small = lax.dynamic_slice_in_dim(sums[4:13], index * (width // 32), width // 32, 1)
        inner_bias_shard = lax.dynamic_slice_in_dim(sums[:4].reshape(-1), index * (width // 8), width // 8, 0)
        return docs, asked, shards, [small[i] for i in range(9)], inner_bias_shard


class Far:
    def one(self, value):
        return lax.all_gather(value, AXES, axis=0, tiled=True)

    def weights(self, matrices, vectors, wide_vector, positives):
        return (
            [self.one(m) for m in matrices],
            jnp.stack([self.one(v) for v in vectors]),
            self.one(wide_vector),
            self.one(positives),
        )

    def forward(self, attend, shards, row_vectors, inner_bias):
        tokens = attend[1]
        weights = [self.one(m) for m in shards]
        outs = attend_forward(*attend)
        bias, gain, shift = row_vectors
        normal, inverse = normalize_rows(tokens.astype(f32) + dense(outs[3], weights[0]) + bias)
        low = (normal * gain + shift).astype(bf16)
        activated, slope = gelu_both(dense(low, weights[1]) + inner_bias.astype(f32))
        return outs, normal, inverse, (low, tokens), activated.astype(bf16), slope.astype(bf16), weights

    def rows(self, rows):
        return self.one(rows)

    def totals(self, totals):
        return self.one(totals[None])

    def row_grads(self, grads):
        return self.spread(grads)

    def spread(self, value):
        return lax.psum_scatter(value.astype(f32), AXES, scatter_dimension=0, tiled=True)

    def middle(self, grad, second, low, w_outer, w_inner, slope, part):
        hidden = (dense_back(grad, w_outer) * slope.astype(f32)).astype(bf16)
        return second + dense_back(hidden, w_inner), weight_grad(low, hidden), row_sum(hidden), self.spread(part)

    def back(self, attend, tokens, weights, vectors, inner_bias_grad, first_grad, parts):
        slot = attend[-2]
        grads = attend_backward(*attend)
        total = first_grad
        for grad, weight in zip(grads, weights):
            total = total + dense_back(grad, weight)
        parts = list(parts) + [weight_grad(tokens, grad) for grad in grads]
        vectors = list(vectors) + [row_sum(grad) for grad in grads]
        return (
            total[:slot],
            total[slot:],
            [self.spread(part) for part in parts],
            [self.spread(vector) for vector in vectors],
            self.spread(inner_bias_grad),
        )


def local(
    link,
    doc_tokens,
    query_tokens,
    doc_lengths,
    positives,
    query_weight,
    key_weight,
    value_weight,
    output_weight,
    query_bias,
    key_bias,
    value_bias,
    output_bias,
    attn_gain,
    attn_shift,
    inner_weight,
    inner_bias,
    outer_weight,
    outer_bias,
    final_gain,
    final_shift,
    proj_weight,
):
    slot, width = doc_tokens.shape[1:]
    count, question = query_tokens.shape[:2]
    tokens = jnp.concatenate([doc_tokens[0], query_tokens.reshape(count * question, width)])
    cosine, sine = rotary_tables(slot, question, count)

    matrices, vectors, b_inner, chosen = link.weights(
        [query_weight, key_weight, value_weight],
        [
            query_bias,
            key_bias,
            value_bias,
            output_bias,
            attn_gain,
            attn_shift,
            outer_bias,
            final_gain,
            final_shift,
        ],
        inner_bias,
        positives,
    )
    w_query, w_key, w_value = matrices
    b_output, g_attn, s_attn, b_outer, g_final, s_final = [vectors[i].astype(f32) for i in range(3, 9)]

    outs, first_normal, first_inverse, (normed_low, tokens_kept), activated, slope, matrices = link.forward(
        (doc_lengths, tokens, w_query, w_key, w_value, vectors[0:8], cosine, sine, slot, question),
        [output_weight, inner_weight, outer_weight, proj_weight],
        [b_output, g_attn, s_attn],
        b_inner,
    )
    query_rot, key_rot, value_low, mixed, mass = outs
    w_output, w_inner, w_outer, w_proj = matrices
    normed = first_normal * g_attn + s_attn
    outer_branch = dense(activated, w_outer) + b_outer
    second_normal, second_inverse = normalize_rows(normed + outer_branch)
    states_low = (second_normal * g_final + s_final).astype(bf16)
    projected = dense(states_low, w_proj)
    inverse_norm = lax.rsqrt(jnp.sum(projected * projected, axis=-1, keepdims=True) + unit_eps)
    encoded = (projected * inverse_norm).astype(bf16)

    doc_rows = encoded[:slot]
    all_rows = link.rows(encoded[slot:])
    key_mask = jnp.arange(slot)[None, :] < doc_lengths[0]
    vector_width = encoded.shape[1]
    block_rows = 32 * question
    row_blocks = all_rows.reshape(-1, block_rows, vector_width)

    def block_scores(rows_block):
        scores = jnp.einsum("qe,ke->qk", rows_block, doc_rows, preferred_element_type=f32)
        return jnp.where(key_mask, scores / sharpness_divisor, masked_value)

    def smooth_block(unused, rows_block):
        scores = block_scores(rows_block)
        peak = jnp.max(scores, axis=1, keepdims=True)
        return unused, sharpness_divisor * (
            peak[:, 0] + jnp.log(jnp.sum(jnp.exp(scores - peak), axis=1))
        )

    unused, smooth = lax.scan(smooth_block, jnp.zeros((), f32), row_blocks)
    totals = smooth.reshape(-1, question).sum(axis=1)
    doc_index = lax.axis_index(AXES)
    all_totals = link.totals(totals)
    peak = jnp.max(all_totals, axis=0)
    log_total = peak + jnp.log(jnp.sum(jnp.exp(all_totals - peak), axis=0))
    hit = jnp.arange(all_totals.shape[0])[:, None] == chosen[None, :]
    losses = log_total - jnp.sum(jnp.where(hit, all_totals, 0.0), axis=0)
    query_loss = lax.dynamic_slice_in_dim(losses, doc_index * count, count, 0)
    coefficient = loss_scale * (jnp.exp(totals - log_total) - (chosen == doc_index).astype(f32))
    token_coefficient = jnp.broadcast_to(coefficient[:, None], (coefficient.shape[0], question))
    token_coefficient = token_coefficient.reshape(row_blocks.shape[0], block_rows)

    def grad_block(doc_grad, inputs):
        rows_block, smooth_rows, coefficient_rows = inputs
        weight = jnp.exp(block_scores(rows_block) - (smooth_rows / sharpness_divisor)[:, None])
        score_grad = (weight * coefficient_rows[:, None]).astype(bf16)
        row_grad = jnp.einsum("qk,ke->qe", score_grad, doc_rows, preferred_element_type=f32)
        doc_grad = doc_grad + jnp.einsum("qk,qe->ke", score_grad, rows_block, preferred_element_type=f32)
        return doc_grad, row_grad

    doc_vector_grad, row_grads = lax.scan(
        grad_block, jnp.zeros(doc_rows.shape, f32), (row_blocks, smooth, token_coefficient)
    )
    query_vector_grad = link.row_grads(row_grads.reshape(-1, vector_width))
    vector_grad = jnp.concatenate([doc_vector_grad, query_vector_grad])

    radial = jnp.sum(vector_grad * projected, axis=-1, keepdims=True)
    proj_grad = (
        vector_grad * inverse_norm - projected * (inverse_norm * inverse_norm * inverse_norm) * radial
    ).astype(bf16)
    proj_weight_grad = weight_grad(states_low, proj_grad)
    states_grad = dense_back(proj_grad, w_proj)
    final_gain_grad = row_sum(states_grad * second_normal)
    final_shift_grad = row_sum(states_grad)
    second_grad = norm_back(states_grad * g_final, second_normal, second_inverse)
    outer_grad = second_grad.astype(bf16)
    outer_weight_grad = weight_grad(activated, outer_grad)
    outer_bias_grad = row_sum(outer_grad)
    normed_grad, inner_weight_grad, inner_bias_grad, outer_shard = link.middle(
        outer_grad, second_grad, normed_low, w_outer, w_inner, slope, outer_weight_grad
    )
    attn_gain_grad = row_sum(normed_grad * first_normal)
    attn_shift_grad = row_sum(normed_grad)
    first_grad = norm_back(normed_grad * g_attn, first_normal, first_inverse)
    attended_grad = first_grad.astype(bf16)
    output_weight_grad = weight_grad(mixed, attended_grad)
    output_bias_grad = row_sum(attended_grad)
    mixed_grad = dense_back(attended_grad, w_output).astype(bf16)
    attend = (
        doc_lengths, query_rot, key_rot, value_low, mixed, mixed_grad, mass, cosine, sine, slot, question,
    )
    docs_grad, asked_grad, shards, small, inner_bias_shard = link.back(
        attend,
        tokens_kept,
        (w_query, w_key, w_value),
        [outer_bias_grad, final_gain_grad, final_shift_grad, attn_gain_grad, attn_shift_grad, output_bias_grad],
        inner_bias_grad,
        first_grad,
        [inner_weight_grad, output_weight_grad, proj_weight_grad],
    )
    inner_shard, output_shard, proj_shard, query_shard, key_shard, value_shard = shards
    b_outer_shard, gain_shard, shift_shard, attn_gain_shard, attn_shift_shard, b_output_shard, *b_heads = small
    return (
        query_loss,
        states_low[None, :slot],
        states_low[slot:].reshape(count, question, width),
        docs_grad[None],
        asked_grad.reshape(count, question, width),
        query_shard,
        key_shard,
        value_shard,
        output_shard,
        *b_heads,
        b_output_shard,
        attn_gain_shard,
        attn_shift_shard,
        inner_shard,
        inner_bias_shard,
        outer_shard,
        b_outer_shard,
        gain_shard,
        shift_shard,
        proj_shard,
    )


def solution(mesh):
    row = P(AXES)
    flat = P(AXES, None)
    deep = P(AXES, None, None)
    in_specs = (deep, deep, row, row) + (flat,) * 4 + (row,) * 6 + (flat, row, flat, row, row, row, flat)
    out_specs = (row, deep, deep, deep, deep) + (flat,) * 4 + (row,) * 6 + (flat, row, flat, row, row, row, flat)
    link = Close() if (mesh.shape["fsdp"], mesh.shape["dp"]) == (2, 16) else Far()
    return jax.shard_map(
        functools.partial(local, link), mesh=mesh, in_specs=in_specs, out_specs=out_specs, check_vma=False
    )
```
